32 devices in a mesh: seq: 8 (over z, y), dp: 4 (over x, core).
Axes of the slice: x: 2, y: 2, z: 4, core: 2. Of those that a mesh axis runs over, the one named last changes fastest.
Arguments:
- inputs: bfloat16 [8, 1024, 1024], P('dp', 'seq'), may hold values from -6 to 6
- first_values: bfloat16 [8, 1024, 1024], P('dp', 'seq'), may hold values from -6 to 6
- teacher_states: bfloat16 [8, 1024, 1024], P('dp', 'seq'), may hold values from -6 to 6
- out_cotangent: bfloat16 [8, 1024, 1024], P('dp', 'seq'), may hold values from -6 to 6
- token_valid: int32 [8, 1024], P('dp', 'seq'), may hold values from 0 to 1, as said below
- attn_gain: bfloat16 [1024], P(('seq', 'dp')), may hold values from 0.5 to 1.5
- w_query: bfloat16 [1024, 1024], P(('seq', 'dp')), may hold values from -0.1875 to 0.1875
- w_key: bfloat16 [1024, 1024], P(('seq', 'dp')), may hold values from -0.1875 to 0.1875
- w_value: bfloat16 [1024, 1024], P(('seq', 'dp')), may hold values from -0.1875 to 0.1875
- w_output: bfloat16 [1024, 1024], P(('seq', 'dp')), may hold values from -3 to 3
- mlp_gain: bfloat16 [1024], P(('seq', 'dp')), may hold values from 0.5 to 1.5
- w_gate: bfloat16 [1024, 2816], P(('seq', 'dp')), may hold values from -0.1875 to 0.1875
- w_up: bfloat16 [1024, 2816], P(('seq', 'dp')), may hold values from -0.1875 to 0.1875
- w_down: bfloat16 [2816, 1024], P(('seq', 'dp')), may hold values from -0.109375 to 0.109375
Outputs:
- output: float32 [8, 1024, 1024], P('dp', 'seq')
- loss_value: float32 [], replicated
- grad_inputs: float32 [8, 1024, 1024], P('dp', 'seq')
- grad_first_values: float32 [8, 1024, 1024], P('dp', 'seq')
- grad_attn_gain: float32 [1024], P(('seq', 'dp'))
- grad_query: float32 [1024, 1024], P(('seq', 'dp'))
- grad_key: float32 [1024, 1024], P(('seq', 'dp'))
- grad_value: float32 [1024, 1024], P(('seq', 'dp'))
- grad_output: float32 [1024, 1024], P(('seq', 'dp'))
- grad_mlp_gain: float32 [1024], P(('seq', 'dp'))
- grad_gate: float32 [1024, 2816], P(('seq', 'dp'))
- grad_up: float32 [1024, 2816], P(('seq', 'dp'))
- grad_down: float32 [2816, 1024], P(('seq', 'dp'))
The draws below stay inside these ranges and needn't reach their ends.
Inputs may be any that keep to these rules, and one draw needn't show every extreme that they name: `token_valid`: 1 marks a token that counts in the loss; the last position of every sequence is 1.
All inputs are finite; a program needn't handle non-finite values.
Results may differ from the reference program's by a relative error of at most 0.018.
Values may be sent and summed in bfloat16 or wider, within the bound.
No kernel may reach another device: no remote copies, remote signals or barrier semaphores. Data moves between devices by JAX's collectives and lax.ppermute only.
A program may use at most 256 MiB of HBM per device.

```python
import math
import jax
import jax.numpy as jnp
from jax import lax

D = 1024
HEAD_DIM = 64
FF = 2816
BLOCK = 256
LEN = 1024
SEQS = 8


def draw_token_valid(key, part):
    position = jnp.arange(LEN, dtype=jnp.int32)[None, :]
    drawn = jax.random.randint(key, (SEQS, LEN), 0, 4 * LEN, dtype=jnp.int32)
    chosen = (drawn < LEN + 3 * position) | (position == LEN - 1)
    return jnp.where(chosen, 1, 0).astype(jnp.int32)


def block_scale(own_key, shape, shards, low, high):
    level, own = 1.0, jax.random.fold_in(own_key, 6)
    for axis_at, parts in shards:
        heights = jnp.exp(jax.random.uniform(jax.random.fold_in(own, axis_at), (parts,), jnp.float32, low / len(shards), high / len(shards)))
        level = level * jnp.repeat(heights, shape[axis_at] // parts).reshape([-1 if axis == axis_at else 1 for axis in range(len(shape))])
    return level


def scatter_about(key, extent, scale, reach, split=(), kind=jnp.bfloat16):
    factor_of = block_scale(key, extent, split, -0.22, 0.18) if split else 1.0
    array = jax.random.normal(key, extent, jnp.float32) * scale * factor_of
    return jnp.minimum(jnp.maximum(array, -reach), reach).astype(kind)


def setup_inputs(seed: int = 0) -> dict:
    arg_keys = jax.random.split(jax.random.key(seed), 15)
    return {
        "inputs": scatter_about(arg_keys[0], (SEQS, LEN, D), 1.0, 6.0, ((0, 4), (1, 8))),
        "first_values": scatter_about(arg_keys[1], (SEQS, LEN, D), 1.0, 6.0, ((0, 4), (1, 8))),
        "teacher_states": scatter_about(arg_keys[2], (SEQS, LEN, D), 1.0, 6.0, ((0, 4), (1, 8))),
        "out_cotangent": scatter_about(arg_keys[3], (SEQS, LEN, D), 1.0, 6.0, ((0, 4), (1, 8))),
        "token_valid": draw_token_valid(jax.random.fold_in(arg_keys[14], 71), 0),
        "attn_gain": jnp.clip(1.0 + 0.1 * jax.random.normal(arg_keys[5], (D,), jnp.float32), 0.5, 1.5).astype(jnp.bfloat16),
        "w_query": scatter_about(arg_keys[6], (D, D), D ** -0.5, 0.1875, ((0, 32),)),
        "w_key": scatter_about(arg_keys[7], (D, D), D ** -0.5, 0.1875, ((0, 32),)),
        "w_value": scatter_about(arg_keys[8], (D, D), D ** -0.5, 0.1875, ((0, 32),)),
        "w_output": scatter_about(arg_keys[9], (D, D), 4 ** -0.5, 3.0, ((0, 32),)),
        "mlp_gain": jnp.clip(1.0 + 0.1 * jax.random.normal(arg_keys[10], (D,), jnp.float32), 0.5, 1.5).astype(jnp.bfloat16),
        "w_gate": scatter_about(arg_keys[11], (D, FF), D ** -0.5, 0.1875, ((0, 32),)),
        "w_up": scatter_about(arg_keys[12], (D, FF), D ** -0.5, 0.1875, ((0, 32),)),
        "w_down": scatter_about(arg_keys[13], (FF, D), FF ** -0.5, 0.109375, ((0, 32),)),
    }


EPSILON = 1e-06
THETA = 10000.0
MASKED = -1000000000.0
SCALE = 0.125
HIGHEST_PRECISION = lax.Precision.HIGHEST

@jax.custom_vjp
def low(v):
    return lax.optimization_barrier(v.astype(jnp.bfloat16)).astype(jnp.float32)

@jax.custom_vjp
def low_back(v):
    return v

def low_keep(v):
    return (low(v), None)

def low_pass(kept, grad):
    return (grad,)

def back_keep(v):
    return (v, None)

def back_low(kept, grad):
    return (low(grad),)
low.defvjp(low_keep, low_pass)
low_back.defvjp(back_keep, back_low)

def rotary_tables(positions, head_dim):
    half_dim = head_dim // 2
    frequency = THETA ** (-(jnp.arange(half_dim, dtype=jnp.float32) * 2.0 / head_dim))
    angles = positions[:, None] * frequency[None, :]
    return (jnp.cos(angles), jnp.sin(angles))

def rotate(values, cosines, sines):
    half_dim = values.shape[-1] // 2
    first_half = values[..., :half_dim]
    second_half = values[..., half_dim:]
    cos_rows = cosines[:, None, :]
    sin_rows = sines[:, None, :]
    return jnp.concatenate([first_half * cos_rows - second_half * sin_rows, second_half * cos_rows + first_half * sin_rows], axis=-1)

def rms_scale(values):
    return lax.rsqrt(lax.optimization_barrier(jnp.mean(values * values, axis=-1, keepdims=True)) + EPSILON)

def project(left, weight):
    return jnp.einsum('gtd,de->gte', left, weight, precision=HIGHEST_PRECISION)

def block_layer(params, inputs, firsts, teacher, valid_rows, valid_total):
    attn_gain, w_query, w_key, w_value, w_output, mlp_gain, w_gate, w_up, w_down = params
    group_size, length, model_width = inputs.shape
    head_count = model_width // HEAD_DIM

    def to_heads(values):
        return values.reshape(group_size, length, head_count, HEAD_DIM)
    normed = low(inputs * rms_scale(inputs) * attn_gain)
    cosines, sines = rotary_tables(jnp.arange(length, dtype=jnp.float32), HEAD_DIM)
    queries = low(rotate(to_heads(low_back(project(normed, w_query))), cosines, sines))
    key_rows = low(rotate(to_heads(low_back(project(normed, w_key))), cosines, sines))
    mixed = to_heads(low(low_back(0.5 * project(normed, w_value) + 0.5 * firsts)))
    block_ids = jnp.arange(length, dtype=jnp.int32) // BLOCK
    block_rows = min(512, length)

    def attend(block_index):
        row_start = block_index * block_rows
        query_block = lax.dynamic_slice_in_dim(queries, row_start, block_rows, 1)
        scores = low_back(SCALE * jnp.einsum('gqhd,gkhd->ghqk', query_block, key_rows, precision=HIGHEST_PRECISION))
        query_ids = lax.dynamic_slice_in_dim(block_ids, row_start, block_rows, 0)
        allowed = block_ids[None, :] <= query_ids[:, None]
        scores = jnp.where(allowed[None, None], scores, MASKED)
        row_top = lax.optimization_barrier(jnp.max(scores, axis=-1, keepdims=True))
        log_total = row_top + jnp.log(lax.optimization_barrier(jnp.sum(jnp.exp(scores - row_top), axis=-1, keepdims=True)))
        probabilities = low(jnp.exp(scores - log_total))
        return jnp.einsum('ghqk,gkhd->gqhd', probabilities, mixed, precision=HIGHEST_PRECISION)
    pieces = lax.map(jax.checkpoint(attend), jnp.arange(length // block_rows, dtype=jnp.int32))
    attended = jnp.moveaxis(pieces, 0, 1).reshape(group_size, length, model_width)
    branch = low_back(project(low(low_back(attended)), w_output))
    hidden_in = inputs + branch
    normed_mlp = low(hidden_in * rms_scale(hidden_in) * mlp_gain)
    gate_pre = low_back(project(normed_mlp, w_gate))
    up_part = low_back(project(normed_mlp, w_up))
    activated = low(jax.nn.silu(gate_pre) * up_part)
    result = hidden_in + low_back(project(activated, w_down))
    residual_err = result - teacher
    loss_part = jnp.sum(valid_rows * lax.optimization_barrier(jnp.mean(residual_err * residual_err, axis=-1))) / valid_total
    return (result, loss_part)

def reference(inputs, first_values, teacher_states, out_cotangent, token_valid, attn_gain, w_query, w_key, w_value, w_output, mlp_gain, w_gate, w_up, w_down):
    params = tuple((weight.astype(jnp.float32) for weight in (attn_gain, w_query, w_key, w_value, w_output, mlp_gain, w_gate, w_up, w_down)))
    valid_float = token_valid.astype(jnp.float32)
    valid_total = jnp.sum(valid_float)
    group_size = math.gcd(SEQS, max(1, 4096 // LEN))
    group_count = SEQS // group_size

    def regroup(values):
        return values.reshape((group_count, group_size) + values.shape[1:])
    series = (regroup(inputs.astype(jnp.float32)), regroup(first_values.astype(jnp.float32)), regroup(teacher_states.astype(jnp.float32)), regroup(out_cotangent.astype(jnp.float32)), regroup(valid_float))

    def scan_step(running, batch_slice):
        grad_sums, loss_sum = running
        x_group, first_group, teacher_group, cot_group, valid_group = batch_slice

        def forward(weights, x_in, first_in):
            return block_layer(weights, x_in, first_in, teacher_group, valid_group, valid_total)
        (result, loss_part), pullback = jax.vjp(forward, params, x_group, first_group)
        grad_weights, grad_x, grad_first = pullback((cot_group, jnp.ones((), jnp.float32)))
        grad_sums = jax.tree.map(lambda left, right: left + right, grad_sums, grad_weights)
        return ((grad_sums, loss_sum + loss_part), (result, grad_x, grad_first))
    initial = (jax.tree.map(jnp.zeros_like, params), jnp.zeros((), jnp.float32))
    (grad_sums, loss_sum), (results, grad_x, grad_first) = lax.scan(scan_step, initial, series)
    full_shape = (SEQS, LEN, D)
    return (results.reshape(full_shape), loss_sum, grad_x.reshape(full_shape), grad_first.reshape(full_shape), grad_sums[0], grad_sums[1], grad_sums[2], grad_sums[3], grad_sums[4], grad_sums[5], grad_sums[6], grad_sums[7], grad_sums[8])
```

```python
import functools

import jax
import jax.numpy as jnp
from jax import lax
from jax.experimental import pallas as pl
from jax.experimental.pallas import tpu as pltpu
from jax.sharding import Mesh
from jax.sharding import PartitionSpec as P

HEAD_DIM = 64
BLOCK = 256
PAIR = 2 * HEAD_DIM

EPSILON = 1e-06
THETA = 10000.0
SCALE = 0.125
ALL = ("z", "y", "x", "c")
SEQ = ("z", "y")
F32 = jnp.float32
BF16 = jnp.bfloat16


def rotary_tables(positions):
    lane = jnp.arange(PAIR, dtype=jnp.int32)
    half = HEAD_DIM // 2
    index = (lane % half).astype(F32)
    frequency = THETA ** (-(index * 2.0 / HEAD_DIM))
    angles = positions.astype(F32)[:, None] * frequency[None, :]
    sign = jnp.where(lane % HEAD_DIM < half, -1.0, 1.0)[None, :]
    return jnp.cos(angles), jnp.sin(angles) * sign


def partner(values):
    half = HEAD_DIM // 2
    lane = lax.broadcasted_iota(jnp.int32, values.shape, values.ndim - 1)
    first = lane % HEAD_DIM < half
    width = values.shape[-1]
    return jnp.where(
        first,
        pltpu.roll(values, width - half, values.ndim - 1),
        pltpu.roll(values, half, values.ndim - 1),
    )


def dot_t(left, right):
    return lax.dot_general(left, right, (((1,), (1,)), ((), ())), preferred_element_type=F32)


def t_dot(left, right):
    return lax.dot_general(left, right, (((0,), (0,)), ((), ())), preferred_element_type=F32)


def dot(left, right):
    return jnp.dot(left, right, preferred_element_type=F32)


def attend_forward_kernel(qkv_ref, out_ref, total_ref):
    parts, _, _, rows, _ = qkv_ref.shape
    per_block = BLOCK // rows
    blocks = parts // per_block
    for head in range(2):
        lanes = pl.ds(head * HEAD_DIM, HEAD_DIM)
        for block in range(blocks):
            lo, hi = block * per_block, (block + 1) * per_block
            query = qkv_ref[lo:hi, 0, 0, :, lanes].reshape(BLOCK, HEAD_DIM)
            keys = qkv_ref[0:hi, 1, 0, :, lanes].reshape(hi * rows, HEAD_DIM)
            values = qkv_ref[0:hi, 2, 0, :, lanes].reshape(hi * rows, HEAD_DIM)
            scores = dot_t(keys, query) * SCALE
            top = jnp.max(scores, axis=0, keepdims=True)
            total = top + jnp.log(jnp.sum(jnp.exp(scores - top), axis=0, keepdims=True))
            probs = jnp.exp(scores - total).astype(BF16)
            mixed = t_dot(values, probs)
            out_ref[lo:hi, 0, :, lanes] = mixed.T.astype(BF16).reshape(per_block, rows, HEAD_DIM)
            total_ref[0, head, block : block + 1, :] = total


def attend_backward_kernel(qkv_ref, grad_ref, total_ref, cos_ref, sin_ref, out_ref, dk_acc, dv_acc):
    parts, _, _, rows, _ = qkv_ref.shape
    per_block = BLOCK // rows
    blocks = parts // per_block
    dk_acc[...] = jnp.zeros_like(dk_acc)
    dv_acc[...] = jnp.zeros_like(dv_acc)
    for block in range(blocks):
        lo, hi = block * per_block, (block + 1) * per_block
        keys_n = hi * rows
        dq_parts = []
        for head in range(2):
            lanes = pl.ds(head * HEAD_DIM, HEAD_DIM)
            query = qkv_ref[lo:hi, 0, 0, :, lanes].reshape(BLOCK, HEAD_DIM)
            grad = grad_ref[lo:hi, 0, :, lanes].reshape(BLOCK, HEAD_DIM)
            keys = qkv_ref[0:hi, 1, 0, :, lanes].reshape(keys_n, HEAD_DIM)
            values = qkv_ref[0:hi, 2, 0, :, lanes].reshape(keys_n, HEAD_DIM)
            scores = dot_t(keys, query) * SCALE
            probs = jnp.exp(scores - total_ref[0, head, block : block + 1, :])
            grad_probs = dot_t(values, grad)
            inner = jnp.sum(probs * grad_probs, axis=0, keepdims=True)
            grad_scores = (probs * (grad_probs - inner)).astype(BF16)
            dk_acc[0:keys_n, lanes] += dot(grad_scores, query) * SCALE
            dv_acc[0:keys_n, lanes] += dot(probs.astype(BF16), grad)
            dq_parts.append(t_dot(keys, grad_scores).T * SCALE)
        dq = jnp.concatenate(dq_parts, axis=1)
        cos = cos_ref[block * BLOCK : (block + 1) * BLOCK, :]
        sin = sin_ref[block * BLOCK : (block + 1) * BLOCK, :]
        dq = (dq * cos - partner(dq) * sin).astype(BF16)
        out_ref[lo:hi, 0, 0, :, :] = dq.reshape(per_block, rows, PAIR)
    dk = dk_acc[...]
    dk = (dk * cos_ref[...] - partner(dk) * sin_ref[...]).astype(BF16)
    out_ref[:, 1, 0, :, :] = dk.reshape(parts, rows, PAIR)
    out_ref[:, 2, 0, :, :] = dv_acc[...].astype(BF16).reshape(parts, rows, PAIR)


VMEM_LIMIT = 60 * 1024 * 1024


def attend_forward(qkv):
    parts, _, units, rows, _ = qkv.shape
    blocks = parts * rows // BLOCK
    return pl.pallas_call(
        attend_forward_kernel,
        grid=(units,),
        in_specs=[pl.BlockSpec((parts, 3, 1, rows, PAIR), lambda u: (0, 0, u, 0, 0))],
        out_specs=[
            pl.BlockSpec((parts, 1, rows, PAIR), lambda u: (0, u, 0, 0)),
            pl.BlockSpec((1, 2, blocks, BLOCK), lambda u: (u, 0, 0, 0)),
        ],
        out_shape=[
            jax.ShapeDtypeStruct((parts, units, rows, PAIR), BF16),
            jax.ShapeDtypeStruct((units, 2, blocks, BLOCK), F32),
        ],
        compiler_params=pltpu.CompilerParams(vmem_limit_bytes=VMEM_LIMIT),
        name="attend_forward",
    )(qkv)


def attend_backward(qkv, grad_att, totals, cos, sin):
    parts, _, units, rows, _ = qkv.shape
    length = parts * rows
    blocks = length // BLOCK
    return pl.pallas_call(
        attend_backward_kernel,
        grid=(units,),
        in_specs=[
            pl.BlockSpec((parts, 3, 1, rows, PAIR), lambda u: (0, 0, u, 0, 0)),
            pl.BlockSpec((parts, 1, rows, PAIR), lambda u: (0, u, 0, 0)),
            pl.BlockSpec((1, 2, blocks, BLOCK), lambda u: (u, 0, 0, 0)),
            pl.BlockSpec((length, PAIR), lambda u: (0, 0)),
            pl.BlockSpec((length, PAIR), lambda u: (0, 0)),
        ],
        out_specs=pl.BlockSpec((parts, 3, 1, rows, PAIR), lambda u: (0, 0, u, 0, 0)),
        out_shape=jax.ShapeDtypeStruct((parts, 3, units, rows, PAIR), BF16),
        scratch_shapes=[pltpu.VMEM((length, PAIR), F32), pltpu.VMEM((length, PAIR), F32)],
        compiler_params=pltpu.CompilerParams(vmem_limit_bytes=VMEM_LIMIT),
        name="attend_backward",
    )(qkv, grad_att, totals, cos, sin)


def swap(array, name, distance):
    size = lax.axis_size(name)
    return lax.ppermute(array, name, [(i, i ^ distance) for i in range(size)])


def arrange(pieces, at):
    bit = 1
    while bit < len(pieces):
        odd = (at & bit) != 0
        pieces = [jnp.where(odd, pieces[j ^ bit], pieces[j]) for j in range(len(pieces))]
        bit *= 2
    return pieces


def gather_rows(shard, order):
    value = shard
    held = []
    for name in order:
        at = lax.axis_index(name)
        pieces = [value] + [swap(value, name, k) for k in range(1, lax.axis_size(name))]
        held.append(name)
        held.sort(key=ALL.index)
        value = jnp.stack(arrange(pieces, at), axis=held.index(name))
    return value.reshape(-1, shard.shape[1])


def stage_rows(rows, order):
    sizes = [lax.axis_size(name) for name in order]
    per = rows // functools.reduce(lambda a, b: a * b, sizes)
    index = lax.broadcasted_iota(jnp.int32, (rows, 1), 0)
    left, inner = index // per, index % per
    place = {}
    for name, size in zip(reversed(order), reversed(sizes)):
        place[name] = (left % size) ^ lax.axis_index(name)
        left = left // size
    device = jnp.zeros_like(index)
    for name in ALL:
        device = device * lax.axis_size(name) + place[name]
    return device * per + inner


def reduce_staged(partial, order):
    columns = partial.shape[1]
    value = partial
    for stage, name in enumerate(order):
        size = lax.axis_size(name)
        value = value.reshape(size, -1, columns)
        received = [swap(value[k], name, k) for k in range(1, size)]
        total = value[0].astype(F32)
        for piece in received:
            total = total + piece.astype(F32)
        value = total if stage == len(order) - 1 else total.astype(BF16)
    return value


def params():
    return pltpu.CompilerParams(vmem_limit_bytes=VMEM_LIMIT)


def project_kernel(x_ref, first_ref, gain_ref, cos_ref, sin_ref, wq_ref, wk_ref, wv_ref, normed_ref, out_ref):
    @pl.when(pl.program_id(0) == 0)
    def _():
        x = x_ref[...].astype(F32)
        inv = lax.rsqrt(jnp.mean(x * x, axis=-1, keepdims=True) + EPSILON)
        normed_ref[...] = (x * inv * gain_ref[...]).astype(BF16)

    normed = normed_ref[...]
    width = wq_ref.shape[1]
    copies = normed.shape[0] // cos_ref.shape[0]
    cos = jnp.concatenate([jnp.concatenate([cos_ref[...]] * copies, 0)] * (width // PAIR), 1)
    sin = jnp.concatenate([jnp.concatenate([sin_ref[...]] * copies, 0)] * (width // PAIR), 1)
    query = dot(normed, wq_ref[...])
    query = (query * cos + partner(query) * sin).astype(BF16)
    key = dot(normed, wk_ref[...])
    key = (key * cos + partner(key) * sin).astype(BF16)
    mixed = (0.5 * dot(normed, wv_ref[...]) + 0.5 * first_ref[...].astype(F32)).astype(BF16)
    _, groups, _, units, rows, _ = out_ref.shape
    for kind, value in enumerate((query, key, mixed)):
        for pair in range(width // PAIR):
            piece = value[:, pair * PAIR : (pair + 1) * PAIR]
            out_ref[pair, :, kind] = piece.reshape(groups, units, rows, PAIR)


def project(x, first, gain, cos, sin, weights, groups, units):
    tokens, width = x.shape
    local_len = tokens // (groups * units)
    pairs = width // PAIR
    wide = 2 * PAIR
    steps = width // wide
    return pl.pallas_call(
        project_kernel,
        grid=(steps,),
        in_specs=[
            pl.BlockSpec((tokens, width), lambda j: (0, 0)),
            pl.BlockSpec((tokens, wide), lambda j: (0, j)),
            pl.BlockSpec((1, width), lambda j: (0, 0)),
            pl.BlockSpec((local_len, PAIR), lambda j: (0, 0)),
            pl.BlockSpec((local_len, PAIR), lambda j: (0, 0)),
            pl.BlockSpec((width, wide), lambda j: (0, j)),
            pl.BlockSpec((width, wide), lambda j: (0, steps + j)),
            pl.BlockSpec((width, wide), lambda j: (0, 2 * steps + j)),
        ],
        out_specs=[
            pl.BlockSpec((tokens, width), lambda j: (0, 0)),
            pl.BlockSpec((2, groups, 3, units, local_len, PAIR), lambda j: (j, 0, 0, 0, 0, 0)),
        ],
        out_shape=[
            jax.ShapeDtypeStruct((tokens, width), BF16),
            jax.ShapeDtypeStruct((pairs, groups, 3, units, local_len, PAIR), BF16),
        ],
        compiler_params=params(),
        name="project",
    )(x, first, gain, cos, sin, weights, weights, weights)


def join_kernel(x_ref, heads_ref, weight_ref, gain_ref, att_ref, hidden_ref, scaled_ref, inv_ref, normed_ref):
    pairs = heads_ref.shape[0]
    tokens = x_ref.shape[0]
    for pair in range(pairs):
        att_ref[:, pair * PAIR : (pair + 1) * PAIR] = heads_ref[pair].reshape(tokens, PAIR)
    hidden = x_ref[...].astype(F32) + dot(att_ref[...], weight_ref[...])
    inv = lax.rsqrt(jnp.mean(hidden * hidden, axis=-1, keepdims=True) + EPSILON)
    scaled = hidden * inv
    hidden_ref[...] = hidden
    scaled_ref[...] = scaled
    inv_ref[...] = jnp.broadcast_to(inv, inv_ref.shape)
    normed_ref[...] = (scaled * gain_ref[...]).astype(BF16)


def join(x, heads, weight, gain):
    tokens, width = x.shape
    return pl.pallas_call(
        join_kernel,
        out_shape=[
            jax.ShapeDtypeStruct((tokens, width), BF16),
            jax.ShapeDtypeStruct((tokens, width), F32),
            jax.ShapeDtypeStruct((tokens, width), F32),
            jax.ShapeDtypeStruct((tokens, PAIR), F32),
            jax.ShapeDtypeStruct((tokens, width), BF16),
        ],
        compiler_params=params(),
        name="join",
    )(x, heads, weight, gain)


def split_kernel(grad_ref, weight_ref, out_ref):
    value = dot_t(grad_ref[...], weight_ref[...]).astype(BF16)
    pairs, groups, _, units, rows, _ = out_ref.shape
    for pair in range(pairs):
        out_ref[pair, :, 0] = value[:, pair * PAIR : (pair + 1) * PAIR].reshape(groups, units, rows, PAIR)


def split(grad, weight, groups, units):
    tokens, width = grad.shape
    return pl.pallas_call(
        split_kernel,
        out_shape=jax.ShapeDtypeStruct(
            (width // PAIR, groups, 1, units, tokens // (groups * units), PAIR), BF16
        ),
        compiler_params=params(),
        name="split",
    )(grad, weight)


def picker(place, width):
    lane = lax.broadcasted_iota(jnp.int32, (place.shape[0], width), 1)
    return jnp.where(lane == place, 1.0, 0.0).astype(BF16)


def staged_kernel(left_ref, right_ref, place_ref, out_ref, turned):
    @pl.when(pl.program_id(0) == 0)
    def _():
        pick = picker(place_ref[...], left_ref.shape[1])
        turned[...] = dot_t(pick, left_ref[...]).astype(BF16)

    out_ref[...] = dot(turned[...], right_ref[...]).astype(BF16)


def staged_grad(left, right, place):
    tokens, width = left.shape
    columns = right.shape[1]
    wide = 2 * PAIR
    return pl.pallas_call(
        staged_kernel,
        grid=(columns // wide,),
        in_specs=[
            pl.BlockSpec((tokens, width), lambda j: (0, 0)),
            pl.BlockSpec((tokens, wide), lambda j: (0, j)),
            pl.BlockSpec((width, 1), lambda j: (0, 0)),
        ],
        out_specs=pl.BlockSpec((width, wide), lambda j: (0, j)),
        out_shape=jax.ShapeDtypeStruct((width, columns), BF16),
        scratch_shapes=[pltpu.VMEM((width, tokens), BF16)],
        compiler_params=params(),
        name="staged_grad",
    )(left, right, place)


def last_kernel(
    heads_ref, normed_ref, x_ref, gain_ref, wq_ref, wk_ref, wv_ref, grad_hidden_ref, gain_m_ref, loss_ref, place_b_ref,
    place_c_ref, grad_in_ref, first_ref, out_b_ref, out_c_ref, grads,
):
    pairs = heads_ref.shape[0]
    tokens, width = x_ref.shape
    for kind in range(3):
        for pair in range(pairs):
            grads[kind, :, pair * PAIR : (pair + 1) * PAIR] = heads_ref[pair, :, kind].reshape(tokens, PAIR)
    first_ref[...] = 0.5 * grads[2].astype(F32)
    grad_norm = (
        dot_t(grads[0], wq_ref[...]) + dot_t(grads[1], wk_ref[...]) + 0.5 * dot_t(grads[2], wv_ref[...])
    )
    x = x_ref[...].astype(F32)
    inv = lax.rsqrt(jnp.mean(x * x, axis=-1, keepdims=True) + EPSILON)
    scaled = x * inv
    gain_part = jnp.sum(grad_norm * scaled, axis=0, keepdims=True)
    scaled_grad = grad_norm * gain_ref[...]
    grad_in_ref[...] = grad_hidden_ref[...] + inv * (
        scaled_grad - scaled * jnp.mean(scaled_grad * scaled, axis=-1, keepdims=True)
    )
    half = width // 2
    pick_b = picker(place_b_ref[...], width)
    turned = dot_t(pick_b, normed_ref[...]).astype(BF16)
    out_b_ref[:, :width] = dot(turned, grads[0]).astype(BF16)
    out_b_ref[:, width : width + half] = (0.5 * dot(turned, grads[2, :, :half])).astype(BF16)
    pick_c = picker(place_c_ref[...], width)
    turned = dot_t(pick_c, normed_ref[...]).astype(BF16)
    out_c_ref[:, :width] = dot(turned, grads[1]).astype(BF16)
    out_c_ref[:, width : width + half] = (0.5 * dot(turned, grads[2, :, half:])).astype(BF16)
    row = lax.broadcasted_iota(jnp.int32, (PAIR, width), 0)
    extra = jnp.where(row == 0, gain_part, jnp.where(row == 1, gain_m_ref[...], loss_ref[...]))
    out_c_ref[:, width + half :] = dot_t(pick_c, extra.astype(BF16)).astype(BF16)


def last(heads, normed, x, gain, weights, grad_hidden, gain_m_part, loss_rows, place_b, place_c):
    tokens, width = x.shape
    whole = lambda *shape: pl.BlockSpec(shape, lambda i: (0,) * len(shape))
    half = width // 2
    return pl.pallas_call(
        last_kernel,
        grid=(1,),
        in_specs=[
            whole(*heads.shape),
            whole(tokens, width),
            whole(tokens, width),
            whole(1, width),
            pl.BlockSpec((width, width), lambda i: (0, 0)),
            pl.BlockSpec((width, width), lambda i: (0, 1)),
            pl.BlockSpec((width, width), lambda i: (0, 2)),
            whole(tokens, width),
            whole(1, width),
            whole(PAIR, 1),
            whole(width, 1),
            whole(width, 1),
        ],
        out_specs=[
            whole(tokens, width),
            whole(tokens, width),
            whole(width, width + half),
            whole(width, width + half + PAIR),
        ],
        out_shape=[
            jax.ShapeDtypeStruct((tokens, width), F32),
            jax.ShapeDtypeStruct((tokens, width), F32),
            jax.ShapeDtypeStruct((width, width + half), BF16),
            jax.ShapeDtypeStruct((width, width + half + PAIR), BF16),
        ],
        scratch_shapes=[pltpu.VMEM((3, tokens, width), BF16)],
        compiler_params=params(),
        name="last",
    )(heads, normed, x, gain, weights, weights, weights, grad_hidden, gain_m_part, loss_rows, place_b, place_c)


STAGES_B = ("c", "y", "x", "z")
STAGES_C = ("c", "x", "y", "z")


def on_device(
    inputs,
    first_values,
    teacher_states,
    out_cotangent,
    token_valid,
    attn_gain,
    w_query,
    w_key,
    w_value,
    w_output,
    mlp_gain,
    w_gate,
    w_up,
    w_down,
):
    batch, local_len, width = inputs.shape
    seqs = lax.axis_size(SEQ)
    devices = lax.axis_size(ALL)
    tokens = batch * local_len
    length = local_len * seqs
    pairs = width // PAIR
    own_rows = w_query.shape[0]
    own_down = w_down.shape[0]
    groups = seqs // pairs
    units = batch // groups

    valid_float = token_valid.astype(F32)
    count = jnp.sum(token_valid)
    extra = jnp.stack(
        [
            attn_gain,
            mlp_gain,
            jnp.full((own_rows,), count // 256, jnp.int32).astype(BF16),
            jnp.full((own_rows,), count % 256, jnp.int32).astype(BF16),
        ],
        axis=1,
    )
    extra = jnp.pad(extra, ((0, 0), (0, PAIR - 4)))
    first_w = lax.all_gather(
        jnp.concatenate([w_query, w_key, w_value, extra], axis=1), ALL, axis=0, tiled=True
    )
    gate_w = gather_rows(w_gate, ("z", "x", "y", "c"))
    up_w = gather_rows(w_up, ("z", "y", "x", "c"))
    rest_w = lax.all_gather(jnp.concatenate([w_down, w_output], axis=0), ALL, axis=0)
    down_w = rest_w[:, :own_down].reshape(-1, width)
    output_w = rest_w[:, own_down:].reshape(-1, width)

    extra_all = first_w[:, 3 * width :].astype(F32).T
    gain_a = extra_all[0:1, :]
    gain_m = extra_all[1:2, :]
    valid_total = jnp.sum(extra_all[2] * 256.0 + extra_all[3]) / own_rows

    cos_all, sin_all = rotary_tables(jnp.arange(length, dtype=jnp.int32))
    here = lax.axis_index(SEQ) * local_len
    cos = lax.dynamic_slice_in_dim(cos_all, here, local_len, 0)
    sin = lax.dynamic_slice_in_dim(sin_all, here, local_len, 0)
    place_b = stage_rows(width, STAGES_B)
    place_c = stage_rows(width, STAGES_C)

    x_low = inputs.reshape(tokens, width)
    normed, packed = project(
        x_low, first_values.reshape(tokens, width), gain_a, cos, sin, first_w, groups, units
    )

    def exchange(array, kinds):
        array = array.reshape(seqs, kinds, units, local_len, PAIR)
        return lax.all_to_all(array, SEQ, split_axis=0, concat_axis=0, tiled=True)

    def by_pair(array):
        return array.reshape(pairs, groups, array.shape[1], units, local_len, PAIR)

    qkv = exchange(packed, 3)
    attended, totals = attend_forward(qkv)
    att_heads = by_pair(exchange(attended, 1))

    att_low, hidden_in, scaled_m, inv_wide, normed_mlp = join(
        x_low, att_heads.reshape(pairs, groups, units, local_len, PAIR), output_w, gain_m
    )
    inv_rms_m = inv_wide[:, :1]
    gate_pre = dot(normed_mlp, gate_w)
    up_part = dot(normed_mlp, up_w)
    gate_sigmoid = jax.nn.sigmoid(gate_pre)
    swish_value = gate_pre * gate_sigmoid
    activated = (swish_value * up_part).astype(BF16)
    result = hidden_in + dot(activated, down_w)
    residual_err = result - teacher_states.astype(F32).reshape(tokens, width)
    valid_rows = valid_float.reshape(tokens, 1)
    token_loss = valid_rows * jnp.mean(residual_err * residual_err, axis=-1, keepdims=True)
    grad_out = (
        out_cotangent.astype(F32).reshape(tokens, width)
        + 2.0 / width * valid_rows * residual_err / valid_total
    )

    grad_down_in = grad_out.astype(BF16)
    grad_act = dot_t(grad_down_in, down_w)
    swish_slope = gate_sigmoid * (1.0 + gate_pre * (1.0 - gate_sigmoid))
    grad_gate_in = (grad_act * up_part * swish_slope).astype(BF16)
    grad_up_in = (grad_act * swish_value).astype(BF16)
    grad_norm_m = dot_t(grad_gate_in, gate_w) + dot_t(grad_up_in, up_w)
    gain_part_m = jnp.sum(grad_norm_m * scaled_m, axis=0, keepdims=True)
    scaled_grad_m = grad_norm_m * gain_m
    grad_hidden = grad_out + inv_rms_m * (
        scaled_grad_m - scaled_m * jnp.mean(scaled_grad_m * scaled_m, axis=-1, keepdims=True)
    )
    grad_branch = grad_hidden.astype(BF16)
    grad_heads = exchange(split(grad_branch, output_w, groups, units), 1)

    down_part = t_dot(activated, grad_down_in).astype(BF16).reshape(devices, own_down, width)
    output_part = t_dot(att_low, grad_branch).astype(BF16).reshape(devices, own_rows, width)
    owned_rest = lax.psum_scatter(
        jnp.concatenate([down_part, output_part], axis=1), ALL, scatter_dimension=0, tiled=True
    )[0].astype(F32)
    owned_gate = reduce_staged(staged_grad(normed_mlp, grad_gate_in, place_b), STAGES_B)
    owned_up = reduce_staged(staged_grad(normed_mlp, grad_up_in, place_c), STAGES_C)

    grad_qkv = attend_backward(qkv, grad_heads[:, 0], totals, cos_all, sin_all)
    grad_qkv = by_pair(exchange(grad_qkv, 3))

    loss_rows = jnp.sum(token_loss.reshape(-1, 64), axis=0)
    loss_rows = jnp.concatenate([jnp.zeros((PAIR - 64,), F32), loss_rows])[:, None]
    grad_in, grad_first, part_b, part_c = last(
        grad_qkv, normed, x_low, gain_a, first_w, grad_hidden, gain_part_m, loss_rows, place_b, place_c
    )
    owned_b = reduce_staged(part_b, STAGES_B)
    owned_c = reduce_staged(part_c, STAGES_C)
    half = width // 2
    owned_tail = owned_c[:, width + half :]
    loss_value = jnp.sum(owned_tail[0, PAIR - 64 :]) / valid_total
    return (
        result.reshape(batch, local_len, width),
        loss_value,
        grad_in.reshape(batch, local_len, width),
        grad_first.reshape(batch, local_len, width),
        owned_tail[:, 0],
        owned_b[:, :width],
        owned_c[:, :width],
        jnp.concatenate([owned_b[:, width:], owned_c[:, width : width + half]], axis=1),
        owned_rest[own_down:],
        owned_tail[:, 1],
        owned_gate,
        owned_up,
        owned_rest[:own_down],
    )


def solution(mesh):
    seqs, dps = mesh.devices.shape
    fine = Mesh(mesh.devices.reshape(seqs // 2, 2, dps // 2, 2), ALL)
    tokens = P(("x", "c"), SEQ, None)
    rows = P(ALL, None)
    gain = P(ALL)
    return jax.shard_map(
        on_device,
        mesh=fine,
        in_specs=(
            tokens, tokens, tokens, tokens, P(("x", "c"), SEQ), gain, rows, rows, rows, rows, gain, rows, rows, rows,
        ),
        out_specs=(
            tokens, P(), tokens, tokens, gain, rows, rows, rows, rows, gain, rows, rows, rows,
        ),
        check_vma=False,
    )
```

```python
import functools

import jax
import jax.numpy as jnp
from jax import lax
from jax.experimental import pallas as pl
from jax.experimental.pallas import tpu as pltpu
from jax.sharding import Mesh
from jax.sharding import PartitionSpec as P

HEAD_DIM = 64
BLOCK = 256
PAIR = 2 * HEAD_DIM

EPSILON = 1e-06
THETA = 10000.0
SCALE = 0.125
ALL = ("z", "y", "x", "c")
SEQ = ("z", "y")
F32 = jnp.float32
BF16 = jnp.bfloat16


def rotary_tables(positions):
    lane = jnp.arange(PAIR, dtype=jnp.int32)
    half = HEAD_DIM // 2
    index = (lane % half).astype(F32)
    frequency = THETA ** (-(index * 2.0 / HEAD_DIM))
    angles = positions.astype(F32)[:, None] * frequency[None, :]
    sign = jnp.where(lane % HEAD_DIM < half, -1.0, 1.0)[None, :]
    return jnp.cos(angles), jnp.sin(angles) * sign


def partner(values):
    half = HEAD_DIM // 2
    lane = lax.broadcasted_iota(jnp.int32, values.shape, values.ndim - 1)
    first = lane % HEAD_DIM < half
    width = values.shape[-1]
    return jnp.where(
        first,
        pltpu.roll(values, width - half, values.ndim - 1),
        pltpu.roll(values, half, values.ndim - 1),
    )


def dot_t(left, right):
    return lax.dot_general(left, right, (((1,), (1,)), ((), ())), preferred_element_type=F32)


def t_dot(left, right):
    return lax.dot_general(left, right, (((0,), (0,)), ((), ())), preferred_element_type=F32)


def dot(left, right):
    return jnp.dot(left, right, preferred_element_type=F32)


def attend_forward_kernel(qkv_ref, out_ref, total_ref):
    parts, _, _, rows, _ = qkv_ref.shape
    per_block = BLOCK // rows
    blocks = parts // per_block
    for head in range(2):
        lanes = pl.ds(head * HEAD_DIM, HEAD_DIM)
        for block in range(blocks):
            lo, hi = block * per_block, (block + 1) * per_block
            query = qkv_ref[lo:hi, 0, 0, :, lanes].reshape(BLOCK, HEAD_DIM)
            keys = qkv_ref[0:hi, 1, 0, :, lanes].reshape(hi * rows, HEAD_DIM)
            values = qkv_ref[0:hi, 2, 0, :, lanes].reshape(hi * rows, HEAD_DIM)
            scores = dot_t(keys, query) * SCALE
            top = jnp.max(scores, axis=0, keepdims=True)
            total = top + jnp.log(jnp.sum(jnp.exp(scores - top), axis=0, keepdims=True))
            probs = jnp.exp(scores - total).astype(BF16)
            mixed = t_dot(values, probs)
            out_ref[lo:hi, 0, :, lanes] = mixed.T.astype(BF16).reshape(per_block, rows, HEAD_DIM)
            total_ref[0, head, block : block + 1, :] = total


def attend_backward_kernel(qkv_ref, grad_ref, total_ref, cos_ref, sin_ref, out_ref, dk_acc, dv_acc):
    parts, _, _, rows, _ = qkv_ref.shape
    per_block = BLOCK // rows
    blocks = parts // per_block
    dk_acc[...] = jnp.zeros_like(dk_acc)
    dv_acc[...] = jnp.zeros_like(dv_acc)
    for block in range(blocks):
        lo, hi = block * per_block, (block + 1) * per_block
        keys_n = hi * rows
        dq_parts = []
        for head in range(2):
            lanes = pl.ds(head * HEAD_DIM, HEAD_DIM)
            query = qkv_ref[lo:hi, 0, 0, :, lanes].reshape(BLOCK, HEAD_DIM)
            grad = grad_ref[lo:hi, 0, :, lanes].reshape(BLOCK, HEAD_DIM)
            keys = qkv_ref[0:hi, 1, 0, :, lanes].reshape(keys_n, HEAD_DIM)
            values = qkv_ref[0:hi, 2, 0, :, lanes].reshape(keys_n, HEAD_DIM)
            scores = dot_t(keys, query) * SCALE
            probs = jnp.exp(scores - total_ref[0, head, block : block + 1, :])
            grad_probs = dot_t(values, grad)
            inner = jnp.sum(probs * grad_probs, axis=0, keepdims=True)
            grad_scores = (probs * (grad_probs - inner)).astype(BF16)
            dk_acc[0:keys_n, lanes] += dot(grad_scores, query) * SCALE
            dv_acc[0:keys_n, lanes] += dot(probs.astype(BF16), grad)
            dq_parts.append(t_dot(keys, grad_scores).T * SCALE)
        dq = jnp.concatenate(dq_parts, axis=1)
        cos = cos_ref[block * BLOCK : (block + 1) * BLOCK, :]
        sin = sin_ref[block * BLOCK : (block + 1) * BLOCK, :]
        dq = (dq * cos - partner(dq) * sin).astype(BF16)
        out_ref[lo:hi, 0, 0, :, :] = dq.reshape(per_block, rows, PAIR)
    dk = dk_acc[...]
    dk = (dk * cos_ref[...] - partner(dk) * sin_ref[...]).astype(BF16)
    out_ref[:, 1, 0, :, :] = dk.reshape(parts, rows, PAIR)
    out_ref[:, 2, 0, :, :] = dv_acc[...].astype(BF16).reshape(parts, rows, PAIR)


VMEM_LIMIT = 60 * 1024 * 1024


def attend_backward(qkv, grad_att, totals, cos, sin):
    parts, _, units, rows, _ = qkv.shape
    length = parts * rows
    blocks = length // BLOCK
    return pl.pallas_call(
        attend_backward_kernel,
        grid=(units,),
        in_specs=[
            pl.BlockSpec((parts, 3, 1, rows, PAIR), lambda u: (0, 0, u, 0, 0)),
            pl.BlockSpec((parts, 1, rows, PAIR), lambda u: (0, u, 0, 0)),
            pl.BlockSpec((1, 2, blocks, BLOCK), lambda u: (u, 0, 0, 0)),
            pl.BlockSpec((length, PAIR), lambda u: (0, 0)),
            pl.BlockSpec((length, PAIR), lambda u: (0, 0)),
        ],
        out_specs=pl.BlockSpec((parts, 3, 1, rows, PAIR), lambda u: (0, 0, u, 0, 0)),
        out_shape=jax.ShapeDtypeStruct((parts, 3, units, rows, PAIR), BF16),
        scratch_shapes=[pltpu.VMEM((length, PAIR), F32), pltpu.VMEM((length, PAIR), F32)],
        compiler_params=pltpu.CompilerParams(vmem_limit_bytes=VMEM_LIMIT),
        name="attend_backward",
    )(qkv, grad_att, totals, cos, sin)


def swap(array, name, distance):
    size = lax.axis_size(name)
    return lax.ppermute(array, name, [(i, i ^ distance) for i in range(size)])


def arrange(pieces, at):
    bit = 1
    while bit < len(pieces):
        odd = (at & bit) != 0
        pieces = [jnp.where(odd, pieces[j ^ bit], pieces[j]) for j in range(len(pieces))]
        bit *= 2
    return pieces


def gather_rows(shard, order):
    value = shard
    held = []
    for name in order:
        at = lax.axis_index(name)
        pieces = [value] + [swap(value, name, k) for k in range(1, lax.axis_size(name))]
        held.append(name)
        held.sort(key=ALL.index)
        value = jnp.stack(arrange(pieces, at), axis=held.index(name))
    return value.reshape(-1, shard.shape[1])


def stage_rows(rows, order, relative=ALL):
    sizes = [lax.axis_size(name) for name in order]
    per = rows // functools.reduce(lambda a, b: a * b, sizes)
    index = lax.broadcasted_iota(jnp.int32, (rows, 1), 0)
    left, inner = index // per, index % per
    place = {}
    for name, size in zip(reversed(order), reversed(sizes)):
        place[name] = left % size
        if name in relative:
            place[name] = place[name] ^ lax.axis_index(name)
        left = left // size
    device = jnp.zeros_like(index)
    for name in ALL:
        device = device * lax.axis_size(name) + place[name]
    return device * per + inner


def reduce_staged(sent, kept, order):
    columns = kept.shape[1]
    value = kept.astype(F32) + swap(sent, order[0], 1).astype(F32)
    for name in order[1:]:
        size = lax.axis_size(name)
        value = value.astype(BF16).reshape(size, -1, columns)
        received = [swap(value[k], name, k) for k in range(1, size)]
        value = value[0].astype(F32)
        for piece in received:
            value = value + piece.astype(F32)
    return value


def params():
    return pltpu.CompilerParams(vmem_limit_bytes=VMEM_LIMIT)


def front_kernel(
    x_ref, first_ref, gain_ref, cos_ref, sin_ref, weight_ref, normed_ref, qkv_ref, att_ref, total_ref
):
    parts, _, rows, width = x_ref.shape
    per_block = BLOCK // rows
    blocks = parts // per_block
    gain = gain_ref[...]
    for block in range(blocks):
        lo, hi = block * per_block, (block + 1) * per_block
        x = x_ref[lo:hi, 0].reshape(BLOCK, width).astype(F32)
        inv = lax.rsqrt(jnp.mean(x * x, axis=-1, keepdims=True) + EPSILON)
        normed = (x * inv * gain).astype(BF16)
        normed_ref[lo:hi, 0] = normed.reshape(per_block, rows, width)
        cos = cos_ref[block * BLOCK : (block + 1) * BLOCK, :]
        sin = sin_ref[block * BLOCK : (block + 1) * BLOCK, :]
        for kind in range(2):
            value = dot(normed, weight_ref[kind])
            value = (value * cos + partner(value) * sin).astype(BF16)
            qkv_ref[lo:hi, kind, 0] = value.reshape(per_block, rows, PAIR)
        first = first_ref[lo:hi, 0].reshape(BLOCK, PAIR).astype(F32)
        mixed = (0.5 * dot(normed, weight_ref[2]) + 0.5 * first).astype(BF16)
        qkv_ref[lo:hi, 2, 0] = mixed.reshape(per_block, rows, PAIR)
    attend_forward_kernel(qkv_ref, att_ref, total_ref)


def front(x, first, gain, cos, sin, weights):
    parts, units, rows, width = x.shape
    length = parts * rows
    blocks = length // BLOCK
    return pl.pallas_call(
        front_kernel,
        grid=(units,),
        in_specs=[
            pl.BlockSpec((parts, 1, rows, width), lambda u: (0, u, 0, 0)),
            pl.BlockSpec((parts, 1, rows, PAIR), lambda u: (0, u, 0, 0)),
            pl.BlockSpec((1, width), lambda u: (0, 0)),
            pl.BlockSpec((length, PAIR), lambda u: (0, 0)),
            pl.BlockSpec((length, PAIR), lambda u: (0, 0)),
            pl.BlockSpec((3, width, PAIR), lambda u: (0, 0, 0)),
        ],
        out_specs=[
            pl.BlockSpec((parts, 1, rows, width), lambda u: (0, u, 0, 0)),
            pl.BlockSpec((parts, 3, 1, rows, PAIR), lambda u: (0, 0, u, 0, 0)),
            pl.BlockSpec((parts, 1, rows, PAIR), lambda u: (0, u, 0, 0)),
            pl.BlockSpec((1, 2, blocks, BLOCK), lambda u: (u, 0, 0, 0)),
        ],
        out_shape=[
            jax.ShapeDtypeStruct((parts, units, rows, width), BF16),
            jax.ShapeDtypeStruct((parts, 3, units, rows, PAIR), BF16),
            jax.ShapeDtypeStruct((parts, units, rows, PAIR), BF16),
            jax.ShapeDtypeStruct((units, 2, blocks, BLOCK), F32),
        ],
        compiler_params=params(),
        name="front",
    )(x, first, gain, cos, sin, weights)


def join_kernel(
    x_ref, heads_ref, weight_ref, gain_ref, pick_b_ref, pick_c_ref,
    att_ref, hidden_ref, scaled_ref, inv_ref, normed_ref, turned_b_ref, turned_c_ref,
):
    pairs = heads_ref.shape[0]
    tokens = x_ref.shape[0]
    for pair in range(pairs):
        att_ref[:, pair * PAIR : (pair + 1) * PAIR] = heads_ref[pair].reshape(tokens, PAIR)
    hidden = x_ref[...].astype(F32) + dot(att_ref[...], weight_ref[...])
    inv = lax.rsqrt(jnp.mean(hidden * hidden, axis=-1, keepdims=True) + EPSILON)
    scaled = hidden * inv
    hidden_ref[...] = hidden
    scaled_ref[...] = scaled
    inv_ref[...] = jnp.broadcast_to(inv, inv_ref.shape)
    normed = (scaled * gain_ref[...]).astype(BF16)
    normed_ref[...] = normed
    turned_b_ref[...] = dot_t(pick_b_ref[...], normed).astype(BF16)
    turned_c_ref[...] = dot_t(pick_c_ref[...], normed).astype(BF16)


def join(x, heads, weight, gain, pick_b, pick_c):
    tokens, width = x.shape
    return pl.pallas_call(
        join_kernel,
        out_shape=[
            jax.ShapeDtypeStruct((tokens, width), BF16),
            jax.ShapeDtypeStruct((tokens, width), F32),
            jax.ShapeDtypeStruct((tokens, width), F32),
            jax.ShapeDtypeStruct((tokens, PAIR), F32),
            jax.ShapeDtypeStruct((tokens, width), BF16),
            jax.ShapeDtypeStruct((width, tokens), BF16),
            jax.ShapeDtypeStruct((width, tokens), BF16),
        ],
        compiler_params=params(),
        name="join",
    )(x, heads, weight, gain, pick_b, pick_c)


def split_kernel(grad_ref, weight_ref, out_ref):
    value = dot_t(grad_ref[...], weight_ref[...]).astype(BF16)
    pairs, groups, _, units, rows, _ = out_ref.shape
    for pair in range(pairs):
        out_ref[pair, :, 0] = value[:, pair * PAIR : (pair + 1) * PAIR].reshape(groups, units, rows, PAIR)


def split(grad, weight, groups, units):
    tokens, width = grad.shape
    return pl.pallas_call(
        split_kernel,
        out_shape=jax.ShapeDtypeStruct(
            (width // PAIR, groups, 1, units, tokens // (groups * units), PAIR), BF16
        ),
        compiler_params=params(),
        name="split",
    )(grad, weight)


def picker(place, width):
    lane = lax.broadcasted_iota(jnp.int32, (place.shape[0], width), 1)
    return jnp.where(lane == place, 1.0, 0.0).astype(BF16)


def head_grads_kernel(normed_ref, grads_ref, loss_ref, pick_ref, out_ref, turned):
    unit = pl.program_id(0)
    parts, _, rows, width = normed_ref.shape
    normed = normed_ref[...].reshape(parts * rows, width)
    for kind in range(3):
        grad = grads_ref[:, kind, 0].reshape(parts * rows, PAIR)
        value = t_dot(grad, normed)
        if kind == 2:
            value = 0.5 * value
        at = pl.ds(kind * PAIR, PAIR)
        turned[at, :] = jnp.where(unit == 0, value, turned[at, :] + value)

    @pl.when(unit == pl.num_programs(0) - 1)
    def _():
        out_ref[:, : 3 * PAIR] = dot_t(pick_ref[...], turned[...].astype(BF16)).astype(BF16)
        out_ref[:, 3 * PAIR :] = jnp.broadcast_to(loss_ref[...], (width, PAIR)).astype(BF16)


def head_grads(normed, grads, loss_row, pick):
    parts, units, rows, width = normed.shape
    return pl.pallas_call(
        head_grads_kernel,
        grid=(units,),
        in_specs=[
            pl.BlockSpec((parts, 1, rows, width), lambda u: (0, u, 0, 0)),
            pl.BlockSpec((parts, 3, 1, rows, PAIR), lambda u: (0, 0, u, 0, 0)),
            pl.BlockSpec((1, PAIR), lambda u: (0, 0)),
            pl.BlockSpec((width, width), lambda u: (0, 0)),
        ],
        out_specs=pl.BlockSpec((width, 4 * PAIR), lambda u: (0, 0)),
        out_shape=jax.ShapeDtypeStruct((width, 4 * PAIR), BF16),
        scratch_shapes=[pltpu.VMEM((3 * PAIR, width), F32)],
        compiler_params=params(),
        name="head_grads",
    )(normed, grads, loss_row, pick)


def last_kernel(heads_ref, x_ref, gain_ref, weight_ref, grad_hidden_ref, grad_in_ref, first_ref, grads):
    pairs = heads_ref.shape[0]
    tokens, width = x_ref.shape
    for kind in range(3):
        for pair in range(pairs):
            at = kind * width + pair * PAIR
            piece = heads_ref[pair, :, kind].reshape(tokens, PAIR)
            if kind == 2:
                half = 0.5 * piece.astype(F32)
                first_ref[:, pair * PAIR : (pair + 1) * PAIR] = half
                piece = half.astype(BF16)
            grads[:, at : at + PAIR] = piece
    grad_norm = dot_t(grads[...], weight_ref[...])
    x = x_ref[...].astype(F32)
    inv = lax.rsqrt(jnp.mean(x * x, axis=-1, keepdims=True) + EPSILON)
    scaled = x * inv
    scaled_grad = grad_norm * gain_ref[...]
    grad_in_ref[...] = grad_hidden_ref[...] + inv * (
        scaled_grad - scaled * jnp.mean(scaled_grad * scaled, axis=-1, keepdims=True)
    )


def last(heads, x, gain, weights, grad_hidden):
    tokens, width = x.shape
    return pl.pallas_call(
        last_kernel,
        out_shape=[
            jax.ShapeDtypeStruct((tokens, width), F32),
            jax.ShapeDtypeStruct((tokens, width), F32),
        ],
        scratch_shapes=[pltpu.VMEM((tokens, 3 * width), BF16)],
        compiler_params=params(),
        name="last",
    )(heads, x, gain, weights, grad_hidden)


STAGES_B = ("c", "y", "x", "z")
STAGES_C = ("c", "x", "y", "z")
STAGES_H = ("c", "x", "z", "y")


def on_device(
    inputs,
    first_values,
    teacher_states,
    out_cotangent,
    token_valid,
    attn_gain,
    w_query,
    w_key,
    w_value,
    w_output,
    mlp_gain,
    w_gate,
    w_up,
    w_down,
):
    batch, local_len, width = inputs.shape
    seqs = lax.axis_size(SEQ)
    devices = lax.axis_size(ALL)
    tokens = batch * local_len
    length = local_len * seqs
    pairs = width // PAIR
    own_rows = w_query.shape[0]
    own_down = w_down.shape[0]
    hidden = w_gate.shape[1]
    groups = seqs // pairs
    units = batch // groups
    my_group = lax.axis_index(SEQ) % groups

    def gather_positions(value):
        for name in ("z", "y"):
            pieces = [value] + [swap(value, name, k) for k in range(1, lax.axis_size(name))]
            value = jnp.stack(arrange(pieces, lax.axis_index(name)), axis=-3)
        return value.reshape(seqs, local_len, width)

    x_all = jnp.stack([gather_positions(inputs[b]) for b in range(batch)], axis=1)
    x_all = lax.dynamic_slice_in_dim(x_all, my_group * units, units, 1)

    valid_float = token_valid.astype(F32)
    count = jnp.sum(token_valid)
    extra = jnp.stack(
        [
            attn_gain,
            mlp_gain,
            jnp.full((own_rows,), count // 256, jnp.int32).astype(BF16),
            jnp.full((own_rows,), count % 256, jnp.int32).astype(BF16),
        ],
        axis=1,
    )
    extra = jnp.pad(extra, ((0, 0), (0, PAIR - 4)))
    columns = jnp.stack([w_query, w_key, w_value]).reshape(3, own_rows, pairs, PAIR)
    columns = jnp.concatenate(
        [columns, jnp.broadcast_to(extra[None, :, None, :], (1, own_rows, pairs, PAIR))]
    )
    columns = columns.transpose(2, 0, 1, 3).reshape(pairs, 1, 4 * own_rows, PAIR)
    columns = jnp.broadcast_to(columns, (pairs, groups, 4 * own_rows, PAIR))
    firsts = first_values.reshape(groups, units, local_len, pairs, PAIR)
    firsts = firsts.transpose(3, 0, 1, 2, 4).reshape(pairs, groups, units * local_len, PAIR)
    parcel = jnp.concatenate([columns, firsts], axis=2).reshape(seqs, -1, PAIR)
    parcel = lax.all_to_all(parcel, SEQ, split_axis=0, concat_axis=0, tiled=True)
    first_all = parcel[:, 4 * own_rows :].reshape(seqs, units, local_len, PAIR)
    head_w = parcel[:, : 4 * own_rows].reshape(seqs, 4, own_rows, PAIR).transpose(1, 0, 2, 3)
    for at, name in ((2, "x"), (3, "c")):
        pieces = [head_w] + [swap(head_w, name, k) for k in range(1, lax.axis_size(name))]
        head_w = jnp.stack(arrange(pieces, lax.axis_index(name)), axis=at)
    head_w = head_w.reshape(4, width, PAIR)
    extra_all = head_w[3].astype(F32).T
    gain_a = extra_all[0:1, :]
    gain_m = extra_all[1:2, :]
    valid_total = jnp.sum(extra_all[2] * 256.0 + extra_all[3]) / own_rows

    mlp_w = lax.all_gather(jnp.concatenate([w_gate, w_up, w_output], axis=1), ALL, axis=0, tiled=True)
    down_w = gather_rows(w_down, ("z", "y", "x", "c"))
    attn_w = lax.all_gather(jnp.concatenate([w_query, w_key, w_value], axis=1), ALL, axis=0, tiled=True)
    gate_w = mlp_w[:, :hidden]
    up_w = mlp_w[:, hidden : 2 * hidden]
    output_w = mlp_w[:, 2 * hidden :]

    cos_all, sin_all = rotary_tables(jnp.arange(length, dtype=jnp.int32))
    pick_b = picker(stage_rows(width, STAGES_B), width)
    pick_c = picker(stage_rows(width, STAGES_C), width)
    pick_h = picker(stage_rows(width, STAGES_H, ("c", "x")), width)

    normed_all, qkv, attended, totals = front(x_all, first_all, gain_a, cos_all, sin_all, head_w[:3])

    def exchange(array):
        return lax.all_to_all(array, SEQ, split_axis=0, concat_axis=0, tiled=True)

    att_heads = exchange(attended).reshape(pairs, groups, units, local_len, PAIR)
    x_low = inputs.reshape(tokens, width)
    att_low, hidden_in, scaled_m, inv_wide, normed_mlp, turned_b, turned_c = join(
        x_low, att_heads, output_w, gain_m, pick_b, pick_c
    )
    inv_rms_m = inv_wide[:, :1]
    gate_pre = dot(normed_mlp, gate_w)
    up_part = dot(normed_mlp, up_w)
    gate_sigmoid = jax.nn.sigmoid(gate_pre)
    swish_value = gate_pre * gate_sigmoid
    activated = (swish_value * up_part).astype(BF16)
    result = hidden_in + dot(activated, down_w)
    residual_err = result - teacher_states.astype(F32).reshape(tokens, width)
    valid_rows = valid_float.reshape(tokens, 1)
    token_loss = valid_rows * jnp.mean(residual_err * residual_err, axis=-1, keepdims=True)
    grad_out = (
        out_cotangent.astype(F32).reshape(tokens, width)
        + 2.0 / width * valid_rows * residual_err / valid_total
    )

    grad_down_in = grad_out.astype(BF16)
    grad_act = dot_t(grad_down_in, down_w)
    swish_slope = gate_sigmoid * (1.0 + gate_pre * (1.0 - gate_sigmoid))
    grad_gate_in = (grad_act * up_part * swish_slope).astype(BF16)
    grad_up_in = (grad_act * swish_value).astype(BF16)
    half = width // 2
    gate_sent = dot(turned_b[half:], grad_gate_in).astype(BF16)
    up_sent = dot(turned_c[half:], grad_up_in).astype(BF16)
    gate_kept = dot(turned_b[:half], grad_gate_in)
    up_kept = dot(turned_c[:half], grad_up_in)
    owned_gate = reduce_staged(gate_sent, gate_kept, STAGES_B)
    owned_up = reduce_staged(up_sent, up_kept, STAGES_C)
    grad_norm_m = dot_t(grad_gate_in, gate_w) + dot_t(grad_up_in, up_w)
    scaled_grad_m = grad_norm_m * gain_m
    grad_hidden = grad_out + inv_rms_m * (
        scaled_grad_m - scaled_m * jnp.mean(scaled_grad_m * scaled_m, axis=-1, keepdims=True)
    )
    grad_branch = grad_hidden.astype(BF16)
    grad_heads = split(grad_branch, output_w, groups, units)
    grad_heads = exchange(grad_heads.reshape(seqs, units, local_len, PAIR))

    down_part = t_dot(activated, grad_down_in).astype(BF16).reshape(devices, own_down, width)
    output_part = t_dot(att_low, grad_branch).astype(BF16).reshape(devices, own_rows, width)
    owned_rest = lax.psum_scatter(
        jnp.concatenate([down_part, output_part], axis=1), ALL, scatter_dimension=0, tiled=True
    )[0].astype(F32)

    grad_qkv = attend_backward(qkv, grad_heads, totals, cos_all, sin_all)
    grad_own = exchange(grad_qkv).reshape(pairs, groups, 3, units, local_len, PAIR)

    loss_row = jnp.sum(token_loss.reshape(-1, PAIR), axis=0)[None, :]
    value = head_grads(normed_all, grad_qkv, loss_row, pick_h)
    for name in ("c", "x"):
        size = lax.axis_size(name)
        value = value.reshape(size, -1, 4 * PAIR)
        received = [swap(value[k], name, k) for k in range(1, size)]
        value = value[0].astype(F32)
        for piece in received:
            value = value + piece.astype(F32)
        value = value.astype(BF16)
    value = exchange(value.reshape(seqs, own_rows, 4 * PAIR))
    loss_value = jnp.sum(value[:, 0, 3 * PAIR :].astype(F32)) / valid_total
    value = value[:, :, : 3 * PAIR].reshape(pairs, groups, own_rows, 3, PAIR).astype(F32).sum(1)
    owned_qkv = value.transpose(2, 1, 0, 3).reshape(3, own_rows, width)

    grad_in, grad_first = last(grad_own, x_low, gain_a, attn_w, grad_hidden)

    gain_grad_a = (
        jnp.sum(w_query.astype(F32) * owned_qkv[0], axis=1)
        + jnp.sum(w_key.astype(F32) * owned_qkv[1], axis=1)
        + jnp.sum(w_value.astype(F32) * owned_qkv[2], axis=1)
    ) / attn_gain.astype(F32)
    gain_grad_m = (
        jnp.sum(w_gate.astype(F32) * owned_gate, axis=1) + jnp.sum(w_up.astype(F32) * owned_up, axis=1)
    ) / mlp_gain.astype(F32)
    return (
        result.reshape(batch, local_len, width),
        loss_value,
        grad_in.reshape(batch, local_len, width),
        grad_first.reshape(batch, local_len, width),
        gain_grad_a,
        owned_qkv[0],
        owned_qkv[1],
        owned_qkv[2],
        owned_rest[own_down:],
        gain_grad_m,
        owned_gate,
        owned_up,
        owned_rest[:own_down],
    )


def solution(mesh):
    seqs, dps = mesh.devices.shape
    fine = Mesh(mesh.devices.reshape(seqs // 2, 2, dps // 2, 2), ALL)
    tokens = P(("x", "c"), SEQ, None)
    rows = P(ALL, None)
    gain = P(ALL)
    return jax.shard_map(
        on_device,
        mesh=fine,
        in_specs=(
            tokens, tokens, tokens, tokens, P(("x", "c"), SEQ), gain, rows, rows, rows, rows, gain, rows, rows, rows,
        ),
        out_specs=(
            tokens, P(), tokens, tokens, gain, rows, rows, rows, rows, gain, rows, rows, rows,
        ),
        check_vma=False,
    )
```

```python
import functools

import jax
import jax.numpy as jnp
from jax import lax
from jax.experimental import pallas as pl
from jax.experimental.pallas import tpu as pltpu
from jax.sharding import Mesh
from jax.sharding import PartitionSpec as P

HEAD_DIM = 64
BLOCK = 256
PAIR = 2 * HEAD_DIM

EPSILON = 1e-06
THETA = 10000.0
SCALE = 0.125
ALL = ("z", "y", "x", "c")
SEQ = ("z", "y")
F32 = jnp.float32
BF16 = jnp.bfloat16


def rotary_tables(positions):
    lane = jnp.arange(PAIR, dtype=jnp.int32)
    half = HEAD_DIM // 2
    index = (lane % half).astype(F32)
    frequency = THETA ** (-(index * 2.0 / HEAD_DIM))
    angles = positions.astype(F32)[:, None] * frequency[None, :]
    sign = jnp.where(lane % HEAD_DIM < half, -1.0, 1.0)[None, :]
    return jnp.cos(angles), jnp.sin(angles) * sign


def partner(values):
    half = HEAD_DIM // 2
    lane = lax.broadcasted_iota(jnp.int32, values.shape, values.ndim - 1)
    first = lane % HEAD_DIM < half
    width = values.shape[-1]
    return jnp.where(
        first,
        pltpu.roll(values, width - half, values.ndim - 1),
        pltpu.roll(values, half, values.ndim - 1),
    )


def dot_t(left, right):
    return lax.dot_general(left, right, (((1,), (1,)), ((), ())), preferred_element_type=F32)


def t_dot(left, right):
    return lax.dot_general(left, right, (((0,), (0,)), ((), ())), preferred_element_type=F32)


def dot(left, right):
    return jnp.dot(left, right, preferred_element_type=F32)


def attend_forward_kernel(qkv_ref, out_ref, total_ref):
    parts, _, _, rows, _ = qkv_ref.shape
    per_block = BLOCK // rows
    blocks = parts // per_block
    for head in range(2):
        lanes = pl.ds(head * HEAD_DIM, HEAD_DIM)
        for block in range(blocks):
            lo, hi = block * per_block, (block + 1) * per_block
            query = qkv_ref[lo:hi, 0, 0, :, lanes].reshape(BLOCK, HEAD_DIM)
            keys = qkv_ref[0:hi, 1, 0, :, lanes].reshape(hi * rows, HEAD_DIM)
            values = qkv_ref[0:hi, 2, 0, :, lanes].reshape(hi * rows, HEAD_DIM)
            scores = dot_t(keys, query) * SCALE
            top = jnp.max(scores, axis=0, keepdims=True)
            total = top + jnp.log(jnp.sum(jnp.exp(scores - top), axis=0, keepdims=True))
            probs = jnp.exp(scores - total).astype(BF16)
            mixed = t_dot(values, probs)
            out_ref[lo:hi, 0, :, lanes] = mixed.T.astype(BF16).reshape(per_block, rows, HEAD_DIM)
            total_ref[0, head, block : block + 1, :] = total


def attend_backward_kernel(qkv_ref, grad_ref, total_ref, cos_ref, sin_ref, out_ref, dk_acc, dv_acc):
    parts, _, _, rows, _ = qkv_ref.shape
    per_block = BLOCK // rows
    blocks = parts // per_block
    dk_acc[...] = jnp.zeros_like(dk_acc)
    dv_acc[...] = jnp.zeros_like(dv_acc)
    for block in range(blocks):
        lo, hi = block * per_block, (block + 1) * per_block
        keys_n = hi * rows
        dq_parts = []
        for head in range(2):
            lanes = pl.ds(head * HEAD_DIM, HEAD_DIM)
            query = qkv_ref[lo:hi, 0, 0, :, lanes].reshape(BLOCK, HEAD_DIM)
            grad = grad_ref[lo:hi, 0, :, lanes].reshape(BLOCK, HEAD_DIM)
            keys = qkv_ref[0:hi, 1, 0, :, lanes].reshape(keys_n, HEAD_DIM)
            values = qkv_ref[0:hi, 2, 0, :, lanes].reshape(keys_n, HEAD_DIM)
            scores = dot_t(keys, query) * SCALE
            probs = jnp.exp(scores - total_ref[0, head, block : block + 1, :])
            grad_probs = dot_t(values, grad)
            inner = jnp.sum(probs * grad_probs, axis=0, keepdims=True)
            grad_scores = (probs * (grad_probs - inner)).astype(BF16)
            dk_acc[0:keys_n, lanes] += dot(grad_scores, query) * SCALE
            dv_acc[0:keys_n, lanes] += dot(probs.astype(BF16), grad)
            dq_parts.append(t_dot(keys, grad_scores).T * SCALE)
        dq = jnp.concatenate(dq_parts, axis=1)
        cos = cos_ref[block * BLOCK : (block + 1) * BLOCK, :]
        sin = sin_ref[block * BLOCK : (block + 1) * BLOCK, :]
        dq = (dq * cos - partner(dq) * sin).astype(BF16)
        out_ref[lo:hi, 0, 0, :, :] = dq.reshape(per_block, rows, PAIR)
    dk = dk_acc[...]
    dk = (dk * cos_ref[...] - partner(dk) * sin_ref[...]).astype(BF16)
    out_ref[:, 1, 0, :, :] = dk.reshape(parts, rows, PAIR)
    out_ref[:, 2, 0, :, :] = dv_acc[...].astype(BF16).reshape(parts, rows, PAIR)


VMEM_LIMIT = 60 * 1024 * 1024


def attend_backward(qkv, grad_att, totals, cos, sin):
    parts, _, units, rows, _ = qkv.shape
    length = parts * rows
    blocks = length // BLOCK
    return pl.pallas_call(
        attend_backward_kernel,
        grid=(units,),
        in_specs=[
            pl.BlockSpec((parts, 3, 1, rows, PAIR), lambda u: (0, 0, u, 0, 0)),
            pl.BlockSpec((parts, 1, rows, PAIR), lambda u: (0, u, 0, 0)),
            pl.BlockSpec((1, 2, blocks, BLOCK), lambda u: (u, 0, 0, 0)),
            pl.BlockSpec((length, PAIR), lambda u: (0, 0)),
            pl.BlockSpec((length, PAIR), lambda u: (0, 0)),
        ],
        out_specs=pl.BlockSpec((parts, 3, 1, rows, PAIR), lambda u: (0, 0, u, 0, 0)),
        out_shape=jax.ShapeDtypeStruct((parts, 3, units, rows, PAIR), BF16),
        scratch_shapes=[pltpu.VMEM((length, PAIR), F32), pltpu.VMEM((length, PAIR), F32)],
        compiler_params=pltpu.CompilerParams(vmem_limit_bytes=VMEM_LIMIT),
        name="attend_backward",
    )(qkv, grad_att, totals, cos, sin)


def swap(array, name, distance):
    size = lax.axis_size(name)
    return lax.ppermute(array, name, [(i, i ^ distance) for i in range(size)])


def pick(array, index, axis):
    return lax.dynamic_index_in_dim(array, index, axis, keepdims=False)


def arrange(pieces, at):
    bit = 1
    while bit < len(pieces):
        odd = (at & bit) != 0
        pieces = [jnp.where(odd, pieces[j ^ bit], pieces[j]) for j in range(len(pieces))]
        bit *= 2
    return pieces


def stage_rows(rows, order, relative=ALL):
    sizes = [lax.axis_size(name) for name in order]
    per = rows // functools.reduce(lambda a, b: a * b, sizes)
    index = lax.broadcasted_iota(jnp.int32, (rows, 1), 0)
    left, inner = index // per, index % per
    place = {}
    for name, size in zip(reversed(order), reversed(sizes)):
        place[name] = left % size
        if name in relative:
            place[name] = place[name] ^ lax.axis_index(name)
        left = left // size
    device = jnp.zeros_like(index)
    for name in ALL:
        device = device * lax.axis_size(name) + place[name]
    return device * per + inner


def add_stage(value, name):
    size = lax.axis_size(name)
    value = value.astype(BF16).reshape(size, -1, value.shape[1])
    received = [swap(value[k], name, k) for k in range(1, size)]
    value = value[0].astype(F32)
    for piece in received:
        value = value + piece.astype(F32)
    return value


def together(*values):
    return lax.optimization_barrier(values)


def params():
    return pltpu.CompilerParams(vmem_limit_bytes=VMEM_LIMIT)


def front_kernel(
    x_ref, first_ref, gain_ref, cos_ref, sin_ref, weight_ref, normed_ref, qkv_ref, att_ref, total_ref
):
    parts, rows, width = x_ref.shape
    per_block = BLOCK // rows
    blocks = parts // per_block
    gain = gain_ref[...]
    for block in range(blocks):
        lo, hi = block * per_block, (block + 1) * per_block

        @pl.when(pl.program_id(0) == 0)
        def _(lo=lo, hi=hi):
            x = x_ref[lo:hi].reshape(BLOCK, width).astype(F32)
            inv = lax.rsqrt(jnp.mean(x * x, axis=-1, keepdims=True) + EPSILON)
            normed_ref[lo:hi] = (x * inv * gain).astype(BF16).reshape(per_block, rows, width)

        normed = normed_ref[lo:hi].reshape(BLOCK, width)
        cos = cos_ref[block * BLOCK : (block + 1) * BLOCK, :]
        sin = sin_ref[block * BLOCK : (block + 1) * BLOCK, :]
        for kind in range(2):
            value = dot(normed, weight_ref[kind])
            value = (value * cos + partner(value) * sin).astype(BF16)
            qkv_ref[lo:hi, kind, 0] = value.reshape(per_block, rows, PAIR)
        first = first_ref[lo:hi, 0].reshape(BLOCK, PAIR).astype(F32)
        mixed = (0.5 * dot(normed, weight_ref[2]) + 0.5 * first).astype(BF16)
        qkv_ref[lo:hi, 2, 0] = mixed.reshape(per_block, rows, PAIR)
    attend_forward_kernel(qkv_ref, att_ref, total_ref)


def front(x, first, gain, cos, sin, weights):
    parts, rows, width = x.shape
    units = first.shape[1]
    length = parts * rows
    blocks = length // BLOCK
    return pl.pallas_call(
        front_kernel,
        grid=(units,),
        in_specs=[
            pl.BlockSpec((parts, rows, width), lambda u: (0, 0, 0)),
            pl.BlockSpec((parts, 1, rows, PAIR), lambda u: (0, u, 0, 0)),
            pl.BlockSpec((1, width), lambda u: (0, 0)),
            pl.BlockSpec((length, PAIR), lambda u: (0, 0)),
            pl.BlockSpec((length, PAIR), lambda u: (0, 0)),
            pl.BlockSpec((3, width, PAIR), lambda u: (u, 0, 0)),
        ],
        out_specs=[
            pl.BlockSpec((parts, rows, width), lambda u: (0, 0, 0)),
            pl.BlockSpec((parts, 3, 1, rows, PAIR), lambda u: (0, 0, u, 0, 0)),
            pl.BlockSpec((parts, 1, rows, PAIR), lambda u: (0, u, 0, 0)),
            pl.BlockSpec((1, 2, blocks, BLOCK), lambda u: (u, 0, 0, 0)),
        ],
        out_shape=[
            jax.ShapeDtypeStruct((parts, rows, width), BF16),
            jax.ShapeDtypeStruct((parts, 3, units, rows, PAIR), BF16),
            jax.ShapeDtypeStruct((parts, units, rows, PAIR), BF16),
            jax.ShapeDtypeStruct((units, 2, blocks, BLOCK), F32),
        ],
        compiler_params=params(),
        name="front",
    )(x, first, gain, cos, sin, weights)


def sections(weight_ref):
    outer, parts, rows, columns = weight_ref.shape
    return [weight_ref[:, part].reshape(outer * rows, columns) for part in range(parts)]


def dot_sections(left, weight_ref):
    parts = sections(weight_ref)
    wide = left.shape[1] // len(parts)
    total = dot(left[:, :wide], parts[0])
    for at in range(1, len(parts)):
        total = total + dot(left[:, at * wide : (at + 1) * wide], parts[at])
    return total


def dot_t_sections(left, weight_ref):
    return jnp.concatenate([dot_t(left, part) for part in sections(weight_ref)], axis=1)


def forward_kernel(
    x_ref, heads_ref, gain_ref, teacher_ref, cotangent_ref, valid_ref, rate_ref, wo_ref, wg_ref, wu_ref, wd_ref,
    att_ref, hidden_ref, normed_ref, gate_ref, up_ref, act_ref, result_ref, grad_ref, grad_low_ref, loss_ref,
):
    step = pl.program_id(0)
    tokens, width = x_ref.shape

    @pl.when(step == 0)
    def _():
        for pair in range(width // PAIR):
            at, unit = divmod(pair, heads_ref.shape[2])
            att_ref[:, pair * PAIR : (pair + 1) * PAIR] = heads_ref[at, :, unit].reshape(tokens, PAIR)
        hidden = x_ref[...].astype(F32) + dot_sections(att_ref[...], wo_ref)
        inv = lax.rsqrt(jnp.mean(hidden * hidden, axis=-1, keepdims=True) + EPSILON)
        hidden_ref[...] = hidden
        result_ref[...] = hidden
        normed_ref[...] = (hidden * inv * gain_ref[...]).astype(BF16)

    gate = dot_sections(normed_ref[...], wg_ref)
    up = dot_sections(normed_ref[...], wu_ref)
    act = (gate * jax.nn.sigmoid(gate) * up).astype(BF16)
    gate_ref[...] = gate
    up_ref[...] = up
    act_ref[...] = act
    result_ref[...] += dot(act, sections(wd_ref)[0])

    @pl.when(step == pl.num_programs(0) - 1)
    def _():
        error = result_ref[...] - teacher_ref[...].astype(F32)
        valid = valid_ref[...]
        grad = cotangent_ref[...].astype(F32) + rate_ref[0:1, 0:1] * valid * error
        grad_ref[...] = grad
        grad_low_ref[...] = grad.astype(BF16)
        losses = jnp.sum(error * error * (valid / width), axis=0, keepdims=True)
        total = losses[:, :PAIR]
        for at in range(PAIR, width, PAIR):
            total = total + losses[:, at : at + PAIR]
        loss_ref[...] = total


def weight_specs(width, parts, gate_out, rest):
    outer, sides, rows, _ = rest.shape
    wide = outer * rows
    per = width // wide
    whole = (outer, sides, rows)
    return wide, [
        pl.BlockSpec(whole + (width,), lambda j: (0, 0, 0, parts)),
        pl.BlockSpec(whole + (wide,), lambda j: (0, 0, 0, j)),
        pl.BlockSpec(whole + (wide,), lambda j: (0, 0, 0, 3 * per + j)),
        pl.BlockSpec((outer, 1, rows, width), lambda j: (0, j % per, 0, 3 + parts + j // per)),
    ], (gate_out, gate_out, rest, rest)


def still(*shape):
    return pl.BlockSpec(shape, lambda j: (0,) * len(shape))


def mlp_forward(x, heads, gain, teacher, cotangent, valid, rate, gate_out, rest):
    tokens, width = x.shape
    parts = gate_out.shape[3] // width - 1
    wide, specs, weights = weight_specs(width, parts, gate_out, rest)
    moving = pl.BlockSpec((tokens, wide), lambda j: (0, j))
    whole = still(tokens, width)
    hidden = (tokens, parts * width)
    return pl.pallas_call(
        forward_kernel,
        grid=(parts * width // wide,),
        in_specs=[whole, still(*heads.shape), still(1, width), whole, whole, still(tokens, 1), still(1, PAIR)]
        + specs,
        out_specs=[whole, whole, whole, moving, moving, moving, whole, whole, whole, still(1, PAIR)],
        out_shape=[
            jax.ShapeDtypeStruct((tokens, width), BF16),
            jax.ShapeDtypeStruct((tokens, width), F32),
            jax.ShapeDtypeStruct((tokens, width), BF16),
            jax.ShapeDtypeStruct(hidden, F32),
            jax.ShapeDtypeStruct(hidden, F32),
            jax.ShapeDtypeStruct(hidden, BF16),
            jax.ShapeDtypeStruct((tokens, width), F32),
            jax.ShapeDtypeStruct((tokens, width), F32),
            jax.ShapeDtypeStruct((tokens, width), BF16),
            jax.ShapeDtypeStruct((1, PAIR), F32),
        ],
        compiler_params=params(),
        name="mlp_forward",
    )(x, heads, gain, teacher, cotangent, valid, rate, *weights)


def backward_kernel(
    grad_ref, grad_low_ref, hidden_ref, gain_ref, gate_ref, up_ref, wo_ref, wg_ref, wu_ref, wd_ref,
    grads_ref, grad_hidden_ref, branch_ref, heads_ref, total,
):
    step = pl.program_id(0)
    wide = gate_ref.shape[1]
    gate = gate_ref[...]
    up = up_ref[...]
    sigmoid = jax.nn.sigmoid(gate)
    grad_act = dot_t(grad_low_ref[...], sections(wd_ref)[0])
    grad_gate = (grad_act * up * (sigmoid * (1.0 + gate * (1.0 - sigmoid)))).astype(BF16)
    grad_up = (grad_act * (gate * sigmoid)).astype(BF16)
    grads_ref[:, :wide] = grad_gate
    grads_ref[:, wide:] = grad_up
    value = dot_t_sections(grad_gate, wg_ref) + dot_t_sections(grad_up, wu_ref)

    @pl.when(step == 0)
    def _():
        total[...] = value

    @pl.when(step > 0)
    def _():
        total[...] += value

    @pl.when(step == pl.num_programs(0) - 1)
    def _():
        hidden = hidden_ref[...]
        inv = lax.rsqrt(jnp.mean(hidden * hidden, axis=-1, keepdims=True) + EPSILON)
        scaled = hidden * inv
        scaled_grad = total[...] * gain_ref[...]
        grad = grad_ref[...] + inv * (
            scaled_grad - scaled * jnp.mean(scaled_grad * scaled, axis=-1, keepdims=True)
        )
        grad_hidden_ref[...] = grad
        branch = grad.astype(BF16)
        branch_ref[...] = branch
        value = dot_t_sections(branch, wo_ref).astype(BF16)
        _, batch, units, rows, _ = heads_ref.shape
        for pair in range(value.shape[1] // PAIR):
            at, unit = divmod(pair, units)
            heads_ref[at, :, unit] = value[:, pair * PAIR : (pair + 1) * PAIR].reshape(batch, rows, PAIR)


def mlp_backward(grad, grad_low, hidden, gain, gate, up, gate_out, rest, heads):
    tokens, width = grad.shape
    parts = gate_out.shape[3] // width - 1
    wide, specs, weights = weight_specs(width, parts, gate_out, rest)
    moving = pl.BlockSpec((tokens, wide), lambda j: (0, j))
    whole = still(tokens, width)
    return pl.pallas_call(
        backward_kernel,
        grid=(parts * width // wide,),
        in_specs=[whole, whole, whole, still(1, width), moving, moving] + specs,
        out_specs=[pl.BlockSpec((tokens, 2 * wide), lambda j: (0, j)), whole, whole, still(*heads)],
        out_shape=[
            jax.ShapeDtypeStruct((tokens, 2 * parts * width), BF16),
            jax.ShapeDtypeStruct((tokens, width), F32),
            jax.ShapeDtypeStruct((tokens, width), BF16),
            jax.ShapeDtypeStruct(heads, BF16),
        ],
        scratch_shapes=[pltpu.VMEM((tokens, width), F32)],
        compiler_params=params(),
        name="mlp_backward",
    )(grad, grad_low, hidden, gain, gate, up, *weights)


def picker(place, width):
    lane = lax.broadcasted_iota(jnp.int32, (place.shape[0], width), 1)
    return jnp.where(lane == place, 1.0, 0.0).astype(BF16)


def head_grads_kernel(normed_ref, grads_ref, loss_ref, pick_ref, out_ref, turned):
    parts, kinds, units, rows, _ = grads_ref.shape
    width = normed_ref.shape[2]
    normed = normed_ref[...].reshape(parts * rows, width)
    for unit in range(units):
        for kind in range(kinds):
            value = t_dot(grads_ref[:, kind, unit].reshape(parts * rows, PAIR), normed)
            if kind == 2:
                value = 0.5 * value
            at = (unit * kinds + kind) * PAIR
            turned[at : at + PAIR, :] = value.astype(BF16)
    columns = turned.shape[0]
    out_ref[:, :columns] = dot_t(pick_ref[...], turned[...]).astype(BF16)
    out_ref[:, columns:] = jnp.broadcast_to(loss_ref[...], (width, PAIR)).astype(BF16)


def head_grads(normed, grads, loss_row, pick):
    width = normed.shape[2]
    columns = 3 * grads.shape[2] * PAIR
    return pl.pallas_call(
        head_grads_kernel,
        out_shape=jax.ShapeDtypeStruct((width, columns + PAIR), BF16),
        scratch_shapes=[pltpu.VMEM((columns, width), BF16)],
        compiler_params=params(),
        name="head_grads",
    )(normed, grads, loss_row, pick)


def last_kernel(heads_ref, x_ref, gain_ref, weight_ref, grad_hidden_ref, grad_in_ref, first_ref, grads):
    tokens, width = x_ref.shape
    for kind in range(3):
        for pair in range(width // PAIR):
            at = kind * width + pair * PAIR
            place, unit = divmod(pair, heads_ref.shape[3])
            piece = heads_ref[place, :, kind, unit].reshape(tokens, PAIR)
            if kind == 2:
                half = 0.5 * piece.astype(F32)
                first_ref[:, pair * PAIR : (pair + 1) * PAIR] = half
                piece = half.astype(BF16)
            grads[:, at : at + PAIR] = piece
    grad_norm = dot_t_sections(grads[...], weight_ref)
    x = x_ref[...].astype(F32)
    inv = lax.rsqrt(jnp.mean(x * x, axis=-1, keepdims=True) + EPSILON)
    scaled = x * inv
    scaled_grad = grad_norm * gain_ref[...]
    grad_in_ref[...] = grad_hidden_ref[...] + inv * (
        scaled_grad - scaled * jnp.mean(scaled_grad * scaled, axis=-1, keepdims=True)
    )


def last(heads, x, gain, weights, grad_hidden):
    tokens, width = x.shape
    return pl.pallas_call(
        last_kernel,
        grid=(1,),
        in_specs=[
            still(*heads.shape),
            still(tokens, width),
            still(1, width),
            pl.BlockSpec(weights.shape[:3] + (3 * width,), lambda j: (0, 0, 0, 0)),
            still(tokens, width),
        ],
        out_specs=[still(tokens, width), still(tokens, width)],
        out_shape=[
            jax.ShapeDtypeStruct((tokens, width), F32),
            jax.ShapeDtypeStruct((tokens, width), F32),
        ],
        scratch_shapes=[pltpu.VMEM((tokens, 3 * width), BF16)],
        compiler_params=params(),
        name="last",
    )(heads, x, gain, weights, grad_hidden)


STAGES_NATIVE = ("c", "y", "x", "z")
STAGES_OUTPUT = ("c", "z", "y", "x")
STAGES_HEADS = ("c", "x", "y", "z")


def on_device(
    inputs,
    first_values,
    teacher_states,
    out_cotangent,
    token_valid,
    attn_gain,
    w_query,
    w_key,
    w_value,
    w_output,
    mlp_gain,
    w_gate,
    w_up,
    w_down,
):
    batch, local_len, width = inputs.shape
    seqs = lax.axis_size(SEQ)
    tokens = batch * local_len
    length = local_len * seqs
    pairs = width // PAIR
    own_rows = w_query.shape[0]
    own_down = w_down.shape[0]
    zs = lax.axis_size("z")
    units = pairs // zs
    mine = lax.axis_index("y")

    valid_float = token_valid.astype(F32)
    count = jnp.sum(token_valid)
    extra = jnp.stack(
        [
            attn_gain,
            mlp_gain,
            jnp.full((own_rows,), count // 256, jnp.int32).astype(BF16),
            jnp.full((own_rows,), count % 256, jnp.int32).astype(BF16),
        ],
        axis=1,
    )
    extra = jnp.pad(extra, ((0, 0), (0, PAIR - 4)))
    columns = jnp.stack([w_query, w_key, w_value]).reshape(3, own_rows, zs, units, PAIR)
    columns = columns.transpose(2, 3, 0, 1, 4).reshape(zs, 3 * units, own_rows, PAIR)
    columns = jnp.concatenate(
        [columns, jnp.broadcast_to(extra[None, None], (zs, 1, own_rows, PAIR))], axis=1
    )
    blocks = 3 * units + 1
    columns = jnp.broadcast_to(
        columns.reshape(zs, 1, blocks * own_rows, PAIR), (zs, batch, blocks * own_rows, PAIR)
    )
    firsts = first_values.reshape(batch, local_len, zs, units, PAIR).transpose(2, 0, 3, 1, 4)
    firsts = firsts.reshape(zs, batch, units * local_len, PAIR)
    parcel = jnp.concatenate([columns, firsts], axis=2).reshape(seqs, -1, PAIR)

    hidden_parts = -(-own_down // own_rows)
    padded = hidden_parts * own_rows - own_down

    def pack_columns(weight):
        weight = jnp.pad(weight.reshape(own_rows, -1, own_down), ((0, 0), (0, 0), (0, padded)))
        weight = weight.reshape(own_rows, -1, hidden_parts, own_rows)
        return weight.transpose(0, 2, 1, 3).reshape(own_rows, hidden_parts * width)

    def unpack_columns(grad):
        grad = grad.reshape(own_rows, hidden_parts, -1, own_rows).transpose(0, 2, 1, 3)
        return grad.reshape(own_rows, -1, hidden_parts * own_rows)[:, :, :own_down].reshape(own_rows, -1)

    down_rows = jnp.pad(w_down, ((0, padded), (0, 0))).reshape(hidden_parts, own_rows, width)
    down_rows = down_rows.transpose(1, 0, 2).reshape(own_rows, hidden_parts * width)
    def along_z(rows):
        pieces = [rows] + [swap(rows, "z", k) for k in range(1, zs)]
        return jnp.stack(arrange(pieces, lax.axis_index("z")), axis=0)

    def across(rows):
        rows = lax.all_gather(rows, ("y", "x", "c"), axis=0)
        if own_rows % 16:
            rows = rows.transpose(1, 0, 2, 3).reshape(1, width // BLOCK, BLOCK, rows.shape[3])
        return rows

    gate_out = along_z(jnp.concatenate([pack_columns(w_gate), w_output], axis=1))
    rest = jnp.concatenate([w_query, w_key, w_value, pack_columns(w_up), down_rows], axis=1)
    gate_out, rest, parcel = together(gate_out, rest, parcel)
    gate_out = across(gate_out)
    rest = along_z(rest)
    parcel = lax.all_to_all(parcel, SEQ, split_axis=0, concat_axis=0, tiled=True)
    rest, x_own, x_sent = together(rest, pick(inputs, mine, 0), pick(inputs, 1 - mine, 0))
    rest = across(rest)
    pieces = arrange([x_own, swap(x_sent, "y", 1)], mine)
    x_all = along_z(jnp.stack(pieces, axis=0)).reshape(seqs, local_len, width)

    first_all = parcel[:, blocks * own_rows :].reshape(seqs, units, local_len, PAIR)
    head_w = parcel[:, : blocks * own_rows].reshape(seqs, blocks, own_rows, PAIR).transpose(1, 0, 2, 3)
    for at, name in ((2, "x"), (3, "c")):
        pieces = [head_w] + [swap(head_w, name, k) for k in range(1, lax.axis_size(name))]
        head_w = jnp.stack(arrange(pieces, lax.axis_index(name)), axis=at)
    head_w = head_w.reshape(blocks, width, PAIR)
    extra_all = head_w[blocks - 1].astype(F32).T
    gain_a = extra_all[0:1, :]
    gain_m = extra_all[1:2, :]
    valid_total = jnp.sum(extra_all[2] * 256.0 + extra_all[3]) / own_rows

    cos_all, sin_all = rotary_tables(jnp.arange(length, dtype=jnp.int32))
    pick_native = picker(stage_rows(width, STAGES_NATIVE, ("c", "z")), width)
    pick_output = picker(stage_rows(width, STAGES_OUTPUT), width)
    pick_heads = picker(stage_rows(width, STAGES_HEADS, ("c", "x", "y")), width)

    normed_all, qkv, attended, totals = front(x_all, first_all, gain_a, cos_all, sin_all, head_w)

    def exchange(array):
        return lax.all_to_all(array, SEQ, split_axis=0, concat_axis=0, tiled=True)

    att_heads = exchange(attended).reshape(zs, batch, units, local_len, PAIR)
    x_low = inputs.reshape(tokens, width)
    rate = jnp.full((1, PAIR), 2.0 / width, F32) / valid_total
    att_low, hidden_in, normed_mlp, gate, up, activated, result, grad_out, grad_down_in, loss_row = mlp_forward(
        x_low,
        att_heads,
        gain_m,
        teacher_states.reshape(tokens, width),
        out_cotangent.reshape(tokens, width),
        valid_float.reshape(tokens, 1),
        rate,
        gate_out,
        rest,
    )

    half = width // 2
    turned = [
        dot_t(pick_native, activated[:, p * width : (p + 1) * width]).astype(BF16).reshape(-1, own_rows, tokens)
        for p in range(hidden_parts)
    ]
    turned_act = jnp.stack(turned, axis=1).reshape(hidden_parts * width, tokens)
    cut = hidden_parts * half
    down_sent = swap(dot(turned_act[cut:], grad_down_in).astype(BF16), "c", 1)
    down_sum = (dot(turned_act[:cut], grad_down_in) + down_sent.astype(F32)).astype(BF16)
    down_sum, grad_down_in = together(down_sum, grad_down_in)

    def over_yx(value):
        value = value.reshape(2 * lax.axis_size("x"), -1, value.shape[1])
        value = lax.psum_scatter(value, ("y", "x"), scatter_dimension=0, tiled=True)
        return lax.optimization_barrier(value)[0]

    down_sum = over_yx(down_sum)
    grads, grad_hidden, grad_branch, grad_heads = mlp_backward(
        grad_out, grad_down_in, hidden_in, gain_m, gate, up, gate_out, rest, att_heads.shape
    )
    grad_heads = exchange(grad_heads.reshape(seqs, units, local_len, PAIR))
    turned_mlp = dot_t(pick_native, normed_mlp).astype(BF16)
    mlp_sent = swap(dot(turned_mlp[half:], grads).astype(BF16), "c", 1)
    mlp_sum = (dot(turned_mlp[:half], grads) + mlp_sent.astype(F32)).astype(BF16)

    turned_att = dot_t(pick_output, att_low).astype(BF16)
    out_sent = swap(dot(turned_att[half:], grad_branch).astype(BF16), "c", 1)
    out_sum = (dot(turned_att[:half], grad_branch) + out_sent.astype(F32)).astype(BF16)

    grad_heads, mlp_sum, out_sum = together(grad_heads, mlp_sum, out_sum)
    mlp_sum = over_yx(mlp_sum)
    out_sum = add_stage(out_sum, "z").astype(BF16)

    grad_qkv = attend_backward(qkv, grad_heads, totals, cos_all, sin_all)
    grad_own = exchange(grad_qkv).reshape(zs, batch, 3, units, local_len, PAIR)

    value = head_grads(normed_all, grad_qkv, loss_row, pick_heads)
    for name in ("c", "x", "y"):
        value = add_stage(value, name)
    value, grad_own, down_sum, out_sum = together(value.astype(BF16), grad_own, down_sum, out_sum)
    owned_down = add_stage(down_sum, "z")[:own_down]
    owned_output = add_stage(add_stage(out_sum, "y"), "x")
    mlp_sum = add_stage(mlp_sum, "z")
    value = value.reshape(zs, own_rows, value.shape[1])
    value = lax.all_to_all(value, "z", split_axis=0, concat_axis=0, tiled=True)
    columns = 3 * units * PAIR
    loss_value = jnp.sum(value[:, 0, columns:].astype(F32)) / valid_total
    value = value[:, :, :columns].reshape(zs, own_rows, units, 3, PAIR).astype(F32)
    owned_qkv = value.transpose(3, 1, 0, 2, 4).reshape(3, own_rows, width)

    grad_in, grad_first = last(grad_own, x_low, gain_a, rest, grad_hidden)

    gain_grad_a = (
        jnp.sum(w_query.astype(F32) * owned_qkv[0], axis=1)
        + jnp.sum(w_key.astype(F32) * owned_qkv[1], axis=1)
        + jnp.sum(w_value.astype(F32) * owned_qkv[2], axis=1)
    ) / attn_gain.astype(F32)
    mlp_sum = mlp_sum.reshape(own_rows, -1, 2, BLOCK)
    owned_gate = unpack_columns(mlp_sum[:, :, 0])
    owned_up = unpack_columns(mlp_sum[:, :, 1])
    gain_grad_m = (
        jnp.sum(w_gate.astype(F32) * owned_gate, axis=1) + jnp.sum(w_up.astype(F32) * owned_up, axis=1)
    ) / mlp_gain.astype(F32)
    return (
        result.reshape(batch, local_len, width),
        loss_value,
        grad_in.reshape(batch, local_len, width),
        grad_first.reshape(batch, local_len, width),
        gain_grad_a,
        owned_qkv[0],
        owned_qkv[1],
        owned_qkv[2],
        owned_output,
        gain_grad_m,
        owned_gate,
        owned_up,
        owned_down,
    )


def solution(mesh):
    seqs, dps = mesh.devices.shape
    fine = Mesh(mesh.devices.reshape(seqs // 2, 2, dps // 2, 2), ALL)
    tokens = P(("x", "c"), SEQ, None)
    rows = P(ALL, None)
    gain = P(ALL)
    return jax.shard_map(
        on_device,
        mesh=fine,
        in_specs=(
            tokens, tokens, tokens, tokens, P(("x", "c"), SEQ), gain, rows, rows, rows, rows, gain, rows, rows, rows,
        ),
        out_specs=(
            tokens, P(), tokens, tokens, gain, rows, rows, rows, rows, gain, rows, rows, rows,
        ),
        check_vma=False,
    )
```

```python
import functools

import jax
import jax.numpy as jnp
from jax import lax
from jax.experimental import pallas as pl
from jax.experimental.pallas import tpu as pltpu
from jax.sharding import Mesh
from jax.sharding import PartitionSpec as P

HEAD_DIM = 64
BLOCK = 256
MLP_STEP = 512
PAIR = 2 * HEAD_DIM

EPSILON = 1e-06
THETA = 10000.0
SCALE = 0.125
ALL = ("z", "y", "x", "c")
SEQ = ("z", "y")
F32 = jnp.float32
BF16 = jnp.bfloat16


def rotary_tables(positions):
    lane = jnp.arange(PAIR, dtype=jnp.int32)
    half = HEAD_DIM // 2
    index = (lane % half).astype(F32)
    frequency = THETA ** (-(index * 2.0 / HEAD_DIM))
    angles = positions.astype(F32)[:, None] * frequency[None, :]
    sign = jnp.where(lane % HEAD_DIM < half, -1.0, 1.0)[None, :]
    return jnp.cos(angles), jnp.sin(angles) * sign


def partner(values):
    half = HEAD_DIM // 2
    lane = lax.broadcasted_iota(jnp.int32, values.shape, values.ndim - 1)
    first = lane % HEAD_DIM < half
    width = values.shape[-1]
    return jnp.where(
        first,
        pltpu.roll(values, width - half, values.ndim - 1),
        pltpu.roll(values, half, values.ndim - 1),
    )


def dot_t(left, right):
    return lax.dot_general(left, right, (((1,), (1,)), ((), ())), preferred_element_type=F32)


def t_dot(left, right):
    return lax.dot_general(left, right, (((0,), (0,)), ((), ())), preferred_element_type=F32)


def dot(left, right):
    return jnp.dot(left, right, preferred_element_type=F32)


def attend_forward_kernel(qkv_ref, out_ref, total_ref):
    parts, _, _, rows, _ = qkv_ref.shape
    per_block = BLOCK // rows
    blocks = parts // per_block
    for head in range(2):
        lanes = pl.ds(head * HEAD_DIM, HEAD_DIM)
        for block in range(blocks):
            lo, hi = block * per_block, (block + 1) * per_block
            query = qkv_ref[lo:hi, 0, 0, :, lanes].reshape(BLOCK, HEAD_DIM)
            keys = qkv_ref[0:hi, 1, 0, :, lanes].reshape(hi * rows, HEAD_DIM)
            values = qkv_ref[0:hi, 2, 0, :, lanes].reshape(hi * rows, HEAD_DIM)
            scores = dot_t(keys, query * SCALE)
            top = jnp.max(scores, axis=0, keepdims=True)
            weights = jnp.exp(scores - top)
            total = jnp.sum(weights, axis=0, keepdims=True)
            probs = (weights * (1.0 / total)).astype(BF16)
            mixed = t_dot(values, probs)
            out_ref[lo:hi, 0, :, lanes] = mixed.T.astype(BF16).reshape(per_block, rows, HEAD_DIM)
            total_ref[0, head, block : block + 1, :] = top + jnp.log(total)


def attend_backward_kernel(qkv_ref, grad_ref, total_ref, cos_ref, sin_ref, out_ref, dk_acc, dv_acc):
    parts, _, _, rows, _ = qkv_ref.shape
    per_block = BLOCK // rows
    blocks = parts // per_block
    dk_acc[...] = jnp.zeros_like(dk_acc)
    dv_acc[...] = jnp.zeros_like(dv_acc)
    for block in range(blocks):
        lo, hi = block * per_block, (block + 1) * per_block
        keys_n = hi * rows
        dq_parts = []
        for head in range(2):
            lanes = pl.ds(head * HEAD_DIM, HEAD_DIM)
            query = qkv_ref[lo:hi, 0, 0, :, lanes].reshape(BLOCK, HEAD_DIM)
            grad = grad_ref[lo:hi, 0, :, lanes].reshape(BLOCK, HEAD_DIM)
            keys = qkv_ref[0:hi, 1, 0, :, lanes].reshape(keys_n, HEAD_DIM)
            values = qkv_ref[0:hi, 2, 0, :, lanes].reshape(keys_n, HEAD_DIM)
            scores = dot_t(keys, query * SCALE)
            probs = jnp.exp(scores - total_ref[0, head, block : block + 1, :])
            grad_probs = dot_t(values, grad)
            inner = jnp.sum(probs * grad_probs, axis=0, keepdims=True)
            grad_scores = (probs * (grad_probs - inner)).astype(BF16)
            dk_acc[0:keys_n, lanes] += dot(grad_scores, query) * SCALE
            dv_acc[0:keys_n, lanes] += dot(probs.astype(BF16), grad)
            dq_parts.append(t_dot(keys, grad_scores).T * SCALE)
        dq = jnp.concatenate(dq_parts, axis=1)
        cos = cos_ref[block * BLOCK : (block + 1) * BLOCK, :]
        sin = sin_ref[block * BLOCK : (block + 1) * BLOCK, :]
        dq = (dq * cos - partner(dq) * sin).astype(BF16)
        out_ref[lo:hi, 0, 0, :, :] = dq.reshape(per_block, rows, PAIR)
    dk = dk_acc[...]
    dk = (dk * cos_ref[...] - partner(dk) * sin_ref[...]).astype(BF16)
    out_ref[:, 1, 0, :, :] = dk.reshape(parts, rows, PAIR)
    out_ref[:, 2, 0, :, :] = dv_acc[...].astype(BF16).reshape(parts, rows, PAIR)


VMEM_LIMIT = 60 * 1024 * 1024


def attend_backward(qkv, grad_att, totals, cos, sin):
    parts, _, units, rows, _ = qkv.shape
    length = parts * rows
    blocks = length // BLOCK
    return pl.pallas_call(
        attend_backward_kernel,
        grid=(units,),
        in_specs=[
            pl.BlockSpec((parts, 3, 1, rows, PAIR), lambda u: (0, 0, u, 0, 0)),
            pl.BlockSpec((parts, 1, rows, PAIR), lambda u: (0, u, 0, 0)),
            pl.BlockSpec((1, 2, blocks, BLOCK), lambda u: (u, 0, 0, 0)),
            pl.BlockSpec((length, PAIR), lambda u: (0, 0)),
            pl.BlockSpec((length, PAIR), lambda u: (0, 0)),
        ],
        out_specs=pl.BlockSpec((parts, 3, 1, rows, PAIR), lambda u: (0, 0, u, 0, 0)),
        out_shape=jax.ShapeDtypeStruct((parts, 3, units, rows, PAIR), BF16),
        scratch_shapes=[pltpu.VMEM((length, PAIR), F32), pltpu.VMEM((length, PAIR), F32)],
        compiler_params=pltpu.CompilerParams(vmem_limit_bytes=VMEM_LIMIT),
        name="attend_backward",
        cost_estimate=cost(5 * units * length * length * PAIR, 8 * grad_att.size * 8, units * length * length),
    )(qkv, grad_att, totals, cos, sin)


def swap(array, name, distance):
    size = lax.axis_size(name)
    return lax.ppermute(array, name, [(i, i ^ distance) for i in range(size)])


def pick(array, index, axis):
    return lax.dynamic_index_in_dim(array, index, axis, keepdims=False)


def arrange(pieces, at):
    bit = 1
    while bit < len(pieces):
        odd = (at & bit) != 0
        pieces = [jnp.where(odd, pieces[j ^ bit], pieces[j]) for j in range(len(pieces))]
        bit *= 2
    return pieces


def stage_rows(rows, order, relative=ALL):
    sizes = [lax.axis_size(name) for name in order]
    per = rows // functools.reduce(lambda a, b: a * b, sizes)
    index = lax.broadcasted_iota(jnp.int32, (rows, 1), 0)
    left, inner = index // per, index % per
    place = {}
    for name, size in zip(reversed(order), reversed(sizes)):
        place[name] = left % size
        if name in relative:
            place[name] = place[name] ^ lax.axis_index(name)
        left = left // size
    device = jnp.zeros_like(index)
    for name in ALL:
        device = device * lax.axis_size(name) + place[name]
    return device * per + inner


def add_stage(value, name):
    size = lax.axis_size(name)
    value = value.astype(BF16).reshape(size, -1, value.shape[1])
    received = [swap(value[k], name, k) for k in range(1, size)]
    value = value[0].astype(F32)
    for piece in received:
        value = value + piece.astype(F32)
    return value


def together(*values):
    return lax.optimization_barrier(values)


def cost(flops, moved, exps=0):
    return pl.CostEstimate(flops=int(flops), bytes_accessed=int(moved), transcendentals=int(exps))


def params():
    return pltpu.CompilerParams(vmem_limit_bytes=VMEM_LIMIT)


def front_kernel(
    x_ref, first_ref, gain_ref, cos_ref, sin_ref, weight_ref, normed_ref, qkv_ref, att_ref, total_ref
):
    parts, rows, width = x_ref.shape
    per_block = BLOCK // rows
    blocks = parts // per_block
    gain = gain_ref[...]
    for block in range(blocks):
        lo, hi = block * per_block, (block + 1) * per_block

        @pl.when(pl.program_id(0) == 0)
        def _(lo=lo, hi=hi):
            x = x_ref[lo:hi].reshape(BLOCK, width).astype(F32)
            inv = lax.rsqrt(jnp.mean(x * x, axis=-1, keepdims=True) + EPSILON)
            normed_ref[lo:hi] = (x * inv * gain).astype(BF16).reshape(per_block, rows, width)

        normed = normed_ref[lo:hi].reshape(BLOCK, width)
        cos = cos_ref[block * BLOCK : (block + 1) * BLOCK, :]
        sin = sin_ref[block * BLOCK : (block + 1) * BLOCK, :]
        for kind in range(2):
            value = dot(normed, weight_ref[kind])
            value = (value * cos + partner(value) * sin).astype(BF16)
            qkv_ref[lo:hi, kind, 0] = value.reshape(per_block, rows, PAIR)
        first = first_ref[lo:hi, 0].reshape(BLOCK, PAIR).astype(F32)
        mixed = (0.5 * dot(normed, weight_ref[2]) + 0.5 * first).astype(BF16)
        qkv_ref[lo:hi, 2, 0] = mixed.reshape(per_block, rows, PAIR)
    attend_forward_kernel(qkv_ref, att_ref, total_ref)


def front(x, first, gain, cos, sin, weights):
    parts, rows, width = x.shape
    units = first.shape[1]
    length = parts * rows
    blocks = length // BLOCK
    return pl.pallas_call(
        front_kernel,
        grid=(units,),
        in_specs=[
            pl.BlockSpec((parts, rows, width), lambda u: (0, 0, 0)),
            pl.BlockSpec((parts, 1, rows, PAIR), lambda u: (0, u, 0, 0)),
            pl.BlockSpec((1, width), lambda u: (0, 0)),
            pl.BlockSpec((length, PAIR), lambda u: (0, 0)),
            pl.BlockSpec((length, PAIR), lambda u: (0, 0)),
            pl.BlockSpec((3, width, PAIR), lambda u: (u, 0, 0)),
        ],
        out_specs=[
            pl.BlockSpec((parts, rows, width), lambda u: (0, 0, 0)),
            pl.BlockSpec((parts, 3, 1, rows, PAIR), lambda u: (0, 0, u, 0, 0)),
            pl.BlockSpec((parts, 1, rows, PAIR), lambda u: (0, u, 0, 0)),
            pl.BlockSpec((1, 2, blocks, BLOCK), lambda u: (u, 0, 0, 0)),
        ],
        out_shape=[
            jax.ShapeDtypeStruct((parts, rows, width), BF16),
            jax.ShapeDtypeStruct((parts, 3, units, rows, PAIR), BF16),
            jax.ShapeDtypeStruct((parts, units, rows, PAIR), BF16),
            jax.ShapeDtypeStruct((units, 2, blocks, BLOCK), F32),
        ],
        compiler_params=params(),
        name="front",
        cost_estimate=cost(6 * units * length * PAIR * width + 2 * units * length * length * PAIR, 6 * x.size, 2 * units * length * length),
    )(x, first, gain, cos, sin, weights)


def sections(weight_ref):
    outer, parts, rows, columns = weight_ref.shape
    return [weight_ref[:, part].reshape(outer * rows, columns) for part in range(parts)]


def dot_sections(left, weight_ref):
    parts = sections(weight_ref)
    wide = left.shape[1] // len(parts)
    total = dot(left[:, :wide], parts[0])
    for at in range(1, len(parts)):
        total = total + dot(left[:, at * wide : (at + 1) * wide], parts[at])
    return total


def dot_t_sections(left, weight_ref):
    return jnp.concatenate([dot_t(left, part) for part in sections(weight_ref)], axis=1)


def forward_kernel(
    x_ref, heads_ref, gain_ref, teacher_ref, cotangent_ref, valid_ref, rate_ref, wo_ref, wg_ref, wu_ref, wd_ref,
    att_ref, hidden_ref, normed_ref, gate_ref, up_ref, act_ref, result_ref, grad_ref, grad_low_ref, loss_ref,
):
    step = pl.program_id(0)
    tokens, width = x_ref.shape

    @pl.when(step == 0)
    def _():
        for pair in range(width // PAIR):
            at, unit = divmod(pair, heads_ref.shape[2])
            att_ref[:, pair * PAIR : (pair + 1) * PAIR] = heads_ref[at, :, unit].reshape(tokens, PAIR)
        hidden = x_ref[...].astype(F32) + dot_sections(att_ref[...], wo_ref)
        inv = lax.rsqrt(jnp.mean(hidden * hidden, axis=-1, keepdims=True) + EPSILON)
        hidden_ref[...] = hidden
        result_ref[...] = hidden
        normed_ref[...] = (hidden * inv * gain_ref[...]).astype(BF16)

    gate = dot_sections(normed_ref[...], wg_ref)
    up = dot_sections(normed_ref[...], wu_ref)
    act = (gate * jax.nn.sigmoid(gate) * up).astype(BF16)
    gate_ref[...] = gate
    up_ref[...] = up
    act_ref[...] = act
    result_ref[...] += dot_sections(act, wd_ref)

    @pl.when(step == pl.num_programs(0) - 1)
    def _():
        error = result_ref[...] - teacher_ref[...].astype(F32)
        valid = valid_ref[...]
        grad = cotangent_ref[...].astype(F32) + rate_ref[0:1, 0:1] * valid * error
        grad_ref[...] = grad
        grad_low_ref[...] = grad.astype(BF16)
        losses = jnp.sum(error * error * (valid / width), axis=0, keepdims=True)
        total = losses[:, :PAIR]
        for at in range(PAIR, width, PAIR):
            total = total + losses[:, at : at + PAIR]
        loss_ref[...] = total


def weight_specs(width, parts, gate_out, rest):
    outer, sides, rows, _ = rest.shape
    wide = MLP_STEP
    per = width // wide
    whole = (outer, sides, rows)
    return wide, [
        pl.BlockSpec(whole + (width,), lambda j: (0, 0, 0, parts)),
        pl.BlockSpec(whole + (wide,), lambda j: (0, 0, 0, j)),
        pl.BlockSpec(whole + (wide,), lambda j: (0, 0, 0, 3 * per + j)),
        pl.BlockSpec((outer, sides // per, rows, width), lambda j: (0, j % per, 0, 3 + parts + j // per)),
    ], (gate_out, gate_out, rest, rest)


def still(*shape):
    return pl.BlockSpec(shape, lambda j: (0,) * len(shape))


def mlp_forward(x, heads, gain, teacher, cotangent, valid, rate, gate_out, rest):
    tokens, width = x.shape
    parts = gate_out.shape[3] // width - 1
    wide, specs, weights = weight_specs(width, parts, gate_out, rest)
    moving = pl.BlockSpec((tokens, wide), lambda j: (0, j))
    whole = still(tokens, width)
    hidden = (tokens, parts * width)
    return pl.pallas_call(
        forward_kernel,
        grid=(parts * width // wide,),
        in_specs=[whole, still(*heads.shape), still(1, width), whole, whole, still(tokens, 1), still(1, PAIR)]
        + specs,
        out_specs=[whole, whole, whole, moving, moving, moving, whole, whole, whole, still(1, PAIR)],
        out_shape=[
            jax.ShapeDtypeStruct((tokens, width), BF16),
            jax.ShapeDtypeStruct((tokens, width), F32),
            jax.ShapeDtypeStruct((tokens, width), BF16),
            jax.ShapeDtypeStruct(hidden, F32),
            jax.ShapeDtypeStruct(hidden, F32),
            jax.ShapeDtypeStruct(hidden, BF16),
            jax.ShapeDtypeStruct((tokens, width), F32),
            jax.ShapeDtypeStruct((tokens, width), F32),
            jax.ShapeDtypeStruct((tokens, width), BF16),
            jax.ShapeDtypeStruct((1, PAIR), F32),
        ],
        compiler_params=params(),
        name="mlp_forward",
        cost_estimate=cost(2 * tokens * width * width * (3 * parts + 1), 2 * width * width * (3 * parts + 1) + 10 * tokens * width * parts, tokens * width * parts),
    )(x, heads, gain, teacher, cotangent, valid, rate, *weights)


def backward_kernel(
    grad_ref, grad_low_ref, hidden_ref, gain_ref, gate_ref, up_ref, wo_ref, wg_ref, wu_ref, wd_ref,
    grads_ref, grad_hidden_ref, branch_ref, heads_ref, total,
):
    step = pl.program_id(0)
    wide = gate_ref.shape[1]
    gate = gate_ref[...]
    up = up_ref[...]
    sigmoid = jax.nn.sigmoid(gate)
    grad_act = dot_t_sections(grad_low_ref[...], wd_ref)
    grad_gate = (grad_act * up * (sigmoid * (1.0 + gate * (1.0 - sigmoid)))).astype(BF16)
    grad_up = (grad_act * (gate * sigmoid)).astype(BF16)
    grads_ref[:, :wide] = grad_gate
    grads_ref[:, wide:] = grad_up
    value = dot_t_sections(grad_gate, wg_ref) + dot_t_sections(grad_up, wu_ref)

    @pl.when(step == 0)
    def _():
        total[...] = value

    @pl.when(step > 0)
    def _():
        total[...] += value

    @pl.when(step == pl.num_programs(0) - 1)
    def _():
        hidden = hidden_ref[...]
        inv = lax.rsqrt(jnp.mean(hidden * hidden, axis=-1, keepdims=True) + EPSILON)
        scaled = hidden * inv
        scaled_grad = total[...] * gain_ref[...]
        grad = grad_ref[...] + inv * (
            scaled_grad - scaled * jnp.mean(scaled_grad * scaled, axis=-1, keepdims=True)
        )
        grad_hidden_ref[...] = grad
        branch = grad.astype(BF16)
        branch_ref[...] = branch
        value = dot_t_sections(branch, wo_ref).astype(BF16)
        _, batch, units, rows, _ = heads_ref.shape
        for pair in range(value.shape[1] // PAIR):
            at, unit = divmod(pair, units)
            heads_ref[at, :, unit] = value[:, pair * PAIR : (pair + 1) * PAIR].reshape(batch, rows, PAIR)


def mlp_backward(grad, grad_low, hidden, gain, gate, up, gate_out, rest, heads):
    tokens, width = grad.shape
    parts = gate_out.shape[3] // width - 1
    wide, specs, weights = weight_specs(width, parts, gate_out, rest)
    moving = pl.BlockSpec((tokens, wide), lambda j: (0, j))
    whole = still(tokens, width)
    return pl.pallas_call(
        backward_kernel,
        grid=(parts * width // wide,),
        in_specs=[whole, whole, whole, still(1, width), moving, moving] + specs,
        out_specs=[pl.BlockSpec((tokens, 2 * wide), lambda j: (0, j)), whole, whole, still(*heads)],
        out_shape=[
            jax.ShapeDtypeStruct((tokens, 2 * parts * width), BF16),
            jax.ShapeDtypeStruct((tokens, width), F32),
            jax.ShapeDtypeStruct((tokens, width), BF16),
            jax.ShapeDtypeStruct(heads, BF16),
        ],
        scratch_shapes=[pltpu.VMEM((tokens, width), F32)],
        compiler_params=params(),
        name="mlp_backward",
        cost_estimate=cost(2 * tokens * width * width * (3 * parts + 1), 2 * width * width * (3 * parts + 1) + 12 * tokens * width * parts, tokens * width * parts),
    )(grad, grad_low, hidden, gain, gate, up, *weights)


def picker(place, width):
    lane = lax.broadcasted_iota(jnp.int32, (place.shape[0], width), 1)
    return jnp.where(lane == place, 1.0, 0.0).astype(BF16)


def head_grads_kernel(normed_ref, grads_ref, loss_ref, pick_ref, out_ref, turned):
    parts, kinds, units, rows, _ = grads_ref.shape
    width = normed_ref.shape[2]
    normed = normed_ref[...].reshape(parts * rows, width)
    for unit in range(units):
        for kind in range(kinds):
            value = t_dot(grads_ref[:, kind, unit].reshape(parts * rows, PAIR), normed)
            if kind == 2:
                value = 0.5 * value
            at = (unit * kinds + kind) * PAIR
            turned[at : at + PAIR, :] = value.astype(BF16)
    columns = turned.shape[0]
    out_ref[:, :columns] = dot_t(pick_ref[...], turned[...]).astype(BF16)
    out_ref[:, columns:] = jnp.broadcast_to(loss_ref[...], (width, PAIR)).astype(BF16)


def head_grads(normed, grads, loss_row, pick):
    width = normed.shape[2]
    columns = 3 * grads.shape[2] * PAIR
    return pl.pallas_call(
        head_grads_kernel,
        out_shape=jax.ShapeDtypeStruct((width, columns + PAIR), BF16),
        scratch_shapes=[pltpu.VMEM((columns, width), BF16)],
        compiler_params=params(),
        name="head_grads",
        cost_estimate=cost(2 * normed.size * columns + 2 * width * width * columns, 2 * normed.size + 2 * width * width + 4 * width * columns),
    )(normed, grads, loss_row, pick)


def last_kernel(heads_ref, x_ref, gain_ref, weight_ref, grad_hidden_ref, grad_in_ref, first_ref, grads):
    tokens, width = x_ref.shape
    for kind in range(3):
        for pair in range(width // PAIR):
            at = kind * width + pair * PAIR
            place, unit = divmod(pair, heads_ref.shape[3])
            piece = heads_ref[place, :, kind, unit].reshape(tokens, PAIR)
            if kind == 2:
                half = 0.5 * piece.astype(F32)
                first_ref[:, pair * PAIR : (pair + 1) * PAIR] = half
                piece = half.astype(BF16)
            grads[:, at : at + PAIR] = piece
    grad_norm = dot_t_sections(grads[...], weight_ref)
    x = x_ref[...].astype(F32)
    inv = lax.rsqrt(jnp.mean(x * x, axis=-1, keepdims=True) + EPSILON)
    scaled = x * inv
    scaled_grad = grad_norm * gain_ref[...]
    grad_in_ref[...] = grad_hidden_ref[...] + inv * (
        scaled_grad - scaled * jnp.mean(scaled_grad * scaled, axis=-1, keepdims=True)
    )


def last(heads, x, gain, weights, grad_hidden):
    tokens, width = x.shape
    return pl.pallas_call(
        last_kernel,
        grid=(1,),
        in_specs=[
            still(*heads.shape),
            still(tokens, width),
            still(1, width),
            pl.BlockSpec(weights.shape[:3] + (3 * width,), lambda j: (0, 0, 0, 0)),
            still(tokens, width),
        ],
        out_specs=[still(tokens, width), still(tokens, width)],
        out_shape=[
            jax.ShapeDtypeStruct((tokens, width), F32),
            jax.ShapeDtypeStruct((tokens, width), F32),
        ],
        scratch_shapes=[pltpu.VMEM((tokens, 3 * width), BF16)],
        compiler_params=params(),
        name="last",
        cost_estimate=cost(6 * tokens * width * width, 6 * width * width + 20 * tokens * width),
    )(heads, x, gain, weights, grad_hidden)


def finish_kernel(*refs, own_down):
    pieces, (gate_w_ref, up_w_ref), (gate_ref, up_ref, gain_ref) = refs[:-5], refs[-5:-3], refs[-3:]
    rows, columns = pieces[0].shape
    total = pieces[0][...].astype(F32)
    for piece in pieces[1:]:
        total = total + piece[...].astype(F32)
    parts = -(-own_down // rows)
    width = columns // (2 * parts)
    gain = jnp.zeros((rows, 1), F32)
    for side, (weight_ref, out_ref) in enumerate(((gate_w_ref, gate_ref), (up_w_ref, up_ref))):
        values = []
        for device in range(width // rows):
            for part in range(parts):
                step, lane = divmod(part * width + device * rows, MLP_STEP)
                at = (2 * step + side) * MLP_STEP + lane
                values.append(total[:, at : at + min(rows, own_down - part * rows)])
        value = jnp.concatenate(values, axis=1)
        out_ref[...] = value
        gain = gain + jnp.sum(value * weight_ref[...].astype(F32), axis=1, keepdims=True)
    gain_ref[...] = jnp.broadcast_to(gain, gain_ref.shape)


def finish(pieces, w_gate, w_up, own_down):
    rows, hidden = w_gate.shape
    if rows % 8 == 0:
        gate, up, gain = pl.pallas_call(
            functools.partial(finish_kernel, own_down=own_down),
            out_shape=[
                jax.ShapeDtypeStruct((rows, hidden), F32),
                jax.ShapeDtypeStruct((rows, hidden), F32),
                jax.ShapeDtypeStruct((rows, PAIR), F32),
            ],
            compiler_params=params(),
            name="finish",
        )(*pieces, w_gate, w_up)
        return gate, up, gain[:, 0]
    total = sum(piece.astype(F32) for piece in pieces).reshape(rows, -1, 2, MLP_STEP)
    parts = -(-own_down // rows)

    def unpack(grad):
        grad = grad.reshape(rows, parts, -1, rows).transpose(0, 2, 1, 3)
        return grad.reshape(rows, -1, parts * rows)[:, :, :own_down].reshape(rows, hidden)

    gate, up = unpack(total[:, :, 0]), unpack(total[:, :, 1])
    return gate, up, jnp.sum(gate * w_gate.astype(F32) + up * w_up.astype(F32), axis=1)


STAGES_NATIVE = ("c", "y", "x", "z")
STAGES_OUTPUT = ("c", "z", "y", "x")
STAGES_HEADS = ("c", "x", "y", "z")


def on_device(
    inputs,
    first_values,
    teacher_states,
    out_cotangent,
    token_valid,
    attn_gain,
    w_query,
    w_key,
    w_value,
    w_output,
    mlp_gain,
    w_gate,
    w_up,
    w_down,
):
    batch, local_len, width = inputs.shape
    seqs = lax.axis_size(SEQ)
    tokens = batch * local_len
    length = local_len * seqs
    pairs = width // PAIR
    own_rows = w_query.shape[0]
    own_down = w_down.shape[0]
    zs = lax.axis_size("z")
    units = pairs // zs
    mine = lax.axis_index("y")

    valid_float = token_valid.astype(F32)
    count = jnp.sum(token_valid)
    extra = jnp.stack(
        [
            attn_gain,
            mlp_gain,
            jnp.full((own_rows,), count // 256, jnp.int32).astype(BF16),
            jnp.full((own_rows,), count % 256, jnp.int32).astype(BF16),
        ],
        axis=1,
    )
    extra = jnp.pad(extra, ((0, 0), (0, PAIR - 4)))
    columns = jnp.stack([w_query, w_key, w_value]).reshape(3, own_rows, zs, units, PAIR)
    columns = columns.transpose(2, 3, 0, 1, 4).reshape(zs, 3 * units, own_rows, PAIR)
    columns = jnp.concatenate(
        [columns, jnp.broadcast_to(extra[None, None], (zs, 1, own_rows, PAIR))], axis=1
    )
    blocks = 3 * units + 1
    columns = jnp.broadcast_to(
        columns.reshape(zs, 1, blocks * own_rows, PAIR), (zs, batch, blocks * own_rows, PAIR)
    )
    firsts = first_values.reshape(batch, local_len, zs, units, PAIR).transpose(2, 0, 3, 1, 4)
    firsts = firsts.reshape(zs, batch, units * local_len, PAIR)
    parcel = jnp.concatenate([columns, firsts], axis=2).reshape(seqs, -1, PAIR)

    hidden_parts = -(-own_down // own_rows)
    padded = hidden_parts * own_rows - own_down

    def pack_columns(weight):
        weight = jnp.pad(weight.reshape(own_rows, -1, own_down), ((0, 0), (0, 0), (0, padded)))
        weight = weight.reshape(own_rows, -1, hidden_parts, own_rows)
        return weight.transpose(0, 2, 1, 3).reshape(own_rows, hidden_parts * width)

    down_rows = jnp.pad(w_down, ((0, padded), (0, 0))).reshape(hidden_parts, own_rows, width)
    down_rows = down_rows.transpose(1, 0, 2).reshape(own_rows, hidden_parts * width)
    def along_z(rows):
        pieces = [rows] + [swap(rows, "z", k) for k in range(1, zs)]
        return jnp.stack(arrange(pieces, lax.axis_index("z")), axis=0)

    def across(rows):
        rows = lax.all_gather(rows, ("y", "x", "c"), axis=0)
        if own_rows % 16:
            rows = rows.transpose(1, 0, 2, 3).reshape(1, width // BLOCK, BLOCK, rows.shape[3])
        return rows

    gate_out = along_z(jnp.concatenate([pack_columns(w_gate), w_output], axis=1))
    rest = jnp.concatenate([w_query, w_key, w_value, pack_columns(w_up), down_rows], axis=1)
    gate_out, rest, parcel = together(gate_out, rest, parcel)
    gate_out = across(gate_out)
    rest = along_z(rest)
    parcel = lax.all_to_all(parcel, SEQ, split_axis=0, concat_axis=0, tiled=True)
    rest, x_own, x_sent = together(rest, pick(inputs, mine, 0), pick(inputs, 1 - mine, 0))
    rest = across(rest)
    pieces = arrange([x_own, swap(x_sent, "y", 1)], mine)
    x_all = along_z(jnp.stack(pieces, axis=0)).reshape(seqs, local_len, width)

    first_all = parcel[:, blocks * own_rows :].reshape(seqs, units, local_len, PAIR)
    head_w = parcel[:, : blocks * own_rows].reshape(seqs, blocks, own_rows, PAIR).transpose(1, 0, 2, 3)
    for at, name in ((2, "x"), (3, "c")):
        pieces = [head_w] + [swap(head_w, name, k) for k in range(1, lax.axis_size(name))]
        head_w = jnp.stack(arrange(pieces, lax.axis_index(name)), axis=at)
    head_w = head_w.reshape(blocks, width, PAIR)
    extra_all = head_w[blocks - 1].astype(F32).T
    gain_a = extra_all[0:1, :]
    gain_m = extra_all[1:2, :]
    valid_total = jnp.sum(extra_all[2] * 256.0 + extra_all[3]) / own_rows

    cos_all, sin_all = rotary_tables(jnp.arange(length, dtype=jnp.int32))
    pick_native = picker(stage_rows(width, STAGES_NATIVE, ("c", "z")), width)
    pick_output = picker(stage_rows(width, STAGES_OUTPUT), width)
    pick_heads = picker(stage_rows(width, STAGES_HEADS, ("c", "x", "y")), width)

    normed_all, qkv, attended, totals = front(x_all, first_all, gain_a, cos_all, sin_all, head_w)

    def exchange(array):
        return lax.all_to_all(array, SEQ, split_axis=0, concat_axis=0, tiled=True)

    att_heads = exchange(attended).reshape(zs, batch, units, local_len, PAIR)
    x_low = inputs.reshape(tokens, width)
    rate = jnp.full((1, PAIR), 2.0 / width, F32) / valid_total
    att_low, hidden_in, normed_mlp, gate, up, activated, result, grad_out, grad_down_in, loss_row = mlp_forward(
        x_low,
        att_heads,
        gain_m,
        teacher_states.reshape(tokens, width),
        out_cotangent.reshape(tokens, width),
        valid_float.reshape(tokens, 1),
        rate,
        gate_out,
        rest,
    )

    half = width // 2
    turned = [
        dot_t(pick_native, activated[:, p * width : (p + 1) * width]).astype(BF16).reshape(-1, own_rows, tokens)
        for p in range(hidden_parts)
    ]
    turned_act = jnp.stack(turned, axis=1).reshape(hidden_parts * width, tokens)
    cut = hidden_parts * half
    down_sent = swap(dot(turned_act[cut:], grad_down_in).astype(BF16), "c", 1)
    down_sum = (dot(turned_act[:cut], grad_down_in) + down_sent.astype(F32)).astype(BF16)
    down_sum, grad_down_in = together(down_sum, grad_down_in)

    def over_yx(value):
        value = value.reshape(2 * lax.axis_size("x"), -1, value.shape[1])
        value = lax.psum_scatter(value, ("y", "x"), scatter_dimension=0, tiled=True)
        return lax.optimization_barrier(value)[0]

    down_sum = over_yx(down_sum)
    grads, grad_hidden, grad_branch, grad_heads = mlp_backward(
        grad_out, grad_down_in, hidden_in, gain_m, gate, up, gate_out, rest, att_heads.shape
    )
    grad_heads = exchange(grad_heads.reshape(seqs, units, local_len, PAIR))
    turned_mlp = dot_t(pick_native, normed_mlp).astype(BF16)
    mlp_sent = swap(dot(turned_mlp[half:], grads).astype(BF16), "c", 1)
    mlp_sum = (dot(turned_mlp[:half], grads) + mlp_sent.astype(F32)).astype(BF16)

    turned_att = dot_t(pick_output, att_low).astype(BF16)
    out_sent = swap(dot(turned_att[half:], grad_branch).astype(BF16), "c", 1)
    out_sum = (dot(turned_att[:half], grad_branch) + out_sent.astype(F32)).astype(BF16)

    grad_heads, mlp_sum, out_sum, down_sum = together(grad_heads, mlp_sum, out_sum, down_sum)
    mlp_sum = over_yx(mlp_sum)
    out_sum = add_stage(out_sum, "z").astype(BF16)

    grad_qkv = attend_backward(qkv, grad_heads, totals, cos_all, sin_all)
    grad_own = exchange(grad_qkv).reshape(zs, batch, 3, units, local_len, PAIR)

    value = head_grads(normed_all, grad_qkv, loss_row, pick_heads)
    for name in ("c", "x", "y"):
        value = add_stage(value, name)
    value, grad_own, down_sum, out_sum = together(value.astype(BF16), grad_own, down_sum, out_sum)
    owned_down = add_stage(down_sum, "z")[:own_down]
    owned_output = add_stage(add_stage(out_sum, "y"), "x")
    mlp_sum = mlp_sum.reshape(zs, own_rows, -1)
    mlp_sum = [mlp_sum[0]] + [swap(mlp_sum[k], "z", k) for k in range(1, zs)]
    value = value.reshape(zs, own_rows, value.shape[1])
    value = lax.all_to_all(value, "z", split_axis=0, concat_axis=0, tiled=True)
    columns = 3 * units * PAIR
    loss_value = jnp.sum(value[:, 0, columns:].astype(F32)) / valid_total
    value = value[:, :, :columns].reshape(zs, own_rows, units, 3, PAIR).astype(F32)
    owned_qkv = value.transpose(3, 1, 0, 2, 4).reshape(3, own_rows, width)

    grad_in, grad_first = last(grad_own, x_low, gain_a, rest, grad_hidden)

    gain_grad_a = (
        jnp.sum(w_query.astype(F32) * owned_qkv[0], axis=1)
        + jnp.sum(w_key.astype(F32) * owned_qkv[1], axis=1)
        + jnp.sum(w_value.astype(F32) * owned_qkv[2], axis=1)
    ) / attn_gain.astype(F32)
    owned_gate, owned_up, gain_grad_m = finish(mlp_sum, w_gate, w_up, own_down)
    gain_grad_m = gain_grad_m / mlp_gain.astype(F32)
    return (
        result.reshape(batch, local_len, width),
        loss_value,
        grad_in.reshape(batch, local_len, width),
        grad_first.reshape(batch, local_len, width),
        gain_grad_a,
        owned_qkv[0],
        owned_qkv[1],
        owned_qkv[2],
        owned_output,
        gain_grad_m,
        owned_gate,
        owned_up,
        owned_down,
    )


def solution(mesh):
    seqs, dps = mesh.devices.shape
    fine = Mesh(mesh.devices.reshape(seqs // 2, 2, dps // 2, 2), ALL)
    tokens = P(("x", "c"), SEQ, None)
    rows = P(ALL, None)
    gain = P(ALL)
    return jax.shard_map(
        on_device,
        mesh=fine,
        in_specs=(
            tokens, tokens, tokens, tokens, P(("x", "c"), SEQ), gain, rows, rows, rows, rows, gain, rows, rows, rows,
        ),
        out_specs=(
            tokens, P(), tokens, tokens, gain, rows, rows, rows, rows, gain, rows, rows, rows,
        ),
        check_vma=False,
    )
```

```python
import functools

import jax
import jax.numpy as jnp
from jax import lax
from jax.experimental import pallas as pl
from jax.experimental.pallas import tpu as pltpu
from jax.sharding import Mesh
from jax.sharding import PartitionSpec as P

HEAD_DIM = 64
BLOCK = 256
MLP_STEP = 512
PAIR = 2 * HEAD_DIM

EPSILON = 1e-06
THETA = 10000.0
SCALE = 0.125
ALL = ("z", "y", "x", "c")
SEQ = ("z", "y")
F32 = jnp.float32
BF16 = jnp.bfloat16


def rotary_tables(positions):
    lane = jnp.arange(PAIR, dtype=jnp.int32)
    half = HEAD_DIM // 2
    index = (lane % half).astype(F32)
    frequency = THETA ** (-(index * 2.0 / HEAD_DIM))
    angles = positions.astype(F32)[:, None] * frequency[None, :]
    sign = jnp.where(lane % HEAD_DIM < half, -1.0, 1.0)[None, :]
    return jnp.cos(angles), jnp.sin(angles) * sign


def partner(values):
    half = HEAD_DIM // 2
    lane = lax.broadcasted_iota(jnp.int32, values.shape, values.ndim - 1)
    first = lane % HEAD_DIM < half
    width = values.shape[-1]
    return jnp.where(
        first,
        pltpu.roll(values, width - half, values.ndim - 1),
        pltpu.roll(values, half, values.ndim - 1),
    )


def dot_t(left, right):
    return lax.dot_general(left, right, (((1,), (1,)), ((), ())), preferred_element_type=F32)


def t_dot(left, right):
    return lax.dot_general(left, right, (((0,), (0,)), ((), ())), preferred_element_type=F32)


def dot(left, right):
    return jnp.dot(left, right, preferred_element_type=F32)


def attend_forward_kernel(qkv_ref, out_ref, total_ref):
    parts, _, _, rows, _ = qkv_ref.shape
    per_block = BLOCK // rows
    blocks = parts // per_block
    for head in range(2):
        lanes = pl.ds(head * HEAD_DIM, HEAD_DIM)
        for block in range(blocks):
            lo, hi = block * per_block, (block + 1) * per_block
            query = qkv_ref[lo:hi, 0, 0, :, lanes].reshape(BLOCK, HEAD_DIM)
            keys = qkv_ref[0:hi, 1, 0, :, lanes].reshape(hi * rows, HEAD_DIM)
            values = qkv_ref[0:hi, 2, 0, :, lanes].reshape(hi * rows, HEAD_DIM)
            scores = dot_t(keys, query * SCALE)
            top = jnp.max(scores, axis=0, keepdims=True)
            weights = jnp.exp(scores - top)
            total = jnp.sum(weights, axis=0, keepdims=True)
            probs = (weights * (1.0 / total)).astype(BF16)
            mixed = t_dot(values, probs)
            out_ref[lo:hi, 0, :, lanes] = mixed.T.astype(BF16).reshape(per_block, rows, HEAD_DIM)
            total_ref[0, head, block : block + 1, :] = top + jnp.log(total)


def attend_backward_kernel(qkv_ref, grad_ref, total_ref, cos_ref, sin_ref, out_ref, dk_acc, dv_acc):
    parts, _, _, rows, _ = qkv_ref.shape
    per_block = BLOCK // rows
    blocks = parts // per_block
    dk_acc[...] = jnp.zeros_like(dk_acc)
    dv_acc[...] = jnp.zeros_like(dv_acc)
    for block in range(blocks):
        lo, hi = block * per_block, (block + 1) * per_block
        keys_n = hi * rows
        dq_parts = []
        for head in range(2):
            lanes = pl.ds(head * HEAD_DIM, HEAD_DIM)
            query = qkv_ref[lo:hi, 0, 0, :, lanes].reshape(BLOCK, HEAD_DIM)
            grad = grad_ref[lo:hi, 0, :, lanes].reshape(BLOCK, HEAD_DIM)
            keys = qkv_ref[0:hi, 1, 0, :, lanes].reshape(keys_n, HEAD_DIM)
            values = qkv_ref[0:hi, 2, 0, :, lanes].reshape(keys_n, HEAD_DIM)
            scores = dot_t(keys, query * SCALE)
            probs = jnp.exp(scores - total_ref[0, head, block : block + 1, :])
            grad_probs = dot_t(values, grad)
            inner = jnp.sum(probs * grad_probs, axis=0, keepdims=True)
            grad_scores = (probs * (grad_probs - inner)).astype(BF16)
            dk_acc[0:keys_n, lanes] += dot(grad_scores, query) * SCALE
            dv_acc[0:keys_n, lanes] += dot(probs.astype(BF16), grad)
            dq_parts.append(t_dot(keys, grad_scores).T * SCALE)
        dq = jnp.concatenate(dq_parts, axis=1)
        cos = cos_ref[block * BLOCK : (block + 1) * BLOCK, :]
        sin = sin_ref[block * BLOCK : (block + 1) * BLOCK, :]
        dq = (dq * cos - partner(dq) * sin).astype(BF16)
        out_ref[lo:hi, 0, 0, :, :] = dq.reshape(per_block, rows, PAIR)
    dk = dk_acc[...]
    dk = (dk * cos_ref[...] - partner(dk) * sin_ref[...]).astype(BF16)
    out_ref[:, 1, 0, :, :] = dk.reshape(parts, rows, PAIR)
    out_ref[:, 2, 0, :, :] = dv_acc[...].astype(BF16).reshape(parts, rows, PAIR)


VMEM_LIMIT = 60 * 1024 * 1024


def attend_backward(qkv, grad_att, totals, cos, sin):
    parts, _, units, rows, _ = qkv.shape
    length = parts * rows
    blocks = length // BLOCK
    return pl.pallas_call(
        attend_backward_kernel,
        grid=(units,),
        in_specs=[
            pl.BlockSpec((parts, 3, 1, rows, PAIR), lambda u: (0, 0, u, 0, 0)),
            pl.BlockSpec((parts, 1, rows, PAIR), lambda u: (0, u, 0, 0)),
            pl.BlockSpec((1, 2, blocks, BLOCK), lambda u: (u, 0, 0, 0)),
            pl.BlockSpec((length, PAIR), lambda u: (0, 0)),
            pl.BlockSpec((length, PAIR), lambda u: (0, 0)),
        ],
        out_specs=pl.BlockSpec((parts, 3, 1, rows, PAIR), lambda u: (0, 0, u, 0, 0)),
        out_shape=jax.ShapeDtypeStruct((parts, 3, units, rows, PAIR), BF16),
        scratch_shapes=[pltpu.VMEM((length, PAIR), F32), pltpu.VMEM((length, PAIR), F32)],
        compiler_params=pltpu.CompilerParams(vmem_limit_bytes=VMEM_LIMIT),
        name="attend_backward",
        cost_estimate=cost(units * length * length, 22),
    )(qkv, grad_att, totals, cos, sin)


def swap(array, name, distance):
    size = lax.axis_size(name)
    return lax.ppermute(array, name, [(i, i ^ distance) for i in range(size)])


def pick(array, index, axis):
    return lax.dynamic_index_in_dim(array, index, axis, keepdims=False)


def arrange(pieces, at):
    bit = 1
    while bit < len(pieces):
        odd = (at & bit) != 0
        pieces = [jnp.where(odd, pieces[j ^ bit], pieces[j]) for j in range(len(pieces))]
        bit *= 2
    return pieces


def stage_rows(rows, order, relative=ALL):
    sizes = [lax.axis_size(name) for name in order]
    per = rows // functools.reduce(lambda a, b: a * b, sizes)
    index = lax.broadcasted_iota(jnp.int32, (rows, 1), 0)
    left, inner = index // per, index % per
    place = {}
    for name, size in zip(reversed(order), reversed(sizes)):
        place[name] = left % size
        if name in relative:
            place[name] = place[name] ^ lax.axis_index(name)
        left = left // size
    device = jnp.zeros_like(index)
    for name in ALL:
        device = device * lax.axis_size(name) + place[name]
    return device * per + inner


def add_stage(value, name):
    size = lax.axis_size(name)
    value = value.astype(BF16).reshape(size, -1, value.shape[1])
    received = [swap(value[k], name, k) for k in range(1, size)]
    value = value[0].astype(F32)
    for piece in received:
        value = value + piece.astype(F32)
    return value


def together(*values):
    return lax.optimization_barrier(values)


def cost(size, factor):
    return pl.CostEstimate(flops=0, bytes_accessed=int(size * factor), transcendentals=0)


def params():
    return pltpu.CompilerParams(vmem_limit_bytes=VMEM_LIMIT)


def front_kernel(
    x_ref, first_ref, gain_ref, cos_ref, sin_ref, weight_ref, normed_ref, qkv_ref, att_ref, total_ref
):
    parts, rows, width = x_ref.shape
    per_block = BLOCK // rows
    blocks = parts // per_block
    gain = gain_ref[...]
    for block in range(blocks):
        lo, hi = block * per_block, (block + 1) * per_block

        @pl.when(pl.program_id(0) == 0)
        def _(lo=lo, hi=hi):
            x = x_ref[lo:hi].reshape(BLOCK, width).astype(F32)
            inv = lax.rsqrt(jnp.mean(x * x, axis=-1, keepdims=True) + EPSILON)
            normed_ref[lo:hi] = (x * inv * gain).astype(BF16).reshape(per_block, rows, width)

        normed = normed_ref[lo:hi].reshape(BLOCK, width)
        cos = cos_ref[block * BLOCK : (block + 1) * BLOCK, :]
        sin = sin_ref[block * BLOCK : (block + 1) * BLOCK, :]
        for kind in range(2):
            value = dot(normed, weight_ref[kind])
            value = (value * cos + partner(value) * sin).astype(BF16)
            qkv_ref[lo:hi, kind, 0] = value.reshape(per_block, rows, PAIR)
        first = first_ref[lo:hi, 0].reshape(BLOCK, PAIR).astype(F32)
        mixed = (0.5 * dot(normed, weight_ref[2]) + 0.5 * first).astype(BF16)
        qkv_ref[lo:hi, 2, 0] = mixed.reshape(per_block, rows, PAIR)
    attend_forward_kernel(qkv_ref, att_ref, total_ref)


def front(x, first, gain, cos, sin, weights):
    parts, rows, width = x.shape
    units = first.shape[1]
    length = parts * rows
    blocks = length // BLOCK
    return pl.pallas_call(
        front_kernel,
        grid=(units,),
        in_specs=[
            pl.BlockSpec((parts, rows, width), lambda u: (0, 0, 0)),
            pl.BlockSpec((parts, 1, rows, PAIR), lambda u: (0, u, 0, 0)),
            pl.BlockSpec((1, width), lambda u: (0, 0)),
            pl.BlockSpec((length, PAIR), lambda u: (0, 0)),
            pl.BlockSpec((length, PAIR), lambda u: (0, 0)),
            pl.BlockSpec((3, width, PAIR), lambda u: (u, 0, 0)),
        ],
        out_specs=[
            pl.BlockSpec((parts, rows, width), lambda u: (0, 0, 0)),
            pl.BlockSpec((parts, 3, 1, rows, PAIR), lambda u: (0, 0, u, 0, 0)),
            pl.BlockSpec((parts, 1, rows, PAIR), lambda u: (0, u, 0, 0)),
            pl.BlockSpec((1, 2, blocks, BLOCK), lambda u: (u, 0, 0, 0)),
        ],
        out_shape=[
            jax.ShapeDtypeStruct((parts, rows, width), BF16),
            jax.ShapeDtypeStruct((parts, 3, units, rows, PAIR), BF16),
            jax.ShapeDtypeStruct((parts, units, rows, PAIR), BF16),
            jax.ShapeDtypeStruct((units, 2, blocks, BLOCK), F32),
        ],
        compiler_params=params(),
        name="front",
        cost_estimate=cost(units * length * length, 27),
    )(x, first, gain, cos, sin, weights)


def sections(weight_ref):
    outer, parts, rows, columns = weight_ref.shape
    return [weight_ref[:, part].reshape(outer * rows, columns) for part in range(parts)]


def dot_sections(left, weight_ref):
    parts = sections(weight_ref)
    wide = left.shape[1] // len(parts)
    total = dot(left[:, :wide], parts[0])
    for at in range(1, len(parts)):
        total = total + dot(left[:, at * wide : (at + 1) * wide], parts[at])
    return total


def dot_t_sections(left, weight_ref):
    return jnp.concatenate([dot_t(left, part) for part in sections(weight_ref)], axis=1)


def mlp_kernel(
    x_ref, heads_ref, gain_ref, teacher_ref, cotangent_ref, valid_ref, rate_ref, gate_out, up_down,
    att_ref, normed_ref, act_ref, result_ref, grad_low_ref, loss_ref, grads_ref, grad_hidden_ref, branch_ref, out_heads_ref,
    wo, wg, wu, wd, gates, ups, hidden_ref, total, arrived,
):
    tokens, width = x_ref.shape
    steps, _, sides, _, wide = wg.shape
    parts = steps * wide // width
    per = width // wide
    deep = sides // per

    def output_copy():
        return pltpu.make_async_copy(
            gate_out.at[:, :, :, pl.ds(parts * width, width)], wo, arrived.at[3 * steps]
        )

    def copies(step):
        lanes = pl.ds(pl.multiple_of(step * wide, wide), wide)
        rows = pl.ds(step % per * deep, deep)
        across = pl.ds(pl.multiple_of((parts + step // per) * width, width), width)
        return (
            pltpu.make_async_copy(gate_out.at[:, :, :, lanes], wg.at[step], arrived.at[3 * step]),
            pltpu.make_async_copy(up_down.at[:, :, :, lanes], wu.at[step], arrived.at[3 * step + 1]),
            pltpu.make_async_copy(up_down.at[:, rows, :, across], wd.at[step], arrived.at[3 * step + 2]),
        )

    output_copy().start()
    for step in range(steps):
        for copy in copies(step):
            copy.start()

    for pair in range(width // PAIR):
        at, unit = divmod(pair, heads_ref.shape[2])
        att_ref[:, pair * PAIR : (pair + 1) * PAIR] = heads_ref[at, :, unit].reshape(tokens, PAIR)
    output_copy().wait()
    hidden = x_ref[...].astype(F32) + dot_sections(att_ref[...], wo)
    inv = lax.rsqrt(jnp.mean(hidden * hidden, axis=-1, keepdims=True) + EPSILON)
    hidden_ref[...] = hidden
    result_ref[...] = hidden
    normed_ref[...] = (hidden * inv * gain_ref[...]).astype(BF16)

    def forward(step, carry):
        for copy in copies(step):
            copy.wait()
        gate = dot_sections(normed_ref[...], wg.at[step])
        up = dot_sections(normed_ref[...], wu.at[step])
        act = (gate * jax.nn.sigmoid(gate) * up).astype(BF16)
        gates[step] = gate
        ups[step] = up
        act_ref[:, pl.ds(pl.multiple_of(step * wide, wide), wide)] = act
        result_ref[...] += dot_sections(act, wd.at[step])
        return carry

    lax.fori_loop(0, steps, forward, 0)
    error = result_ref[...] - teacher_ref[...].astype(F32)
    valid = valid_ref[...]
    grad = cotangent_ref[...].astype(F32) + rate_ref[0:1, 0:1] * valid * error
    grad_hidden_ref[...] = grad
    grad_low_ref[...] = grad.astype(BF16)
    losses = jnp.sum(error * error * (valid / width), axis=0, keepdims=True)
    loss = losses[:, :PAIR]
    for at in range(PAIR, width, PAIR):
        loss = loss + losses[:, at : at + PAIR]
    loss_ref[...] = loss
    total[...] = jnp.zeros_like(total)

    def backward(step, carry):
        gate = gates[step]
        up = ups[step]
        sigmoid = jax.nn.sigmoid(gate)
        grad_act = dot_t_sections(grad_low_ref[...], wd.at[step])
        grad_gate = (grad_act * up * (sigmoid * (1.0 + gate * (1.0 - sigmoid)))).astype(BF16)
        grad_up = (grad_act * (gate * sigmoid)).astype(BF16)
        at = pl.multiple_of(2 * step * wide, 2 * wide)
        grads_ref[:, pl.ds(at, wide)] = grad_gate
        grads_ref[:, pl.ds(pl.multiple_of(at + wide, wide), wide)] = grad_up
        total[...] += dot_t_sections(grad_gate, wg.at[step]) + dot_t_sections(grad_up, wu.at[step])
        return carry

    lax.fori_loop(0, steps, backward, 0)
    hidden = hidden_ref[...]
    inv = lax.rsqrt(jnp.mean(hidden * hidden, axis=-1, keepdims=True) + EPSILON)
    scaled = hidden * inv
    scaled_grad = total[...] * gain_ref[...]
    grad = grad_hidden_ref[...] + inv * (
        scaled_grad - scaled * jnp.mean(scaled_grad * scaled, axis=-1, keepdims=True)
    )
    grad_hidden_ref[...] = grad
    branch = grad.astype(BF16)
    branch_ref[...] = branch
    value = dot_t_sections(branch, wo).astype(BF16)
    _, batch, units, rows, _ = out_heads_ref.shape
    for pair in range(width // PAIR):
        at, unit = divmod(pair, units)
        out_heads_ref[at, :, unit] = value[:, pair * PAIR : (pair + 1) * PAIR].reshape(batch, rows, PAIR)


def still(*shape):
    return pl.BlockSpec(shape, lambda j: (0,) * len(shape))


def mlp(x, heads, gain, teacher, cotangent, valid, rate, gate_out, up_down):
    tokens, width = x.shape
    outer, sides, rows, _ = gate_out.shape
    parts = gate_out.shape[3] // width - 1
    wide = MLP_STEP
    steps = parts * width // wide
    deep = sides * wide // width
    whole = still(tokens, width)
    outside = pl.BlockSpec(memory_space=pl.ANY)
    low = jax.ShapeDtypeStruct((tokens, width), BF16)
    full = jax.ShapeDtypeStruct((tokens, width), F32)
    hidden = (tokens, parts * width)
    grads = (tokens, 2 * parts * width)
    return pl.pallas_call(
        mlp_kernel,
        grid=(1,),
        in_specs=[whole, still(*heads.shape), still(1, width), whole, whole, still(tokens, 1), still(1, PAIR)]
        + [outside, outside],
        out_specs=[
            whole, whole, still(*hidden), whole, whole, still(1, PAIR), still(*grads), whole, whole, still(*heads.shape),
        ],
        out_shape=[
            low,
            low,
            jax.ShapeDtypeStruct(hidden, BF16),
            full,
            low,
            jax.ShapeDtypeStruct((1, PAIR), F32),
            jax.ShapeDtypeStruct(grads, BF16),
            full,
            low,
            jax.ShapeDtypeStruct(heads.shape, BF16),
        ],
        scratch_shapes=[
            pltpu.VMEM((outer, sides, rows, width), BF16),
            pltpu.VMEM((steps, outer, sides, rows, wide), BF16),
            pltpu.VMEM((steps, outer, sides, rows, wide), BF16),
            pltpu.VMEM((steps, outer, deep, rows, width), BF16),
            pltpu.VMEM((steps, tokens, wide), F32),
            pltpu.VMEM((steps, tokens, wide), F32),
            pltpu.VMEM((tokens, width), F32),
            pltpu.VMEM((tokens, width), F32),
            pltpu.SemaphoreType.DMA((3 * steps + 1,)),
        ],
        compiler_params=params(),
        name="mlp",
        cost_estimate=cost(tokens * width * parts, 80),
    )(x, heads, gain, teacher, cotangent, valid, rate, gate_out, up_down)


def picker(place, width):
    lane = lax.broadcasted_iota(jnp.int32, (place.shape[0], width), 1)
    return jnp.where(lane == place, 1.0, 0.0).astype(BF16)


def head_grads_kernel(normed_ref, grads_ref, loss_ref, pick_ref, out_ref, turned):
    parts, kinds, units, rows, _ = grads_ref.shape
    width = normed_ref.shape[2]
    normed = normed_ref[...].reshape(parts * rows, width)
    for unit in range(units):
        for kind in range(kinds):
            value = t_dot(grads_ref[:, kind, unit].reshape(parts * rows, PAIR), normed)
            if kind == 2:
                value = 0.5 * value
            at = (unit * kinds + kind) * PAIR
            turned[at : at + PAIR, :] = value.astype(BF16)
    columns = turned.shape[0]
    out_ref[:, :columns] = dot_t(pick_ref[...], turned[...]).astype(BF16)
    out_ref[:, columns:] = jnp.broadcast_to(loss_ref[...], (width, PAIR)).astype(BF16)


def head_grads(normed, grads, loss_row, pick):
    width = normed.shape[2]
    columns = 3 * grads.shape[2] * PAIR
    return pl.pallas_call(
        head_grads_kernel,
        out_shape=jax.ShapeDtypeStruct((width, columns + PAIR), BF16),
        scratch_shapes=[pltpu.VMEM((columns, width), BF16)],
        compiler_params=params(),
        name="head_grads",
        cost_estimate=cost(normed.size, 24),
    )(normed, grads, loss_row, pick)


def last_kernel(heads_ref, x_ref, gain_ref, weight_ref, grad_hidden_ref, grad_in_ref, first_ref, grads):
    tokens, width = x_ref.shape
    for kind in range(3):
        for pair in range(width // PAIR):
            at = kind * width + pair * PAIR
            place, unit = divmod(pair, heads_ref.shape[3])
            piece = heads_ref[place, :, kind, unit].reshape(tokens, PAIR)
            if kind == 2:
                half = 0.5 * piece.astype(F32)
                first_ref[:, pair * PAIR : (pair + 1) * PAIR] = half
                piece = half.astype(BF16)
            grads[:, at : at + PAIR] = piece
    grad_norm = dot_t_sections(grads[...], weight_ref)
    x = x_ref[...].astype(F32)
    inv = lax.rsqrt(jnp.mean(x * x, axis=-1, keepdims=True) + EPSILON)
    scaled = x * inv
    scaled_grad = grad_norm * gain_ref[...]
    grad_in_ref[...] = grad_hidden_ref[...] + inv * (
        scaled_grad - scaled * jnp.mean(scaled_grad * scaled, axis=-1, keepdims=True)
    )


def last(heads, x, gain, weights, grad_hidden):
    tokens, width = x.shape
    return pl.pallas_call(
        last_kernel,
        grid=(1,),
        in_specs=[
            still(*heads.shape),
            still(tokens, width),
            still(1, width),
            pl.BlockSpec(weights.shape[:3] + (3 * width,), lambda j: (0, 0, 0, 0)),
            still(tokens, width),
        ],
        out_specs=[still(tokens, width), still(tokens, width)],
        out_shape=[
            jax.ShapeDtypeStruct((tokens, width), F32),
            jax.ShapeDtypeStruct((tokens, width), F32),
        ],
        scratch_shapes=[pltpu.VMEM((tokens, 3 * width), BF16)],
        compiler_params=params(),
        name="last",
        cost_estimate=cost(tokens * width, 84),
    )(heads, x, gain, weights, grad_hidden)


def finish_kernel(*refs, own_down):
    pieces, (gate_w_ref, up_w_ref), (gate_ref, up_ref, gain_ref) = refs[:-5], refs[-5:-3], refs[-3:]
    rows, columns = pieces[0].shape
    total = pieces[0][...].astype(F32)
    for piece in pieces[1:]:
        total = total + piece[...].astype(F32)
    parts = -(-own_down // rows)
    width = columns // (2 * parts)
    gain = jnp.zeros((rows, 1), F32)
    for side, (weight_ref, out_ref) in enumerate(((gate_w_ref, gate_ref), (up_w_ref, up_ref))):
        values = []
        for device in range(width // rows):
            for part in range(parts):
                step, lane = divmod(part * width + device * rows, MLP_STEP)
                at = (2 * step + side) * MLP_STEP + lane
                values.append(total[:, at : at + min(rows, own_down - part * rows)])
        value = jnp.concatenate(values, axis=1)
        out_ref[...] = value
        gain = gain + jnp.sum(value * weight_ref[...].astype(F32), axis=1, keepdims=True)
    gain_ref[...] = jnp.broadcast_to(gain, gain_ref.shape)


def finish(pieces, w_gate, w_up, own_down):
    rows, hidden = w_gate.shape
    if rows % 8 == 0:
        gate, up, gain = pl.pallas_call(
            functools.partial(finish_kernel, own_down=own_down),
            out_shape=[
                jax.ShapeDtypeStruct((rows, hidden), F32),
                jax.ShapeDtypeStruct((rows, hidden), F32),
                jax.ShapeDtypeStruct((rows, PAIR), F32),
            ],
            compiler_params=params(),
            name="finish",
        )(*pieces, w_gate, w_up)
        return gate, up, gain[:, 0]
    total = sum(piece.astype(F32) for piece in pieces).reshape(rows, -1, 2, MLP_STEP)
    parts = -(-own_down // rows)

    def unpack(grad):
        grad = grad.reshape(rows, parts, -1, rows).transpose(0, 2, 1, 3)
        return grad.reshape(rows, -1, parts * rows)[:, :, :own_down].reshape(rows, hidden)

    gate, up = unpack(total[:, :, 0]), unpack(total[:, :, 1])
    return gate, up, jnp.sum(gate * w_gate.astype(F32) + up * w_up.astype(F32), axis=1)


STAGES_NATIVE = ("c", "y", "x", "z")
STAGES_OUTPUT = ("c", "z", "y", "x")
STAGES_HEADS = ("c", "x", "y", "z")


def on_device(
    inputs,
    first_values,
    teacher_states,
    out_cotangent,
    token_valid,
    attn_gain,
    w_query,
    w_key,
    w_value,
    w_output,
    mlp_gain,
    w_gate,
    w_up,
    w_down,
):
    batch, local_len, width = inputs.shape
    seqs = lax.axis_size(SEQ)
    tokens = batch * local_len
    length = local_len * seqs
    pairs = width // PAIR
    own_rows = w_query.shape[0]
    own_down = w_down.shape[0]
    zs = lax.axis_size("z")
    units = pairs // zs
    mine = lax.axis_index("y")

    valid_float = token_valid.astype(F32)
    count = jnp.sum(token_valid)
    extra = jnp.stack(
        [
            attn_gain,
            mlp_gain,
            jnp.full((own_rows,), count // 256, jnp.int32).astype(BF16),
            jnp.full((own_rows,), count % 256, jnp.int32).astype(BF16),
        ],
        axis=1,
    )
    extra = jnp.pad(extra, ((0, 0), (0, PAIR - 4)))
    columns = jnp.stack([w_query, w_key, w_value]).reshape(3, own_rows, zs, units, PAIR)
    columns = columns.transpose(2, 3, 0, 1, 4).reshape(zs, 3 * units, own_rows, PAIR)
    columns = jnp.concatenate(
        [columns, jnp.broadcast_to(extra[None, None], (zs, 1, own_rows, PAIR))], axis=1
    )
    blocks = 3 * units + 1
    columns = jnp.broadcast_to(
        columns.reshape(zs, 1, blocks * own_rows, PAIR), (zs, batch, blocks * own_rows, PAIR)
    )
    firsts = first_values.reshape(batch, local_len, zs, units, PAIR).transpose(2, 0, 3, 1, 4)
    firsts = firsts.reshape(zs, batch, units * local_len, PAIR)
    parcel = jnp.concatenate([columns, firsts], axis=2).reshape(seqs, -1, PAIR)

    hidden_parts = -(-own_down // own_rows)
    padded = hidden_parts * own_rows - own_down

    def pack_columns(weight):
        weight = jnp.pad(weight.reshape(own_rows, -1, own_down), ((0, 0), (0, 0), (0, padded)))
        weight = weight.reshape(own_rows, -1, hidden_parts, own_rows)
        return weight.transpose(0, 2, 1, 3).reshape(own_rows, hidden_parts * width)

    down_rows = jnp.pad(w_down, ((0, padded), (0, 0))).reshape(hidden_parts, own_rows, width)
    down_rows = down_rows.transpose(1, 0, 2).reshape(own_rows, hidden_parts * width)
    def along_z(rows):
        pieces = [rows] + [swap(rows, "z", k) for k in range(1, zs)]
        return jnp.stack(arrange(pieces, lax.axis_index("z")), axis=0)

    def across(rows):
        rows = lax.all_gather(rows, ("y", "x", "c"), axis=0)
        if own_rows % 16:
            rows = rows.transpose(1, 0, 2, 3).reshape(1, width // BLOCK, BLOCK, rows.shape[3])
        return rows

    x_own, x_sent = pick(inputs, mine, 0), pick(inputs, 1 - mine, 0)
    x_sent = swap(x_sent, "y", 1)
    gate_out = along_z(jnp.concatenate([pack_columns(w_gate), w_output], axis=1))
    rest = jnp.concatenate([pack_columns(w_up), down_rows], axis=1)
    gate_out, rest, parcel, x_sent = together(gate_out, rest, parcel, x_sent)
    gate_out = across(gate_out)
    rest = along_z(rest)
    rest, x_own, x_sent, parcel = together(rest, x_own, x_sent, parcel)
    rest = across(rest)
    parcel = lax.all_to_all(parcel, SEQ, split_axis=0, concat_axis=0, tiled=True)
    x_all = along_z(jnp.stack(arrange([x_own, x_sent], mine), axis=0)).reshape(seqs, local_len, width)
    x_all, attn_rows = together(x_all, jnp.concatenate([w_query, w_key, w_value], axis=1))
    attn_w = along_z(attn_rows)

    first_all = parcel[:, blocks * own_rows :].reshape(seqs, units, local_len, PAIR)
    head_w = parcel[:, : blocks * own_rows].reshape(seqs, blocks, own_rows, PAIR).transpose(1, 0, 2, 3)
    for at, name in ((2, "x"), (3, "c")):
        pieces = [head_w] + [swap(head_w, name, k) for k in range(1, lax.axis_size(name))]
        head_w = jnp.stack(arrange(pieces, lax.axis_index(name)), axis=at)
    head_w = head_w.reshape(blocks, width, PAIR)
    extra_all = head_w[blocks - 1].astype(F32).T
    gain_a = extra_all[0:1, :]
    gain_m = extra_all[1:2, :]
    valid_total = jnp.sum(extra_all[2] * 256.0 + extra_all[3]) / own_rows

    cos_all, sin_all = rotary_tables(jnp.arange(length, dtype=jnp.int32))
    pick_native = picker(stage_rows(width, STAGES_NATIVE, ("c", "z")), width)
    pick_down = picker(stage_rows(width, STAGES_NATIVE), width)
    pick_output = picker(stage_rows(width, STAGES_OUTPUT), width)
    pick_heads = picker(stage_rows(width, STAGES_HEADS, ("c", "x", "y")), width)

    normed_all, qkv, attended, totals = front(x_all, first_all, gain_a, cos_all, sin_all, head_w)

    def exchange(array):
        return lax.all_to_all(array, SEQ, split_axis=0, concat_axis=0, tiled=True)

    att_heads = exchange(attended).reshape(zs, batch, units, local_len, PAIR)
    att_heads, attn_w = together(att_heads, attn_w)
    attn_w = across(attn_w)
    x_low = inputs.reshape(tokens, width)
    rate = jnp.full((1, PAIR), 2.0 / width, F32) / valid_total
    (
        att_low, normed_mlp, activated, result, grad_down_in, loss_row, grads, grad_hidden, grad_branch, grad_heads,
    ) = mlp(
        x_low,
        att_heads,
        gain_m,
        teacher_states.reshape(tokens, width),
        out_cotangent.reshape(tokens, width),
        valid_float.reshape(tokens, 1),
        rate,
        gate_out,
        rest,
    )

    half = width // 2
    def down_half(rows):
        turned = [
            dot_t(pick_down[rows], activated[:, p * width : (p + 1) * width]).astype(BF16).reshape(-1, own_rows, tokens)
            for p in range(hidden_parts)
        ]
        return dot(jnp.stack(turned, axis=1).reshape(hidden_parts * half, tokens), grad_down_in)

    down_sent = swap(down_half(slice(half, None)).astype(BF16), "c", 1)
    down_sum = (down_half(slice(half)) + down_sent.astype(F32)).astype(BF16)

    def over_yx(value):
        value = value.reshape(2 * lax.axis_size("x"), -1, value.shape[1])
        value = lax.psum_scatter(value, ("y", "x"), scatter_dimension=0, tiled=True)
        return lax.optimization_barrier(value)[0]

    xs = lax.axis_size("x")
    down_sum = down_sum.reshape(2, xs, -1, width)

    def add_axis(value, name, axis):
        size = value.shape[axis]
        received = [swap(lax.index_in_dim(value, k, axis, False), name, k) for k in range(1, size)]
        value = lax.index_in_dim(value, 0, axis, False).astype(F32)
        for piece in received:
            value = value + piece.astype(F32)
        return value.astype(BF16)

    down_left = add_axis(down_sum[:, :, :, :half], "y", 0)
    down_right = add_axis(down_sum[:, :, :, half:], "x", 1)
    grad_heads = exchange(grad_heads.reshape(seqs, units, local_len, PAIR))
    down_sum = jnp.concatenate([add_axis(down_left, "x", 0), add_axis(down_right, "y", 0)], axis=1)
    turned_mlp = dot_t(pick_native, normed_mlp).astype(BF16)
    mlp_sent = swap(dot(turned_mlp[half:], grads).astype(BF16), "c", 1)
    mlp_sum = (dot(turned_mlp[:half], grads) + mlp_sent.astype(F32)).astype(BF16)

    turned_att = dot_t(pick_output, att_low).astype(BF16)
    out_sent = swap(dot(turned_att[half:], grad_branch).astype(BF16), "c", 1)
    out_sum = (dot(turned_att[:half], grad_branch) + out_sent.astype(F32)).astype(BF16)

    out_sum = add_stage(out_sum, "z").astype(BF16)
    grad_heads, attn_w, *_ = together(grad_heads, attn_w, mlp_sum, out_sum, down_sum)
    mlp_sum = over_yx(mlp_sum)

    grad_qkv = attend_backward(qkv, grad_heads, totals, cos_all, sin_all)
    grad_own = exchange(grad_qkv).reshape(zs, batch, 3, units, local_len, PAIR)

    value = head_grads(normed_all, grad_qkv, loss_row, pick_heads)
    for name in ("c", "x", "y"):
        value = add_stage(value, name)
    owned_down = add_stage(down_sum, "z")[:own_down]
    value, grad_own, owned_down, out_sum, mlp_sum = together(value, grad_own, owned_down, out_sum, mlp_sum)
    value = value.astype(BF16)
    out_sum = add_stage(add_stage(out_sum, "y"), "x")
    owned_output = out_sum
    value = value.reshape(zs, own_rows, value.shape[1])
    value = lax.all_to_all(value, "z", split_axis=0, concat_axis=0, tiled=True)
    columns = 3 * units * PAIR
    loss_value = jnp.sum(value[:, 0, columns:].astype(F32)) / valid_total
    value = value[:, :, :columns].reshape(zs, own_rows, units, 3, PAIR).astype(F32)
    owned_qkv = value.transpose(3, 1, 0, 2, 4).reshape(3, own_rows, width)

    mlp_sum = mlp_sum.reshape(zs, own_rows, -1)
    mlp_sum = [mlp_sum[0]] + [swap(mlp_sum[k], "z", k) for k in range(1, zs)]
    grad_in, grad_first = last(grad_own, x_low, gain_a, attn_w, grad_hidden)

    gain_grad_a = (
        jnp.sum(w_query.astype(F32) * owned_qkv[0], axis=1)
        + jnp.sum(w_key.astype(F32) * owned_qkv[1], axis=1)
        + jnp.sum(w_value.astype(F32) * owned_qkv[2], axis=1)
    ) / attn_gain.astype(F32)
    owned_gate, owned_up, gain_grad_m = finish(mlp_sum, w_gate, w_up, own_down)
    gain_grad_m = gain_grad_m / mlp_gain.astype(F32)
    return (
        result.reshape(batch, local_len, width),
        loss_value,
        grad_in.reshape(batch, local_len, width),
        grad_first.reshape(batch, local_len, width),
        gain_grad_a,
        owned_qkv[0],
        owned_qkv[1],
        owned_qkv[2],
        owned_output,
        gain_grad_m,
        owned_gate,
        owned_up,
        owned_down,
    )


def solution(mesh):
    seqs, dps = mesh.devices.shape
    fine = Mesh(mesh.devices.reshape(seqs // 2, 2, dps // 2, 2), ALL)
    tokens = P(("x", "c"), SEQ, None)
    rows = P(ALL, None)
    gain = P(ALL)
    return jax.shard_map(
        on_device,
        mesh=fine,
        in_specs=(
            tokens, tokens, tokens, tokens, P(("x", "c"), SEQ), gain, rows, rows, rows, rows, gain, rows, rows, rows,
        ),
        out_specs=(
            tokens, P(), tokens, tokens, gain, rows, rows, rows, rows, gain, rows, rows, rows,
        ),
        check_vma=False,
    )
```

```python
import functools

import jax
import jax.numpy as jnp
from jax import lax
from jax.experimental import pallas as pl
from jax.experimental.pallas import tpu as pltpu
from jax.sharding import Mesh
from jax.sharding import PartitionSpec as P

HEAD_DIM = 64
BLOCK = 256
MLP_STEP = 512
PAIR = 2 * HEAD_DIM

EPSILON = 1e-06
THETA = 10000.0
SCALE = 0.125
ALL = ("z", "y", "x", "c")
SEQ = ("z", "y")
F32 = jnp.float32
BF16 = jnp.bfloat16


def rotary_tables(positions):
    lane = jnp.arange(PAIR, dtype=jnp.int32)
    half = HEAD_DIM // 2
    index = (lane % half).astype(F32)
    frequency = THETA ** (-(index * 2.0 / HEAD_DIM))
    angles = positions.astype(F32)[:, None] * frequency[None, :]
    sign = jnp.where(lane % HEAD_DIM < half, -1.0, 1.0)[None, :]
    return jnp.cos(angles), jnp.sin(angles) * sign


def partner(values):
    half = HEAD_DIM // 2
    lane = lax.broadcasted_iota(jnp.int32, values.shape, values.ndim - 1)
    first = lane % HEAD_DIM < half
    width = values.shape[-1]
    return jnp.where(
        first,
        pltpu.roll(values, width - half, values.ndim - 1),
        pltpu.roll(values, half, values.ndim - 1),
    )


def dot_t(left, right):
    return lax.dot_general(left, right, (((1,), (1,)), ((), ())), preferred_element_type=F32)


def t_dot(left, right):
    return lax.dot_general(left, right, (((0,), (0,)), ((), ())), preferred_element_type=F32)


def dot(left, right):
    return jnp.dot(left, right, preferred_element_type=F32)


def attend_forward_kernel(qkv_ref, out_ref, total_ref):
    parts, _, _, rows, _ = qkv_ref.shape
    per_block = BLOCK // rows
    blocks = parts // per_block
    for head in range(2):
        lanes = pl.ds(head * HEAD_DIM, HEAD_DIM)
        for block in range(blocks):
            lo, hi = block * per_block, (block + 1) * per_block
            query = qkv_ref[lo:hi, 0, 0, :, lanes].reshape(BLOCK, HEAD_DIM)
            keys = qkv_ref[0:hi, 1, 0, :, lanes].reshape(hi * rows, HEAD_DIM)
            values = qkv_ref[0:hi, 2, 0, :, lanes].reshape(hi * rows, HEAD_DIM)
            scores = dot_t(keys, query * SCALE)
            top = jnp.max(scores, axis=0, keepdims=True)
            weights = jnp.exp(scores - top)
            total = jnp.sum(weights, axis=0, keepdims=True)
            probs = (weights * (1.0 / total)).astype(BF16)
            mixed = t_dot(values, probs)
            out_ref[lo:hi, 0, :, lanes] = mixed.T.astype(BF16).reshape(per_block, rows, HEAD_DIM)
            total_ref[0, head, block : block + 1, :] = top + jnp.log(total)


def attend_backward_kernel(qkv_ref, grad_ref, total_ref, cos_ref, sin_ref, out_ref, dk_acc, dv_acc):
    parts, _, _, rows, _ = qkv_ref.shape
    per_block = BLOCK // rows
    blocks = parts // per_block
    dk_acc[...] = jnp.zeros_like(dk_acc)
    dv_acc[...] = jnp.zeros_like(dv_acc)
    for block in range(blocks):
        lo, hi = block * per_block, (block + 1) * per_block
        keys_n = hi * rows
        dq_parts = []
        for head in range(2):
            lanes = pl.ds(head * HEAD_DIM, HEAD_DIM)
            query = qkv_ref[lo:hi, 0, 0, :, lanes].reshape(BLOCK, HEAD_DIM)
            grad = grad_ref[lo:hi, 0, :, lanes].reshape(BLOCK, HEAD_DIM)
            keys = qkv_ref[0:hi, 1, 0, :, lanes].reshape(keys_n, HEAD_DIM)
            values = qkv_ref[0:hi, 2, 0, :, lanes].reshape(keys_n, HEAD_DIM)
            scores = dot_t(keys, query * SCALE)
            probs = jnp.exp(scores - total_ref[0, head, block : block + 1, :])
            grad_probs = dot_t(values, grad)
            inner = jnp.sum(probs * grad_probs, axis=0, keepdims=True)
            grad_scores = (probs * (grad_probs - inner)).astype(BF16)
            dk_acc[0:keys_n, lanes] += dot(grad_scores, query) * SCALE
            dv_acc[0:keys_n, lanes] += dot(probs.astype(BF16), grad)
            dq_parts.append(t_dot(keys, grad_scores).T * SCALE)
        dq = jnp.concatenate(dq_parts, axis=1)
        cos = cos_ref[block * BLOCK : (block + 1) * BLOCK, :]
        sin = sin_ref[block * BLOCK : (block + 1) * BLOCK, :]
        dq = (dq * cos - partner(dq) * sin).astype(BF16)
        out_ref[lo:hi, 0, 0, :, :] = dq.reshape(per_block, rows, PAIR)
    dk = dk_acc[...]
    dk = (dk * cos_ref[...] - partner(dk) * sin_ref[...]).astype(BF16)
    out_ref[:, 1, 0, :, :] = dk.reshape(parts, rows, PAIR)
    out_ref[:, 2, 0, :, :] = dv_acc[...].astype(BF16).reshape(parts, rows, PAIR)


VMEM_LIMIT = 60 * 1024 * 1024


def attend_backward(qkv, grad_att, totals, cos, sin):
    parts, _, units, rows, _ = qkv.shape
    length = parts * rows
    blocks = length // BLOCK
    return pl.pallas_call(
        attend_backward_kernel,
        grid=(units,),
        in_specs=[
            pl.BlockSpec((parts, 3, 1, rows, PAIR), lambda u: (0, 0, u, 0, 0)),
            pl.BlockSpec((parts, 1, rows, PAIR), lambda u: (0, u, 0, 0)),
            pl.BlockSpec((1, 2, blocks, BLOCK), lambda u: (u, 0, 0, 0)),
            pl.BlockSpec((length, PAIR), lambda u: (0, 0)),
            pl.BlockSpec((length, PAIR), lambda u: (0, 0)),
        ],
        out_specs=pl.BlockSpec((parts, 3, 1, rows, PAIR), lambda u: (0, 0, u, 0, 0)),
        out_shape=jax.ShapeDtypeStruct((parts, 3, units, rows, PAIR), BF16),
        scratch_shapes=[pltpu.VMEM((length, PAIR), F32), pltpu.VMEM((length, PAIR), F32)],
        compiler_params=pltpu.CompilerParams(vmem_limit_bytes=VMEM_LIMIT),
        name="attend_backward",
        cost_estimate=cost(units * length * length, 22),
    )(qkv, grad_att, totals, cos, sin)


def swap(array, name, distance):
    size = lax.axis_size(name)
    return lax.ppermute(array, name, [(i, i ^ distance) for i in range(size)])


def pick(array, index, axis):
    return lax.dynamic_index_in_dim(array, index, axis, keepdims=False)


def arrange(pieces, at):
    bit = 1
    while bit < len(pieces):
        odd = (at & bit) != 0
        pieces = [jnp.where(odd, pieces[j ^ bit], pieces[j]) for j in range(len(pieces))]
        bit *= 2
    return pieces


def stage_rows(rows, order, relative=ALL):
    sizes = [lax.axis_size(name) for name in order]
    per = rows // functools.reduce(lambda a, b: a * b, sizes)
    index = lax.broadcasted_iota(jnp.int32, (rows, 1), 0)
    left, inner = index // per, index % per
    place = {}
    for name, size in zip(reversed(order), reversed(sizes)):
        place[name] = left % size
        if name in relative:
            place[name] = place[name] ^ lax.axis_index(name)
        left = left // size
    device = jnp.zeros_like(index)
    for name in ALL:
        device = device * lax.axis_size(name) + place[name]
    return device * per + inner


def add_stage(value, name):
    size = lax.axis_size(name)
    value = value.astype(BF16).reshape(size, -1, value.shape[1])
    received = [swap(value[k], name, k) for k in range(1, size)]
    value = value[0].astype(F32)
    for piece in received:
        value = value + piece.astype(F32)
    return value


def together(*values):
    return lax.optimization_barrier(values)


def cost(size, factor):
    return pl.CostEstimate(flops=0, bytes_accessed=int(size * factor), transcendentals=0)


def params():
    return pltpu.CompilerParams(vmem_limit_bytes=VMEM_LIMIT)


def front_kernel(
    x_ref, first_ref, gain_ref, cos_ref, sin_ref, weight_ref, normed_out, qkv_out, att_ref, total_ref, weights, normed_ref,
    qkv_ref, left,
):
    parts, rows, width = x_ref.shape
    units = first_ref.shape[1]
    per_block = BLOCK // rows
    blocks = parts // per_block
    gain = gain_ref[...]
    for kind in range(3):
        for unit in range(units):
            at = (kind * units + unit) * PAIR
            weights[:, at : at + PAIR] = weight_ref[3 * unit + kind]
    wide = units * PAIR
    for block in range(blocks):
        lo, hi = block * per_block, (block + 1) * per_block
        x = x_ref[lo:hi].reshape(BLOCK, width).astype(F32)
        inv = lax.rsqrt(jnp.mean(x * x, axis=-1, keepdims=True) + EPSILON)
        normed = (x * inv * gain).astype(BF16)
        normed_ref[lo:hi] = normed.reshape(per_block, rows, width)
        values = dot(normed, weights[...])
        cos = jnp.concatenate([cos_ref[block * BLOCK : (block + 1) * BLOCK, :]] * (2 * units), axis=1)
        sin = jnp.concatenate([sin_ref[block * BLOCK : (block + 1) * BLOCK, :]] * (2 * units), axis=1)
        turning = values[:, : 2 * wide]
        turned = (turning * cos + partner(turning) * sin).astype(BF16)
        for unit in range(units):
            lanes = slice(unit * PAIR, (unit + 1) * PAIR)
            qkv_ref[lo:hi, 0, unit] = turned[:, :wide][:, lanes].reshape(per_block, rows, PAIR)
            qkv_ref[lo:hi, 1, unit] = turned[:, wide:][:, lanes].reshape(per_block, rows, PAIR)
            first = first_ref[lo:hi, unit].reshape(BLOCK, PAIR).astype(F32)
            mixed = (0.5 * values[:, 2 * wide :][:, lanes] + 0.5 * first).astype(BF16)
            qkv_ref[lo:hi, 2, unit] = mixed.reshape(per_block, rows, PAIR)
    sent = [
        pltpu.make_async_copy(normed_ref, normed_out, left.at[0]),
        pltpu.make_async_copy(qkv_ref, qkv_out, left.at[1]),
    ]
    for copy in sent:
        copy.start()
    for unit in range(units):
        one = pl.ds(unit, 1)
        attend_forward_kernel(qkv_ref.at[:, :, one], att_ref.at[:, one], total_ref.at[one])
    for copy in sent:
        copy.wait()


def front(x, first, gain, cos, sin, weights):
    parts, rows, width = x.shape
    units = first.shape[1]
    length = parts * rows
    blocks = length // BLOCK
    outside = pl.BlockSpec(memory_space=pl.ANY)
    normed = (parts, rows, width)
    qkv = (parts, 3, units, rows, PAIR)
    return pl.pallas_call(
        front_kernel,
        grid=(1,),
        in_specs=[
            still(*normed), still(*first.shape), still(1, width), still(length, PAIR), still(length, PAIR), still(*weights.shape),
        ],
        out_specs=[outside, outside, still(*first.shape), still(units, 2, blocks, BLOCK)],
        out_shape=[
            jax.ShapeDtypeStruct(normed, BF16),
            jax.ShapeDtypeStruct(qkv, BF16),
            jax.ShapeDtypeStruct(first.shape, BF16),
            jax.ShapeDtypeStruct((units, 2, blocks, BLOCK), F32),
        ],
        scratch_shapes=[
            pltpu.VMEM((width, 3 * units * PAIR), BF16),
            pltpu.VMEM(normed, BF16),
            pltpu.VMEM(qkv, BF16),
            pltpu.SemaphoreType.DMA((2,)),
        ],
        compiler_params=params(),
        name="front",
        cost_estimate=cost(units * length * length, 27),
    )(x, first, gain, cos, sin, weights)


def sections(weight_ref):
    outer, parts, rows, columns = weight_ref.shape
    return [weight_ref[:, part].reshape(outer * rows, columns) for part in range(parts)]


def dot_sections(left, weight_ref):
    parts = sections(weight_ref)
    wide = left.shape[1] // len(parts)
    total = dot(left[:, :wide], parts[0])
    for at in range(1, len(parts)):
        total = total + dot(left[:, at * wide : (at + 1) * wide], parts[at])
    return total


def dot_t_sections(left, weight_ref):
    return jnp.concatenate([dot_t(left, part) for part in sections(weight_ref)], axis=1)


def mlp_kernel(
    x_ref, heads_ref, gain_ref, teacher_ref, cotangent_ref, valid_ref, rate_ref, gate_out, up_down,
    att_out, normed_out, act_out, result_out, grad_low_out, grads_out, loss_ref, grad_hidden_ref, branch_ref, out_heads_ref,
    wo, wg, wu, wd, gates, ups, hidden_ref, total, att_ref, normed_ref, act_ref, result_ref, grad_low_ref, grads_ref,
    arrived, left,
):
    tokens, width = x_ref.shape
    steps, _, sides, _, wide = wg.shape
    parts = steps * wide // width
    per = width // wide
    deep = sides // per

    def output_copy():
        return pltpu.make_async_copy(
            gate_out.at[:, :, :, pl.ds(parts * width, width)], wo, arrived.at[3 * steps]
        )

    def copies(step):
        lanes = pl.ds(step * wide, wide)
        rows = pl.ds(step % per * deep, deep)
        across = pl.ds((parts + step // per) * width, width)
        return (
            pltpu.make_async_copy(gate_out.at[:, :, :, lanes], wg.at[step], arrived.at[3 * step]),
            pltpu.make_async_copy(up_down.at[:, :, :, lanes], wu.at[step], arrived.at[3 * step + 1]),
            pltpu.make_async_copy(up_down.at[:, rows, :, across], wd.at[step], arrived.at[3 * step + 2]),
        )

    sent = [
        pltpu.make_async_copy(source, target, left.at[at])
        for at, (source, target) in enumerate(
            (
                (att_ref, att_out),
                (normed_ref, normed_out),
                (act_ref, act_out),
                (result_ref, result_out),
                (grad_low_ref, grad_low_out),
            )
        )
    ]
    sent += [
        pltpu.make_async_copy(
            grads_ref.at[step], grads_out.at[:, pl.ds(2 * step * wide, 2 * wide)], left.at[5 + step]
        )
        for step in range(steps)
    ]

    output_copy().start()
    for step in range(steps):
        for copy in copies(step):
            copy.start()

    for pair in range(width // PAIR):
        at, unit = divmod(pair, heads_ref.shape[2])
        att_ref[:, pair * PAIR : (pair + 1) * PAIR] = heads_ref[at, :, unit].reshape(tokens, PAIR)
    output_copy().wait()
    hidden = x_ref[...].astype(F32) + dot_sections(att_ref[...], wo)
    inv = lax.rsqrt(jnp.mean(hidden * hidden, axis=-1, keepdims=True) + EPSILON)
    hidden_ref[...] = hidden
    result_ref[...] = hidden
    normed_ref[...] = (hidden * inv * gain_ref[...]).astype(BF16)
    sent[0].start()
    sent[1].start()

    for step in range(steps):
        for copy in copies(step):
            copy.wait()
        gate = dot_sections(normed_ref[...], wg.at[step])
        up = dot_sections(normed_ref[...], wu.at[step])
        act = (gate * jax.nn.sigmoid(gate) * up).astype(BF16)
        gates[step] = gate
        ups[step] = up
        act_ref[:, step * wide : (step + 1) * wide] = act
        result_ref[...] += dot_sections(act, wd.at[step])

    sent[2].start()
    sent[3].start()
    error = result_ref[...] - teacher_ref[...].astype(F32)
    valid = valid_ref[...]
    grad = cotangent_ref[...].astype(F32) + rate_ref[0:1, 0:1] * valid * error
    grad_hidden_ref[...] = grad
    grad_low_ref[...] = grad.astype(BF16)
    sent[4].start()
    losses = jnp.sum(error * error * (valid / width), axis=0, keepdims=True)
    loss = losses[:, :PAIR]
    for at in range(PAIR, width, PAIR):
        loss = loss + losses[:, at : at + PAIR]
    loss_ref[...] = loss
    total[...] = jnp.zeros_like(total)

    for step in range(steps):
        gate = gates[step]
        up = ups[step]
        sigmoid = jax.nn.sigmoid(gate)
        grad_act = dot_t_sections(grad_low_ref[...], wd.at[step])
        grad_gate = (grad_act * up * (sigmoid * (1.0 + gate * (1.0 - sigmoid)))).astype(BF16)
        grad_up = (grad_act * (gate * sigmoid)).astype(BF16)
        grads_ref[step, :, :wide] = grad_gate
        grads_ref[step, :, wide:] = grad_up
        sent[5 + step].start()
        total[...] += dot_t_sections(grad_gate, wg.at[step]) + dot_t_sections(grad_up, wu.at[step])

    hidden = hidden_ref[...]
    inv = lax.rsqrt(jnp.mean(hidden * hidden, axis=-1, keepdims=True) + EPSILON)
    scaled = hidden * inv
    scaled_grad = total[...] * gain_ref[...]
    grad = grad_hidden_ref[...] + inv * (
        scaled_grad - scaled * jnp.mean(scaled_grad * scaled, axis=-1, keepdims=True)
    )
    grad_hidden_ref[...] = grad
    branch = grad.astype(BF16)
    branch_ref[...] = branch
    value = dot_t_sections(branch, wo).astype(BF16)
    _, batch, units, rows, _ = out_heads_ref.shape
    for pair in range(width // PAIR):
        at, unit = divmod(pair, units)
        out_heads_ref[at, :, unit] = value[:, pair * PAIR : (pair + 1) * PAIR].reshape(batch, rows, PAIR)
    for copy in sent:
        copy.wait()


def still(*shape):
    return pl.BlockSpec(shape, lambda j: (0,) * len(shape))


def mlp(x, heads, gain, teacher, cotangent, valid, rate, gate_out, up_down):
    tokens, width = x.shape
    outer, sides, rows, _ = gate_out.shape
    parts = gate_out.shape[3] // width - 1
    wide = MLP_STEP
    steps = parts * width // wide
    deep = sides * wide // width
    whole = still(tokens, width)
    outside = pl.BlockSpec(memory_space=pl.ANY)
    low = jax.ShapeDtypeStruct((tokens, width), BF16)
    full = jax.ShapeDtypeStruct((tokens, width), F32)
    hidden = (tokens, parts * width)
    grads = (tokens, 2 * parts * width)
    return pl.pallas_call(
        mlp_kernel,
        grid=(1,),
        in_specs=[whole, still(*heads.shape), still(1, width), whole, whole, still(tokens, 1), still(1, PAIR)]
        + [outside, outside],
        out_specs=[outside] * 6 + [still(1, PAIR), whole, whole, still(*heads.shape)],
        out_shape=[
            low,
            low,
            jax.ShapeDtypeStruct(hidden, BF16),
            full,
            low,
            jax.ShapeDtypeStruct(grads, BF16),
            jax.ShapeDtypeStruct((1, PAIR), F32),
            full,
            low,
            jax.ShapeDtypeStruct(heads.shape, BF16),
        ],
        scratch_shapes=[
            pltpu.VMEM((outer, sides, rows, width), BF16),
            pltpu.VMEM((steps, outer, sides, rows, wide), BF16),
            pltpu.VMEM((steps, outer, sides, rows, wide), BF16),
            pltpu.VMEM((steps, outer, deep, rows, width), BF16),
            pltpu.VMEM((steps, tokens, wide), F32),
            pltpu.VMEM((steps, tokens, wide), F32),
            pltpu.VMEM((tokens, width), F32),
            pltpu.VMEM((tokens, width), F32),
            pltpu.VMEM((tokens, width), BF16),
            pltpu.VMEM((tokens, width), BF16),
            pltpu.VMEM(hidden, BF16),
            pltpu.VMEM((tokens, width), F32),
            pltpu.VMEM((tokens, width), BF16),
            pltpu.VMEM((steps, tokens, 2 * wide), BF16),
            pltpu.SemaphoreType.DMA((3 * steps + 1,)),
            pltpu.SemaphoreType.DMA((5 + steps,)),
        ],
        compiler_params=params(),
        name="mlp",
        cost_estimate=cost(tokens * width * parts, 80),
    )(x, heads, gain, teacher, cotangent, valid, rate, gate_out, up_down)


def picker(place, width):
    lane = lax.broadcasted_iota(jnp.int32, (place.shape[0], width), 1)
    return jnp.where(lane == place, 1.0, 0.0).astype(BF16)


def head_grads_kernel(normed_ref, grads_ref, loss_ref, pick_ref, out_ref, turned):
    parts, kinds, units, rows, _ = grads_ref.shape
    width = normed_ref.shape[2]
    normed = normed_ref[...].reshape(parts * rows, width)
    for unit in range(units):
        for kind in range(kinds):
            value = t_dot(grads_ref[:, kind, unit].reshape(parts * rows, PAIR), normed)
            if kind == 2:
                value = 0.5 * value
            at = (unit * kinds + kind) * PAIR
            turned[at : at + PAIR, :] = value.astype(BF16)
    columns = turned.shape[0]
    out_ref[:, :columns] = dot_t(pick_ref[...], turned[...]).astype(BF16)
    out_ref[:, columns:] = jnp.broadcast_to(loss_ref[...], (width, PAIR)).astype(BF16)


def head_grads(normed, grads, loss_row, pick):
    width = normed.shape[2]
    columns = 3 * grads.shape[2] * PAIR
    return pl.pallas_call(
        head_grads_kernel,
        out_shape=jax.ShapeDtypeStruct((width, columns + PAIR), BF16),
        scratch_shapes=[pltpu.VMEM((columns, width), BF16)],
        compiler_params=params(),
        name="head_grads",
        cost_estimate=cost(normed.size, 24),
    )(normed, grads, loss_row, pick)


def last_kernel(heads_ref, x_ref, gain_ref, weight_ref, grad_hidden_ref, grad_in_ref, first_ref, grads):
    tokens, width = x_ref.shape
    for kind in range(3):
        for pair in range(width // PAIR):
            at = kind * width + pair * PAIR
            place, unit = divmod(pair, heads_ref.shape[3])
            piece = heads_ref[place, :, kind, unit].reshape(tokens, PAIR)
            if kind == 2:
                half = 0.5 * piece.astype(F32)
                first_ref[:, pair * PAIR : (pair + 1) * PAIR] = half
                piece = half.astype(BF16)
            grads[:, at : at + PAIR] = piece
    grad_norm = dot_t_sections(grads[...], weight_ref)
    x = x_ref[...].astype(F32)
    inv = lax.rsqrt(jnp.mean(x * x, axis=-1, keepdims=True) + EPSILON)
    scaled = x * inv
    scaled_grad = grad_norm * gain_ref[...]
    grad_in_ref[...] = grad_hidden_ref[...] + inv * (
        scaled_grad - scaled * jnp.mean(scaled_grad * scaled, axis=-1, keepdims=True)
    )


def last(heads, x, gain, weights, grad_hidden):
    tokens, width = x.shape
    return pl.pallas_call(
        last_kernel,
        grid=(1,),
        in_specs=[
            still(*heads.shape),
            still(tokens, width),
            still(1, width),
            pl.BlockSpec(weights.shape[:3] + (3 * width,), lambda j: (0, 0, 0, 0)),
            still(tokens, width),
        ],
        out_specs=[still(tokens, width), still(tokens, width)],
        out_shape=[
            jax.ShapeDtypeStruct((tokens, width), F32),
            jax.ShapeDtypeStruct((tokens, width), F32),
        ],
        scratch_shapes=[pltpu.VMEM((tokens, 3 * width), BF16)],
        compiler_params=params(),
        name="last",
        cost_estimate=cost(tokens * width, 84),
    )(heads, x, gain, weights, grad_hidden)


def finish_kernel(*refs, own_down):
    pieces, (gate_w_ref, up_w_ref), (gate_ref, up_ref, gain_ref) = refs[:-5], refs[-5:-3], refs[-3:]
    rows, columns = pieces[0].shape
    total = pieces[0][...].astype(F32)
    for piece in pieces[1:]:
        total = total + piece[...].astype(F32)
    parts = -(-own_down // rows)
    width = columns // (2 * parts)
    gain = jnp.zeros((rows, 1), F32)
    for side, (weight_ref, out_ref) in enumerate(((gate_w_ref, gate_ref), (up_w_ref, up_ref))):
        values = []
        for device in range(width // rows):
            for part in range(parts):
                step, lane = divmod(part * width + device * rows, MLP_STEP)
                at = (2 * step + side) * MLP_STEP + lane
                values.append(total[:, at : at + min(rows, own_down - part * rows)])
        value = jnp.concatenate(values, axis=1)
        out_ref[...] = value
        gain = gain + jnp.sum(value * weight_ref[...].astype(F32), axis=1, keepdims=True)
    gain_ref[...] = jnp.broadcast_to(gain, gain_ref.shape)


def finish(pieces, w_gate, w_up, own_down):
    rows, hidden = w_gate.shape
    if rows % 8 == 0:
        gate, up, gain = pl.pallas_call(
            functools.partial(finish_kernel, own_down=own_down),
            out_shape=[
                jax.ShapeDtypeStruct((rows, hidden), F32),
                jax.ShapeDtypeStruct((rows, hidden), F32),
                jax.ShapeDtypeStruct((rows, PAIR), F32),
            ],
            compiler_params=params(),
            name="finish",
        )(*pieces, w_gate, w_up)
        return gate, up, gain[:, 0]
    total = sum(piece.astype(F32) for piece in pieces).reshape(rows, -1, 2, MLP_STEP)
    parts = -(-own_down // rows)

    def unpack(grad):
        grad = grad.reshape(rows, parts, -1, rows).transpose(0, 2, 1, 3)
        return grad.reshape(rows, -1, parts * rows)[:, :, :own_down].reshape(rows, hidden)

    gate, up = unpack(total[:, :, 0]), unpack(total[:, :, 1])
    return gate, up, jnp.sum(gate * w_gate.astype(F32) + up * w_up.astype(F32), axis=1)


STAGES_NATIVE = ("c", "y", "x", "z")
STAGES_OUTPUT = ("c", "z", "y", "x")
STAGES_HEADS = ("c", "x", "y", "z")


def on_device(
    inputs,
    first_values,
    teacher_states,
    out_cotangent,
    token_valid,
    attn_gain,
    w_query,
    w_key,
    w_value,
    w_output,
    mlp_gain,
    w_gate,
    w_up,
    w_down,
):
    batch, local_len, width = inputs.shape
    seqs = lax.axis_size(SEQ)
    tokens = batch * local_len
    length = local_len * seqs
    pairs = width // PAIR
    own_rows = w_query.shape[0]
    own_down = w_down.shape[0]
    zs = lax.axis_size("z")
    units = pairs // zs
    mine = lax.axis_index("y")

    valid_float = token_valid.astype(F32)
    count = jnp.sum(token_valid)
    extra = jnp.stack(
        [
            attn_gain,
            mlp_gain,
            jnp.full((own_rows,), count // 256, jnp.int32).astype(BF16),
            jnp.full((own_rows,), count % 256, jnp.int32).astype(BF16),
        ],
        axis=1,
    )
    extra = jnp.pad(extra, ((0, 0), (0, PAIR - 4)))
    columns = jnp.stack([w_query, w_key, w_value]).reshape(3, own_rows, zs, units, PAIR)
    columns = columns.transpose(2, 3, 0, 1, 4).reshape(zs, 3 * units, own_rows, PAIR)
    columns = jnp.concatenate(
        [columns, jnp.broadcast_to(extra[None, None], (zs, 1, own_rows, PAIR))], axis=1
    )
    blocks = 3 * units + 1
    columns = jnp.broadcast_to(
        columns.reshape(zs, 1, blocks * own_rows, PAIR), (zs, batch, blocks * own_rows, PAIR)
    )
    firsts = first_values.reshape(batch, local_len, zs, units, PAIR).transpose(2, 0, 3, 1, 4)
    firsts = firsts.reshape(zs, batch, units * local_len, PAIR)
    parcel = jnp.concatenate([columns, firsts], axis=2).reshape(seqs, -1, PAIR)

    hidden_parts = -(-own_down // own_rows)
    padded = hidden_parts * own_rows - own_down

    def pack_columns(weight):
        weight = jnp.pad(weight.reshape(own_rows, -1, own_down), ((0, 0), (0, 0), (0, padded)))
        weight = weight.reshape(own_rows, -1, hidden_parts, own_rows)
        return weight.transpose(0, 2, 1, 3).reshape(own_rows, hidden_parts * width)

    down_rows = jnp.pad(w_down, ((0, padded), (0, 0))).reshape(hidden_parts, own_rows, width)
    down_rows = down_rows.transpose(1, 0, 2).reshape(own_rows, hidden_parts * width)
    def along_z(rows):
        pieces = [rows] + [swap(rows, "z", k) for k in range(1, zs)]
        return jnp.stack(arrange(pieces, lax.axis_index("z")), axis=0)

    def across(rows):
        rows = lax.all_gather(rows, ("y", "x", "c"), axis=0)
        if own_rows % 16:
            rows = rows.transpose(1, 0, 2, 3).reshape(1, width // BLOCK, BLOCK, rows.shape[3])
        return rows

    x_own, x_sent = pick(inputs, mine, 0), pick(inputs, 1 - mine, 0)
    x_sent = swap(x_sent, "y", 1)
    gate_out = along_z(jnp.concatenate([pack_columns(w_gate), w_output], axis=1))
    rest = jnp.concatenate([pack_columns(w_up), down_rows], axis=1)
    gate_out, rest, parcel, x_sent = together(gate_out, rest, parcel, x_sent)
    gate_out = across(gate_out)
    rest = along_z(rest)
    rest, x_own, x_sent, parcel = together(rest, x_own, x_sent, parcel)
    rest = across(rest)
    parcel = lax.all_to_all(parcel, SEQ, split_axis=0, concat_axis=0, tiled=True)
    x_all = along_z(jnp.stack(arrange([x_own, x_sent], mine), axis=0)).reshape(seqs, local_len, width)
    x_all, attn_rows = together(x_all, jnp.concatenate([w_query, w_key, w_value], axis=1))
    attn_w = along_z(attn_rows)

    first_all = parcel[:, blocks * own_rows :].reshape(seqs, units, local_len, PAIR)
    head_w = parcel[:, : blocks * own_rows].reshape(seqs, blocks, own_rows, PAIR).transpose(1, 0, 2, 3)
    for at, name in ((2, "x"), (3, "c")):
        pieces = [head_w] + [swap(head_w, name, k) for k in range(1, lax.axis_size(name))]
        head_w = jnp.stack(arrange(pieces, lax.axis_index(name)), axis=at)
    head_w = head_w.reshape(blocks, width, PAIR)
    extra_all = head_w[blocks - 1].astype(F32).T
    gain_a = extra_all[0:1, :]
    gain_m = extra_all[1:2, :]
    valid_total = jnp.sum(extra_all[2] * 256.0 + extra_all[3]) / own_rows

    cos_all, sin_all = rotary_tables(jnp.arange(length, dtype=jnp.int32))
    pick_native = picker(stage_rows(width, STAGES_NATIVE, ("c", "z")), width)
    pick_down = picker(stage_rows(width, STAGES_NATIVE), width)
    pick_output = picker(stage_rows(width, STAGES_OUTPUT), width)
    pick_heads = picker(stage_rows(width, STAGES_HEADS, ("c", "x", "y")), width)

    normed_all, qkv, attended, totals = front(x_all, first_all, gain_a, cos_all, sin_all, head_w)

    def exchange(array):
        return lax.all_to_all(array, SEQ, split_axis=0, concat_axis=0, tiled=True)

    att_heads = exchange(attended).reshape(zs, batch, units, local_len, PAIR)
    att_heads, attn_w = together(att_heads, attn_w)
    attn_w = across(attn_w)
    x_low = inputs.reshape(tokens, width)
    rate = jnp.full((1, PAIR), 2.0 / width, F32) / valid_total
    (
        att_low, normed_mlp, activated, result, grad_down_in, grads, loss_row, grad_hidden, grad_branch, grad_heads,
    ) = mlp(
        x_low,
        att_heads,
        gain_m,
        teacher_states.reshape(tokens, width),
        out_cotangent.reshape(tokens, width),
        valid_float.reshape(tokens, 1),
        rate,
        gate_out,
        rest,
    )

    half = width // 2
    def down_half(rows):
        turned = [
            dot_t(pick_down[rows], activated[:, p * width : (p + 1) * width]).astype(BF16).reshape(-1, own_rows, tokens)
            for p in range(hidden_parts)
        ]
        return dot(jnp.stack(turned, axis=1).reshape(hidden_parts * half, tokens), grad_down_in)

    down_sent = swap(down_half(slice(half, None)).astype(BF16), "c", 1)
    down_sum = (down_half(slice(half)) + down_sent.astype(F32)).astype(BF16)

    def over_yx(value):
        value = value.reshape(2 * lax.axis_size("x"), -1, value.shape[1])
        value = lax.psum_scatter(value, ("y", "x"), scatter_dimension=0, tiled=True)
        return lax.optimization_barrier(value)[0]

    xs = lax.axis_size("x")
    down_sum = down_sum.reshape(2, xs, -1, width)

    def add_axis(value, name, axis):
        size = value.shape[axis]
        received = [swap(lax.index_in_dim(value, k, axis, False), name, k) for k in range(1, size)]
        value = lax.index_in_dim(value, 0, axis, False).astype(F32)
        for piece in received:
            value = value + piece.astype(F32)
        return value.astype(BF16)

    down_left = add_axis(down_sum[:, :, :, :half], "y", 0)
    down_right = add_axis(down_sum[:, :, :, half:], "x", 1)
    grad_heads = exchange(grad_heads.reshape(seqs, units, local_len, PAIR))
    down_sum = jnp.concatenate([add_axis(down_left, "x", 0), add_axis(down_right, "y", 0)], axis=1)
    turned_mlp = dot_t(pick_native, normed_mlp).astype(BF16)
    mlp_sent = swap(dot(turned_mlp[half:], grads).astype(BF16), "c", 1)
    mlp_sum = (dot(turned_mlp[:half], grads) + mlp_sent.astype(F32)).astype(BF16)

    turned_att = dot_t(pick_output, att_low).astype(BF16)
    out_sent = swap(dot(turned_att[half:], grad_branch).astype(BF16), "c", 1)
    out_sum = (dot(turned_att[:half], grad_branch) + out_sent.astype(F32)).astype(BF16)

    out_sum = add_stage(out_sum, "z").astype(BF16)
    grad_heads, attn_w, *_ = together(grad_heads, attn_w, mlp_sum, out_sum, down_sum)
    mlp_sum = over_yx(mlp_sum)

    grad_qkv = attend_backward(qkv, grad_heads, totals, cos_all, sin_all)
    grad_own = exchange(grad_qkv).reshape(zs, batch, 3, units, local_len, PAIR)

    value = head_grads(normed_all, grad_qkv, loss_row, pick_heads)
    for name in ("c", "x", "y"):
        value = add_stage(value, name)
    owned_down = add_stage(down_sum, "z")[:own_down]
    value, grad_own, owned_down, out_sum, mlp_sum = together(value, grad_own, owned_down, out_sum, mlp_sum)
    value = value.astype(BF16)
    out_sum = add_stage(add_stage(out_sum, "y"), "x")
    owned_output = out_sum
    value = value.reshape(zs, own_rows, value.shape[1])
    value = lax.all_to_all(value, "z", split_axis=0, concat_axis=0, tiled=True)
    columns = 3 * units * PAIR
    loss_value = jnp.sum(value[:, 0, columns:].astype(F32)) / valid_total
    value = value[:, :, :columns].reshape(zs, own_rows, units, 3, PAIR).astype(F32)
    owned_qkv = value.transpose(3, 1, 0, 2, 4).reshape(3, own_rows, width)

    mlp_sum = mlp_sum.reshape(zs, own_rows, -1)
    mlp_sum = [mlp_sum[0]] + [swap(mlp_sum[k], "z", k) for k in range(1, zs)]
    grad_in, grad_first = last(grad_own, x_low, gain_a, attn_w, grad_hidden)

    gain_grad_a = (
        jnp.sum(w_query.astype(F32) * owned_qkv[0], axis=1)
        + jnp.sum(w_key.astype(F32) * owned_qkv[1], axis=1)
        + jnp.sum(w_value.astype(F32) * owned_qkv[2], axis=1)
    ) / attn_gain.astype(F32)
    owned_gate, owned_up, gain_grad_m = finish(mlp_sum, w_gate, w_up, own_down)
    gain_grad_m = gain_grad_m / mlp_gain.astype(F32)
    return (
        result.reshape(batch, local_len, width),
        loss_value,
        grad_in.reshape(batch, local_len, width),
        grad_first.reshape(batch, local_len, width),
        gain_grad_a,
        owned_qkv[0],
        owned_qkv[1],
        owned_qkv[2],
        owned_output,
        gain_grad_m,
        owned_gate,
        owned_up,
        owned_down,
    )


def solution(mesh):
    seqs, dps = mesh.devices.shape
    fine = Mesh(mesh.devices.reshape(seqs // 2, 2, dps // 2, 2), ALL)
    tokens = P(("x", "c"), SEQ, None)
    rows = P(ALL, None)
    gain = P(ALL)
    return jax.shard_map(
        on_device,
        mesh=fine,
        in_specs=(
            tokens, tokens, tokens, tokens, P(("x", "c"), SEQ), gain, rows, rows, rows, rows, gain, rows, rows, rows,
        ),
        out_specs=(
            tokens, P(), tokens, tokens, gain, rows, rows, rows, rows, gain, rows, rows, rows,
        ),
        check_vma=False,
    )
```

```python
import functools

import jax
import jax.numpy as jnp
from jax import lax
from jax.experimental import pallas as pl
from jax.experimental.pallas import tpu as pltpu
from jax.sharding import Mesh
from jax.sharding import PartitionSpec as P

HEAD_DIM = 64
BLOCK = 256
MLP_STEP = 512
PAIR = 2 * HEAD_DIM

EPSILON = 1e-06
THETA = 10000.0
SCALE = 0.125
ALL = ("z", "y", "x", "c")
SEQ = ("z", "y")
F32 = jnp.float32
BF16 = jnp.bfloat16


def rotary_tables(positions):
    lane = jnp.arange(PAIR, dtype=jnp.int32)
    half = HEAD_DIM // 2
    index = (lane % half).astype(F32)
    frequency = THETA ** (-(index * 2.0 / HEAD_DIM))
    angles = positions.astype(F32)[:, None] * frequency[None, :]
    sign = jnp.where(lane % HEAD_DIM < half, -1.0, 1.0)[None, :]
    return jnp.cos(angles), jnp.sin(angles) * sign


def partner(values):
    half = HEAD_DIM // 2
    lane = lax.broadcasted_iota(jnp.int32, values.shape, values.ndim - 1)
    first = lane % HEAD_DIM < half
    width = values.shape[-1]
    return jnp.where(
        first,
        pltpu.roll(values, width - half, values.ndim - 1),
        pltpu.roll(values, half, values.ndim - 1),
    )


def dot_t(left, right):
    return lax.dot_general(left, right, (((1,), (1,)), ((), ())), preferred_element_type=F32)


def t_dot(left, right):
    return lax.dot_general(left, right, (((0,), (0,)), ((), ())), preferred_element_type=F32)


def dot(left, right):
    return jnp.dot(left, right, preferred_element_type=F32)


def attend_forward_kernel(qkv_ref, out_ref, total_ref):
    parts, _, _, rows, _ = qkv_ref.shape
    per_block = BLOCK // rows
    blocks = parts // per_block
    for head in range(2):
        lanes = pl.ds(head * HEAD_DIM, HEAD_DIM)
        for block in range(blocks):
            lo, hi = block * per_block, (block + 1) * per_block
            query = qkv_ref[lo:hi, 0, 0, :, lanes].reshape(BLOCK, HEAD_DIM)
            keys = qkv_ref[0:hi, 1, 0, :, lanes].reshape(hi * rows, HEAD_DIM)
            values = qkv_ref[0:hi, 2, 0, :, lanes].reshape(hi * rows, HEAD_DIM)
            scores = dot_t(keys, query * SCALE)
            top = jnp.max(scores, axis=0, keepdims=True)
            weights = jnp.exp(scores - top)
            total = jnp.sum(weights, axis=0, keepdims=True)
            probs = (weights * (1.0 / total)).astype(BF16)
            mixed = t_dot(values, probs)
            out_ref[lo:hi, 0, :, lanes] = mixed.T.astype(BF16).reshape(per_block, rows, HEAD_DIM)
            total_ref[0, head, block : block + 1, :] = top + jnp.log(total)


def attend_backward_kernel(qkv_ref, grad_ref, total_ref, cos_ref, sin_ref, out_ref, dk_acc, dv_acc):
    parts, _, _, rows, _ = qkv_ref.shape
    per_block = BLOCK // rows
    blocks = parts // per_block
    dk_acc[...] = jnp.zeros_like(dk_acc)
    dv_acc[...] = jnp.zeros_like(dv_acc)
    for block in range(blocks):
        lo, hi = block * per_block, (block + 1) * per_block
        keys_n = hi * rows
        dq_parts = []
        for head in range(2):
            lanes = pl.ds(head * HEAD_DIM, HEAD_DIM)
            query = qkv_ref[lo:hi, 0, 0, :, lanes].reshape(BLOCK, HEAD_DIM)
            grad = grad_ref[lo:hi, 0, :, lanes].reshape(BLOCK, HEAD_DIM)
            keys = qkv_ref[0:hi, 1, 0, :, lanes].reshape(keys_n, HEAD_DIM)
            values = qkv_ref[0:hi, 2, 0, :, lanes].reshape(keys_n, HEAD_DIM)
            scores = dot_t(keys, query * SCALE)
            probs = jnp.exp(scores - total_ref[0, head, block : block + 1, :])
            grad_probs = dot_t(values, grad)
            inner = jnp.sum(probs * grad_probs, axis=0, keepdims=True)
            grad_scores = (probs * (grad_probs - inner)).astype(BF16)
            dk_acc[0:keys_n, lanes] += dot(grad_scores, query) * SCALE
            dv_acc[0:keys_n, lanes] += dot(probs.astype(BF16), grad)
            dq_parts.append(t_dot(keys, grad_scores).T * SCALE)
        dq = jnp.concatenate(dq_parts, axis=1)
        cos = cos_ref[block * BLOCK : (block + 1) * BLOCK, :]
        sin = sin_ref[block * BLOCK : (block + 1) * BLOCK, :]
        dq = (dq * cos - partner(dq) * sin).astype(BF16)
        out_ref[lo:hi, 0, 0, :, :] = dq.reshape(per_block, rows, PAIR)
    dk = dk_acc[...]
    dk = (dk * cos_ref[...] - partner(dk) * sin_ref[...]).astype(BF16)
    out_ref[:, 1, 0, :, :] = dk.reshape(parts, rows, PAIR)
    out_ref[:, 2, 0, :, :] = dv_acc[...].astype(BF16).reshape(parts, rows, PAIR)


VMEM_LIMIT = 60 * 1024 * 1024


def attend_backward(qkv, grad_att, totals, cos, sin):
    parts, _, units, rows, _ = qkv.shape
    length = parts * rows
    blocks = length // BLOCK
    return pl.pallas_call(
        attend_backward_kernel,
        grid=(units,),
        in_specs=[
            pl.BlockSpec((parts, 3, 1, rows, PAIR), lambda u: (0, 0, u, 0, 0)),
            pl.BlockSpec((parts, 1, rows, PAIR), lambda u: (0, u, 0, 0)),
            pl.BlockSpec((1, 2, blocks, BLOCK), lambda u: (u, 0, 0, 0)),
            pl.BlockSpec((length, PAIR), lambda u: (0, 0)),
            pl.BlockSpec((length, PAIR), lambda u: (0, 0)),
        ],
        out_specs=pl.BlockSpec((parts, 3, 1, rows, PAIR), lambda u: (0, 0, u, 0, 0)),
        out_shape=jax.ShapeDtypeStruct((parts, 3, units, rows, PAIR), BF16),
        scratch_shapes=[pltpu.VMEM((length, PAIR), F32), pltpu.VMEM((length, PAIR), F32)],
        compiler_params=pltpu.CompilerParams(vmem_limit_bytes=VMEM_LIMIT),
        name="attend_backward",
        cost_estimate=cost(units * length * length, 22),
    )(qkv, grad_att, totals, cos, sin)


def swap(array, name, distance):
    size = lax.axis_size(name)
    return lax.ppermute(array, name, [(i, i ^ distance) for i in range(size)])


def pick(array, index, axis):
    return lax.dynamic_index_in_dim(array, index, axis, keepdims=False)


def arrange(pieces, at):
    bit = 1
    while bit < len(pieces):
        odd = (at & bit) != 0
        pieces = [jnp.where(odd, pieces[j ^ bit], pieces[j]) for j in range(len(pieces))]
        bit *= 2
    return pieces


def stage_rows(rows, order, relative=ALL):
    sizes = [lax.axis_size(name) for name in order]
    per = rows // functools.reduce(lambda a, b: a * b, sizes)
    index = lax.broadcasted_iota(jnp.int32, (rows, 1), 0)
    left, inner = index // per, index % per
    place = {}
    for name, size in zip(reversed(order), reversed(sizes)):
        place[name] = left % size
        if name in relative:
            place[name] = place[name] ^ lax.axis_index(name)
        left = left // size
    device = jnp.zeros_like(index)
    for name in ALL:
        device = device * lax.axis_size(name) + place[name]
    return device * per + inner


def add_stage(value, name):
    size = lax.axis_size(name)
    value = value.astype(BF16).reshape(size, -1, value.shape[1])
    received = [swap(value[k], name, k) for k in range(1, size)]
    value = value[0].astype(F32)
    for piece in received:
        value = value + piece.astype(F32)
    return value


def together(*values):
    return lax.optimization_barrier(values)


def cost(size, factor):
    return pl.CostEstimate(flops=0, bytes_accessed=int(size * factor), transcendentals=0)


def params():
    return pltpu.CompilerParams(vmem_limit_bytes=VMEM_LIMIT)


def front_kernel(
    x_ref, first_ref, gain_ref, cos_ref, sin_ref, weight_ref, normed_out, qkv_out, att_ref, total_ref, weights, normed_ref,
    qkv_ref, left,
):
    parts, rows, width = x_ref.shape
    units = first_ref.shape[1]
    per_block = BLOCK // rows
    blocks = parts // per_block
    gain = gain_ref[...]
    for kind in range(3):
        for unit in range(units):
            at = (kind * units + unit) * PAIR
            weights[:, at : at + PAIR] = weight_ref[3 * unit + kind]
    wide = units * PAIR
    for block in range(blocks):
        lo, hi = block * per_block, (block + 1) * per_block
        x = x_ref[lo:hi].reshape(BLOCK, width).astype(F32)
        inv = lax.rsqrt(jnp.mean(x * x, axis=-1, keepdims=True) + EPSILON)
        normed = (x * inv * gain).astype(BF16)
        normed_ref[lo:hi] = normed.reshape(per_block, rows, width)
        values = dot(normed, weights[...])
        cos = jnp.concatenate([cos_ref[block * BLOCK : (block + 1) * BLOCK, :]] * (2 * units), axis=1)
        sin = jnp.concatenate([sin_ref[block * BLOCK : (block + 1) * BLOCK, :]] * (2 * units), axis=1)
        turning = values[:, : 2 * wide]
        turned = (turning * cos + partner(turning) * sin).astype(BF16)
        for unit in range(units):
            lanes = slice(unit * PAIR, (unit + 1) * PAIR)
            qkv_ref[lo:hi, 0, unit] = turned[:, :wide][:, lanes].reshape(per_block, rows, PAIR)
            qkv_ref[lo:hi, 1, unit] = turned[:, wide:][:, lanes].reshape(per_block, rows, PAIR)
            first = first_ref[lo:hi, unit].reshape(BLOCK, PAIR).astype(F32)
            mixed = (0.5 * values[:, 2 * wide :][:, lanes] + 0.5 * first).astype(BF16)
            qkv_ref[lo:hi, 2, unit] = mixed.reshape(per_block, rows, PAIR)
    sent = [
        pltpu.make_async_copy(normed_ref, normed_out, left.at[0]),
        pltpu.make_async_copy(qkv_ref, qkv_out, left.at[1]),
    ]
    for copy in sent:
        copy.start()
    for unit in range(units):
        one = pl.ds(unit, 1)
        attend_forward_kernel(qkv_ref.at[:, :, one], att_ref.at[:, one], total_ref.at[one])
    for copy in sent:
        copy.wait()


def front(x, first, gain, cos, sin, weights):
    parts, rows, width = x.shape
    units = first.shape[1]
    length = parts * rows
    blocks = length // BLOCK
    outside = pl.BlockSpec(memory_space=pl.ANY)
    normed = (parts, rows, width)
    qkv = (parts, 3, units, rows, PAIR)
    return pl.pallas_call(
        front_kernel,
        grid=(1,),
        in_specs=[
            still(*normed), still(*first.shape), still(1, width), still(length, PAIR), still(length, PAIR), still(*weights.shape),
        ],
        out_specs=[outside, outside, still(*first.shape), still(units, 2, blocks, BLOCK)],
        out_shape=[
            jax.ShapeDtypeStruct(normed, BF16),
            jax.ShapeDtypeStruct(qkv, BF16),
            jax.ShapeDtypeStruct(first.shape, BF16),
            jax.ShapeDtypeStruct((units, 2, blocks, BLOCK), F32),
        ],
        scratch_shapes=[
            pltpu.VMEM((width, 3 * units * PAIR), BF16),
            pltpu.VMEM(normed, BF16),
            pltpu.VMEM(qkv, BF16),
            pltpu.SemaphoreType.DMA((2,)),
        ],
        compiler_params=params(),
        name="front",
        cost_estimate=cost(units * length * length, 27),
    )(x, first, gain, cos, sin, weights)


def sections(weight_ref):
    outer, parts, rows, columns = weight_ref.shape
    return [weight_ref[:, part].reshape(outer * rows, columns) for part in range(parts)]


def dot_sections(left, weight_ref):
    parts = sections(weight_ref)
    wide = left.shape[1] // len(parts)
    total = dot(left[:, :wide], parts[0])
    for at in range(1, len(parts)):
        total = total + dot(left[:, at * wide : (at + 1) * wide], parts[at])
    return total


def dot_t_sections(left, weight_ref):
    return jnp.concatenate([dot_t(left, part) for part in sections(weight_ref)], axis=1)


def mlp_kernel(
    x_ref, heads_ref, gain_ref, teacher_ref, cotangent_ref, valid_ref, rate_ref, gate_out, up_down,
    att_out, normed_out, act_out, result_out, grad_low_out, grads_out, loss_ref, grad_hidden_ref, branch_ref, out_heads_ref,
    wo, wg, wu, wd, gates, ups, hidden_ref, total, att_ref, normed_ref, act_ref, result_ref, grad_low_ref, grads_ref,
    arrived, left,
):
    tokens, width = x_ref.shape
    steps, _, sides, _, wide = wg.shape
    parts = steps * wide // width
    per = width // wide
    deep = sides // per

    def output_copy():
        return pltpu.make_async_copy(
            gate_out.at[:, :, :, pl.ds(parts * width, width)], wo, arrived.at[3 * steps]
        )

    def copies(step):
        lanes = pl.ds(step * wide, wide)
        rows = pl.ds(step % per * deep, deep)
        across = pl.ds((parts + step // per) * width, width)
        return (
            pltpu.make_async_copy(gate_out.at[:, :, :, lanes], wg.at[step], arrived.at[3 * step]),
            pltpu.make_async_copy(up_down.at[:, :, :, lanes], wu.at[step], arrived.at[3 * step + 1]),
            pltpu.make_async_copy(up_down.at[:, rows, :, across], wd.at[step], arrived.at[3 * step + 2]),
        )

    sent = [
        pltpu.make_async_copy(source, target, left.at[at])
        for at, (source, target) in enumerate(
            (
                (att_ref, att_out),
                (normed_ref, normed_out),
                (act_ref, act_out),
                (result_ref, result_out),
                (grad_low_ref, grad_low_out),
            )
        )
    ]
    sent += [
        pltpu.make_async_copy(
            grads_ref.at[step], grads_out.at[:, pl.ds(2 * step * wide, 2 * wide)], left.at[5 + step]
        )
        for step in range(steps)
    ]

    output_copy().start()
    for step in range(steps):
        for copy in copies(step):
            copy.start()

    for pair in range(width // PAIR):
        at, unit = divmod(pair, heads_ref.shape[2])
        att_ref[:, pair * PAIR : (pair + 1) * PAIR] = heads_ref[at, :, unit].reshape(tokens, PAIR)
    output_copy().wait()
    hidden = x_ref[...].astype(F32) + dot_sections(att_ref[...], wo)
    inv = lax.rsqrt(jnp.mean(hidden * hidden, axis=-1, keepdims=True) + EPSILON)
    hidden_ref[...] = hidden
    result_ref[...] = hidden
    normed_ref[...] = (hidden * inv * gain_ref[...]).astype(BF16)
    sent[0].start()
    sent[1].start()

    for step in range(steps):
        for copy in copies(step):
            copy.wait()
        gate = dot_sections(normed_ref[...], wg.at[step])
        up = dot_sections(normed_ref[...], wu.at[step])
        act = (gate * jax.nn.sigmoid(gate) * up).astype(BF16)
        gates[step] = gate
        ups[step] = up
        act_ref[:, step * wide : (step + 1) * wide] = act
        result_ref[...] += dot_sections(act, wd.at[step])

    sent[2].start()
    sent[3].start()
    error = result_ref[...] - teacher_ref[...].astype(F32)
    valid = valid_ref[...]
    grad = cotangent_ref[...].astype(F32) + rate_ref[0:1, 0:1] * valid * error
    grad_hidden_ref[...] = grad
    grad_low_ref[...] = grad.astype(BF16)
    sent[4].start()
    losses = jnp.sum(error * error * (valid / width), axis=0, keepdims=True)
    loss = losses[:, :PAIR]
    for at in range(PAIR, width, PAIR):
        loss = loss + losses[:, at : at + PAIR]
    loss_ref[...] = loss
    total[...] = jnp.zeros_like(total)

    for step in range(steps):
        gate = gates[step]
        up = ups[step]
        sigmoid = jax.nn.sigmoid(gate)
        grad_act = dot_t_sections(grad_low_ref[...], wd.at[step])
        grad_gate = (grad_act * up * (sigmoid * (1.0 + gate * (1.0 - sigmoid)))).astype(BF16)
        grad_up = (grad_act * (gate * sigmoid)).astype(BF16)
        grads_ref[step, :, :wide] = grad_gate
        grads_ref[step, :, wide:] = grad_up
        sent[5 + step].start()
        total[...] += dot_t_sections(grad_gate, wg.at[step]) + dot_t_sections(grad_up, wu.at[step])

    hidden = hidden_ref[...]
    inv = lax.rsqrt(jnp.mean(hidden * hidden, axis=-1, keepdims=True) + EPSILON)
    scaled = hidden * inv
    scaled_grad = total[...] * gain_ref[...]
    grad = grad_hidden_ref[...] + inv * (
        scaled_grad - scaled * jnp.mean(scaled_grad * scaled, axis=-1, keepdims=True)
    )
    grad_hidden_ref[...] = grad
    branch = grad.astype(BF16)
    branch_ref[...] = branch
    value = dot_t_sections(branch, wo).astype(BF16)
    _, batch, units, rows, _ = out_heads_ref.shape
    for pair in range(width // PAIR):
        at, unit = divmod(pair, units)
        out_heads_ref[at, :, unit] = value[:, pair * PAIR : (pair + 1) * PAIR].reshape(batch, rows, PAIR)
    for copy in sent:
        copy.wait()


def still(*shape):
    return pl.BlockSpec(shape, lambda j: (0,) * len(shape))


def mlp(x, heads, gain, teacher, cotangent, valid, rate, gate_out, up_down):
    tokens, width = x.shape
    outer, sides, rows, _ = gate_out.shape
    parts = gate_out.shape[3] // width - 1
    wide = MLP_STEP
    steps = parts * width // wide
    deep = sides * wide // width
    whole = still(tokens, width)
    outside = pl.BlockSpec(memory_space=pl.ANY)
    low = jax.ShapeDtypeStruct((tokens, width), BF16)
    full = jax.ShapeDtypeStruct((tokens, width), F32)
    hidden = (tokens, parts * width)
    grads = (tokens, 2 * parts * width)
    return pl.pallas_call(
        mlp_kernel,
        grid=(1,),
        in_specs=[whole, still(*heads.shape), still(1, width), whole, whole, still(tokens, 1), still(1, PAIR)]
        + [outside, outside],
        out_specs=[outside] * 6 + [still(1, PAIR), whole, whole, still(*heads.shape)],
        out_shape=[
            low,
            low,
            jax.ShapeDtypeStruct(hidden, BF16),
            full,
            low,
            jax.ShapeDtypeStruct(grads, BF16),
            jax.ShapeDtypeStruct((1, PAIR), F32),
            full,
            low,
            jax.ShapeDtypeStruct(heads.shape, BF16),
        ],
        scratch_shapes=[
            pltpu.VMEM((outer, sides, rows, width), BF16),
            pltpu.VMEM((steps, outer, sides, rows, wide), BF16),
            pltpu.VMEM((steps, outer, sides, rows, wide), BF16),
            pltpu.VMEM((steps, outer, deep, rows, width), BF16),
            pltpu.VMEM((steps, tokens, wide), F32),
            pltpu.VMEM((steps, tokens, wide), F32),
            pltpu.VMEM((tokens, width), F32),
            pltpu.VMEM((tokens, width), F32),
            pltpu.VMEM((tokens, width), BF16),
            pltpu.VMEM((tokens, width), BF16),
            pltpu.VMEM(hidden, BF16),
            pltpu.VMEM((tokens, width), F32),
            pltpu.VMEM((tokens, width), BF16),
            pltpu.VMEM((steps, tokens, 2 * wide), BF16),
            pltpu.SemaphoreType.DMA((3 * steps + 1,)),
            pltpu.SemaphoreType.DMA((5 + steps,)),
        ],
        compiler_params=params(),
        name="mlp",
        cost_estimate=cost(tokens * width * parts, 80),
    )(x, heads, gain, teacher, cotangent, valid, rate, gate_out, up_down)


def picker(place, width):
    lane = lax.broadcasted_iota(jnp.int32, (place.shape[0], width), 1)
    return jnp.where(lane == place, 1.0, 0.0).astype(BF16)


def head_grads_kernel(normed_ref, grads_ref, loss_ref, pick_ref, out_ref, turned):
    parts, kinds, units, rows, _ = grads_ref.shape
    width = normed_ref.shape[2]
    normed = normed_ref[...].reshape(parts * rows, width)
    for unit in range(units):
        for kind in range(kinds):
            value = t_dot(grads_ref[:, kind, unit].reshape(parts * rows, PAIR), normed)
            if kind == 2:
                value = 0.5 * value
            at = (unit * kinds + kind) * PAIR
            turned[at : at + PAIR, :] = value.astype(BF16)
    columns = turned.shape[0]
    out_ref[:, :columns] = dot_t(pick_ref[...], turned[...]).astype(BF16)
    out_ref[:, columns:] = jnp.broadcast_to(loss_ref[...], (width, PAIR)).astype(BF16)


def head_grads(normed, grads, loss_row, pick):
    width = normed.shape[2]
    columns = 3 * grads.shape[2] * PAIR
    return pl.pallas_call(
        head_grads_kernel,
        out_shape=jax.ShapeDtypeStruct((width, columns + PAIR), BF16),
        scratch_shapes=[pltpu.VMEM((columns, width), BF16)],
        compiler_params=params(),
        name="head_grads",
        cost_estimate=cost(normed.size, 24),
    )(normed, grads, loss_row, pick)


def last_kernel(heads_ref, x_ref, gain_ref, weight_ref, grad_hidden_ref, grad_in_ref, first_ref, grads):
    tokens, width = x_ref.shape
    for kind in range(3):
        for pair in range(width // PAIR):
            at = kind * width + pair * PAIR
            place, unit = divmod(pair, heads_ref.shape[3])
            piece = heads_ref[place, :, kind, unit].reshape(tokens, PAIR)
            if kind == 2:
                half = 0.5 * piece.astype(F32)
                first_ref[:, pair * PAIR : (pair + 1) * PAIR] = half
                piece = half.astype(BF16)
            grads[:, at : at + PAIR] = piece
    grad_norm = dot_t_sections(grads[...], weight_ref)
    x = x_ref[...].astype(F32)
    inv = lax.rsqrt(jnp.mean(x * x, axis=-1, keepdims=True) + EPSILON)
    scaled = x * inv
    scaled_grad = grad_norm * gain_ref[...]
    grad_in_ref[...] = grad_hidden_ref[...] + inv * (
        scaled_grad - scaled * jnp.mean(scaled_grad * scaled, axis=-1, keepdims=True)
    )


def last(heads, x, gain, weights, grad_hidden):
    tokens, width = x.shape
    return pl.pallas_call(
        last_kernel,
        grid=(1,),
        in_specs=[
            still(*heads.shape),
            still(tokens, width),
            still(1, width),
            pl.BlockSpec(weights.shape[:3] + (3 * width,), lambda j: (0, 0, 0, 0)),
            still(tokens, width),
        ],
        out_specs=[still(tokens, width), still(tokens, width)],
        out_shape=[
            jax.ShapeDtypeStruct((tokens, width), F32),
            jax.ShapeDtypeStruct((tokens, width), F32),
        ],
        scratch_shapes=[pltpu.VMEM((tokens, 3 * width), BF16)],
        compiler_params=params(),
        name="last",
        cost_estimate=cost(tokens * width, 84),
    )(heads, x, gain, weights, grad_hidden)


def finish_kernel(*refs, own_down):
    pieces, (gate_w_ref, up_w_ref), (gate_ref, up_ref, gain_ref) = refs[:-5], refs[-5:-3], refs[-3:]
    rows, columns = pieces[0].shape
    total = pieces[0][...].astype(F32)
    for piece in pieces[1:]:
        total = total + piece[...].astype(F32)
    parts = -(-own_down // rows)
    width = columns // (2 * parts)
    gain = jnp.zeros((rows, 1), F32)
    for side, (weight_ref, out_ref) in enumerate(((gate_w_ref, gate_ref), (up_w_ref, up_ref))):
        values = []
        for device in range(width // rows):
            for part in range(parts):
                step, lane = divmod(part * width + device * rows, MLP_STEP)
                at = (2 * step + side) * MLP_STEP + lane
                values.append(total[:, at : at + min(rows, own_down - part * rows)])
        value = jnp.concatenate(values, axis=1)
        out_ref[...] = value
        gain = gain + jnp.sum(value * weight_ref[...].astype(F32), axis=1, keepdims=True)
    gain_ref[...] = jnp.broadcast_to(gain, gain_ref.shape)


def finish(pieces, w_gate, w_up, own_down):
    rows, hidden = w_gate.shape
    if rows % 8 == 0:
        gate, up, gain = pl.pallas_call(
            functools.partial(finish_kernel, own_down=own_down),
            out_shape=[
                jax.ShapeDtypeStruct((rows, hidden), F32),
                jax.ShapeDtypeStruct((rows, hidden), F32),
                jax.ShapeDtypeStruct((rows, PAIR), F32),
            ],
            compiler_params=params(),
            name="finish",
        )(*pieces, w_gate, w_up)
        return gate, up, gain[:, 0]
    total = sum(piece.astype(F32) for piece in pieces).reshape(rows, -1, 2, MLP_STEP)
    parts = -(-own_down // rows)

    def unpack(grad):
        grad = grad.reshape(rows, parts, -1, rows).transpose(0, 2, 1, 3)
        return grad.reshape(rows, -1, parts * rows)[:, :, :own_down].reshape(rows, hidden)

    gate, up = unpack(total[:, :, 0]), unpack(total[:, :, 1])
    return gate, up, jnp.sum(gate * w_gate.astype(F32) + up * w_up.astype(F32), axis=1)


STAGES_NATIVE = ("c", "y", "x", "z")
STAGES_OUTPUT = ("c", "z", "y", "x")
STAGES_HEADS = ("c", "x", "y", "z")


def on_device(
    inputs,
    first_values,
    teacher_states,
    out_cotangent,
    token_valid,
    attn_gain,
    w_query,
    w_key,
    w_value,
    w_output,
    mlp_gain,
    w_gate,
    w_up,
    w_down,
):
    batch, local_len, width = inputs.shape
    seqs = lax.axis_size(SEQ)
    tokens = batch * local_len
    length = local_len * seqs
    pairs = width // PAIR
    own_rows = w_query.shape[0]
    own_down = w_down.shape[0]
    zs = lax.axis_size("z")
    units = pairs // zs
    mine = lax.axis_index("y")

    valid_float = token_valid.astype(F32)
    count = jnp.sum(token_valid)
    extra = jnp.stack(
        [
            attn_gain,
            mlp_gain,
            jnp.full((own_rows,), count // 256, jnp.int32).astype(BF16),
            jnp.full((own_rows,), count % 256, jnp.int32).astype(BF16),
        ],
        axis=1,
    )
    extra = jnp.pad(extra, ((0, 0), (0, PAIR - 4)))
    columns = jnp.stack([w_query, w_key, w_value]).reshape(3, own_rows, zs, units, PAIR)
    columns = columns.transpose(2, 3, 0, 1, 4).reshape(zs, 3 * units, own_rows, PAIR)
    columns = jnp.concatenate(
        [columns, jnp.broadcast_to(extra[None, None], (zs, 1, own_rows, PAIR))], axis=1
    )
    blocks = 3 * units + 1
    columns = jnp.broadcast_to(
        columns.reshape(zs, 1, blocks * own_rows, PAIR), (zs, batch, blocks * own_rows, PAIR)
    )
    firsts = first_values.reshape(batch, local_len, zs, units, PAIR).transpose(2, 0, 3, 1, 4)
    firsts = firsts.reshape(zs, batch, units * local_len, PAIR)
    parcel = jnp.concatenate([columns, firsts], axis=2).reshape(seqs, -1, PAIR)

    hidden_parts = -(-own_down // own_rows)
    padded = hidden_parts * own_rows - own_down

    def pack_columns(weight):
        weight = jnp.pad(weight.reshape(own_rows, -1, own_down), ((0, 0), (0, 0), (0, padded)))
        weight = weight.reshape(own_rows, -1, hidden_parts, own_rows)
        return weight.transpose(0, 2, 1, 3).reshape(own_rows, hidden_parts * width)

    down_rows = jnp.pad(w_down, ((0, padded), (0, 0))).reshape(hidden_parts, own_rows, width)
    down_rows = down_rows.transpose(1, 0, 2).reshape(own_rows, hidden_parts * width)
    def along_z(rows):
        pieces = [rows] + [swap(rows, "z", k) for k in range(1, zs)]
        return jnp.stack(arrange(pieces, lax.axis_index("z")), axis=0)

    def across(rows):
        rows = lax.all_gather(rows, ("y", "x", "c"), axis=0)
        if own_rows % 16:
            rows = rows.transpose(1, 0, 2, 3).reshape(1, width // BLOCK, BLOCK, rows.shape[3])
        return rows

    x_own, x_sent = pick(inputs, mine, 0), pick(inputs, 1 - mine, 0)
    x_sent = swap(x_sent, "y", 1)
    gate_out = along_z(jnp.concatenate([pack_columns(w_gate), w_output], axis=1))
    rest = jnp.concatenate([pack_columns(w_up), down_rows], axis=1)
    gate_out, rest, parcel, x_sent = together(gate_out, rest, parcel, x_sent)
    gate_out = across(gate_out)
    rest = along_z(rest)
    rest, x_own, x_sent, parcel = together(rest, x_own, x_sent, parcel)
    rest = across(rest)
    parcel = lax.all_to_all(parcel, SEQ, split_axis=0, concat_axis=0, tiled=True)
    x_all = along_z(jnp.stack(arrange([x_own, x_sent], mine), axis=0)).reshape(seqs, local_len, width)
    x_all, attn_rows = together(x_all, jnp.concatenate([w_query, w_key, w_value], axis=1))
    attn_w = along_z(attn_rows)

    first_all = parcel[:, blocks * own_rows :].reshape(seqs, units, local_len, PAIR)
    head_w = parcel[:, : blocks * own_rows].reshape(seqs, blocks, own_rows, PAIR).transpose(1, 0, 2, 3)
    for at, name in ((2, "x"), (3, "c")):
        pieces = [head_w] + [swap(head_w, name, k) for k in range(1, lax.axis_size(name))]
        head_w = jnp.stack(arrange(pieces, lax.axis_index(name)), axis=at)
    head_w = head_w.reshape(blocks, width, PAIR)
    extra_all = head_w[blocks - 1].astype(F32).T
    gain_a = extra_all[0:1, :]
    gain_m = extra_all[1:2, :]
    valid_total = jnp.sum(extra_all[2] * 256.0 + extra_all[3]) / own_rows

    cos_all, sin_all = rotary_tables(jnp.arange(length, dtype=jnp.int32))
    pick_native = picker(stage_rows(width, STAGES_NATIVE, ("c", "z")), width)
    pick_down = picker(stage_rows(width, STAGES_NATIVE), width)
    pick_output = picker(stage_rows(width, STAGES_OUTPUT), width)
    pick_heads = picker(stage_rows(width, STAGES_HEADS, ("c", "x", "y")), width)

    normed_all, qkv, attended, totals = front(x_all, first_all, gain_a, cos_all, sin_all, head_w)

    def exchange(array):
        return lax.all_to_all(array, SEQ, split_axis=0, concat_axis=0, tiled=True)

    att_heads = exchange(attended).reshape(zs, batch, units, local_len, PAIR)
    att_heads, attn_w = together(att_heads, attn_w)
    attn_w = across(attn_w)
    x_low = inputs.reshape(tokens, width)
    rate = jnp.full((1, PAIR), 2.0 / width, F32) / valid_total
    (
        att_low, normed_mlp, activated, result, grad_down_in, grads, loss_row, grad_hidden, grad_branch, grad_heads,
    ) = mlp(
        x_low,
        att_heads,
        gain_m,
        teacher_states.reshape(tokens, width),
        out_cotangent.reshape(tokens, width),
        valid_float.reshape(tokens, 1),
        rate,
        gate_out,
        rest,
    )

    half = width // 2
    def down_half(rows):
        turned = [
            dot_t(pick_down[rows], activated[:, p * width : (p + 1) * width]).astype(BF16).reshape(-1, own_rows, tokens)
            for p in range(hidden_parts)
        ]
        return dot(jnp.stack(turned, axis=1).reshape(hidden_parts * half, tokens), grad_down_in)

    down_first = down_half(slice(half, None)).astype(BF16)
    turned_mlp = dot_t(pick_native, normed_mlp).astype(BF16)
    turned_att = dot_t(pick_output, att_low).astype(BF16)
    out_first = dot(turned_att[half:], grad_branch).astype(BF16)
    mlp_first = dot(turned_mlp[half:], grads).astype(BF16)
    turned_kept, down_first, out_first = together(turned_mlp[:half], down_first, out_first)
    down_sum = (down_half(slice(half)) + swap(down_first, "c", 1).astype(F32)).astype(BF16)

    def over_yx(value):
        value = value.reshape(2 * lax.axis_size("x"), -1, value.shape[1])
        value = lax.psum_scatter(value, ("y", "x"), scatter_dimension=0, tiled=True)
        return lax.optimization_barrier(value)[0]

    xs = lax.axis_size("x")
    down_sum = down_sum.reshape(2, xs, -1, width)

    def add_axis(value, name, axis):
        size = value.shape[axis]
        received = [swap(lax.index_in_dim(value, k, axis, False), name, k) for k in range(1, size)]
        value = lax.index_in_dim(value, 0, axis, False).astype(F32)
        for piece in received:
            value = value + piece.astype(F32)
        return value.astype(BF16)

    down_left = add_axis(down_sum[:, :, :, :half], "y", 0)
    down_right = add_axis(down_sum[:, :, :, half:], "x", 1)
    grad_heads = exchange(grad_heads.reshape(seqs, units, local_len, PAIR))
    down_sum = jnp.concatenate([add_axis(down_left, "x", 0), add_axis(down_right, "y", 0)], axis=1)
    mlp_sent = swap(mlp_first, "c", 1)
    mlp_sum = (dot(turned_kept, grads) + mlp_sent.astype(F32)).astype(BF16)

    out_sent = swap(out_first, "c", 1)
    out_sum = (dot(turned_att[:half], grad_branch) + out_sent.astype(F32)).astype(BF16)

    out_sum = add_stage(out_sum, "z").astype(BF16)
    grad_heads, attn_w, *_ = together(grad_heads, attn_w, mlp_sum, out_sum, down_sum)
    mlp_sum = over_yx(mlp_sum)

    grad_qkv = attend_backward(qkv, grad_heads, totals, cos_all, sin_all)
    grad_own = exchange(grad_qkv).reshape(zs, batch, 3, units, local_len, PAIR)

    value = head_grads(normed_all, grad_qkv, loss_row, pick_heads)
    for name in ("c", "x", "y"):
        value = add_stage(value, name)
    owned_down = add_stage(down_sum, "z")[:own_down]
    value, grad_own, owned_down, out_sum, mlp_sum = together(value, grad_own, owned_down, out_sum, mlp_sum)
    value = value.astype(BF16)
    out_sum = add_stage(add_stage(out_sum, "y"), "x")
    owned_output = out_sum
    value = value.reshape(zs, own_rows, value.shape[1])
    value = lax.all_to_all(value, "z", split_axis=0, concat_axis=0, tiled=True)
    columns = 3 * units * PAIR
    loss_value = jnp.sum(value[:, 0, columns:].astype(F32)) / valid_total
    value = value[:, :, :columns].reshape(zs, own_rows, units, 3, PAIR).astype(F32)
    owned_qkv = value.transpose(3, 1, 0, 2, 4).reshape(3, own_rows, width)

    mlp_sum = mlp_sum.reshape(zs, own_rows, -1)
    mlp_sum = [mlp_sum[0]] + [swap(mlp_sum[k], "z", k) for k in range(1, zs)]
    grad_in, grad_first = last(grad_own, x_low, gain_a, attn_w, grad_hidden)

    gain_grad_a = (
        jnp.sum(w_query.astype(F32) * owned_qkv[0], axis=1)
        + jnp.sum(w_key.astype(F32) * owned_qkv[1], axis=1)
        + jnp.sum(w_value.astype(F32) * owned_qkv[2], axis=1)
    ) / attn_gain.astype(F32)
    owned_gate, owned_up, gain_grad_m = finish(mlp_sum, w_gate, w_up, own_down)
    gain_grad_m = gain_grad_m / mlp_gain.astype(F32)
    return (
        result.reshape(batch, local_len, width),
        loss_value,
        grad_in.reshape(batch, local_len, width),
        grad_first.reshape(batch, local_len, width),
        gain_grad_a,
        owned_qkv[0],
        owned_qkv[1],
        owned_qkv[2],
        owned_output,
        gain_grad_m,
        owned_gate,
        owned_up,
        owned_down,
    )


def solution(mesh):
    seqs, dps = mesh.devices.shape
    fine = Mesh(mesh.devices.reshape(seqs // 2, 2, dps // 2, 2), ALL)
    tokens = P(("x", "c"), SEQ, None)
    rows = P(ALL, None)
    gain = P(ALL)
    return jax.shard_map(
        on_device,
        mesh=fine,
        in_specs=(
            tokens, tokens, tokens, tokens, P(("x", "c"), SEQ), gain, rows, rows, rows, rows, gain, rows, rows, rows,
        ),
        out_specs=(
            tokens, P(), tokens, tokens, gain, rows, rows, rows, rows, gain, rows, rows, rows,
        ),
        check_vma=False,
    )
```

```python
import functools

import jax
import jax.numpy as jnp
from jax import lax
from jax.experimental import pallas as pl
from jax.experimental.pallas import tpu as pltpu
from jax.sharding import Mesh
from jax.sharding import PartitionSpec as P

HEAD_DIM = 64
BLOCK = 256
MLP_STEP = 512
PAIR = 2 * HEAD_DIM

EPSILON = 1e-06
THETA = 10000.0
SCALE = 0.125
ALL = ("z", "y", "x", "c")
SEQ = ("z", "y")
F32 = jnp.float32
BF16 = jnp.bfloat16


def rotary_tables(positions):
    lane = jnp.arange(PAIR, dtype=jnp.int32)
    half = HEAD_DIM // 2
    index = (lane % half).astype(F32)
    frequency = THETA ** (-(index * 2.0 / HEAD_DIM))
    angles = positions.astype(F32)[:, None] * frequency[None, :]
    sign = jnp.where(lane % HEAD_DIM < half, -1.0, 1.0)[None, :]
    return jnp.cos(angles), jnp.sin(angles) * sign


def partner(values):
    half = HEAD_DIM // 2
    lane = lax.broadcasted_iota(jnp.int32, values.shape, values.ndim - 1)
    first = lane % HEAD_DIM < half
    width = values.shape[-1]
    return jnp.where(
        first,
        pltpu.roll(values, width - half, values.ndim - 1),
        pltpu.roll(values, half, values.ndim - 1),
    )


def dot_t(left, right):
    return lax.dot_general(left, right, (((1,), (1,)), ((), ())), preferred_element_type=F32)


def t_dot(left, right):
    return lax.dot_general(left, right, (((0,), (0,)), ((), ())), preferred_element_type=F32)


def dot(left, right):
    return jnp.dot(left, right, preferred_element_type=F32)


def attend_forward_kernel(qkv_ref, out_ref, total_ref):
    parts, _, _, rows, _ = qkv_ref.shape
    per_block = BLOCK // rows
    blocks = parts // per_block
    for head in range(2):
        lanes = pl.ds(head * HEAD_DIM, HEAD_DIM)
        for block in range(blocks):
            lo, hi = block * per_block, (block + 1) * per_block
            query = qkv_ref[lo:hi, 0, 0, :, lanes].reshape(BLOCK, HEAD_DIM)
            keys = qkv_ref[0:hi, 1, 0, :, lanes].reshape(hi * rows, HEAD_DIM)
            values = qkv_ref[0:hi, 2, 0, :, lanes].reshape(hi * rows, HEAD_DIM)
            scores = dot_t(keys, query * SCALE)
            top = jnp.max(scores, axis=0, keepdims=True)
            weights = jnp.exp(scores - top)
            total = jnp.sum(weights, axis=0, keepdims=True)
            probs = (weights * (1.0 / total)).astype(BF16)
            mixed = t_dot(values, probs)
            out_ref[lo:hi, 0, :, lanes] = mixed.T.astype(BF16).reshape(per_block, rows, HEAD_DIM)
            total_ref[0, head, block : block + 1, :] = top + jnp.log(total)


def attend_backward_kernel(qkv_ref, grad_ref, total_ref, cos_ref, sin_ref, out_ref, dk_acc, dv_acc):
    parts, _, _, rows, _ = qkv_ref.shape
    per_block = BLOCK // rows
    blocks = parts // per_block
    dk_acc[...] = jnp.zeros_like(dk_acc)
    dv_acc[...] = jnp.zeros_like(dv_acc)
    for block in range(blocks):
        lo, hi = block * per_block, (block + 1) * per_block
        keys_n = hi * rows
        dq_parts = []
        for head in range(2):
            lanes = pl.ds(head * HEAD_DIM, HEAD_DIM)
            query = qkv_ref[lo:hi, 0, 0, :, lanes].reshape(BLOCK, HEAD_DIM)
            grad = grad_ref[lo:hi, 0, :, lanes].reshape(BLOCK, HEAD_DIM)
            keys = qkv_ref[0:hi, 1, 0, :, lanes].reshape(keys_n, HEAD_DIM)
            values = qkv_ref[0:hi, 2, 0, :, lanes].reshape(keys_n, HEAD_DIM)
            scores = dot_t(keys, query * SCALE)
            probs = jnp.exp(scores - total_ref[0, head, block : block + 1, :])
            grad_probs = dot_t(values, grad)
            inner = jnp.sum(probs * grad_probs, axis=0, keepdims=True)
            grad_scores = (probs * (grad_probs - inner)).astype(BF16)
            dk_acc[0:keys_n, lanes] += dot(grad_scores, query) * SCALE
            dv_acc[0:keys_n, lanes] += dot(probs.astype(BF16), grad)
            dq_parts.append(t_dot(keys, grad_scores).T * SCALE)
        dq = jnp.concatenate(dq_parts, axis=1)
        cos = cos_ref[block * BLOCK : (block + 1) * BLOCK, :]
        sin = sin_ref[block * BLOCK : (block + 1) * BLOCK, :]
        dq = (dq * cos - partner(dq) * sin).astype(BF16)
        out_ref[lo:hi, 0, 0, :, :] = dq.reshape(per_block, rows, PAIR)
    dk = dk_acc[...]
    dk = (dk * cos_ref[...] - partner(dk) * sin_ref[...]).astype(BF16)
    out_ref[:, 1, 0, :, :] = dk.reshape(parts, rows, PAIR)
    out_ref[:, 2, 0, :, :] = dv_acc[...].astype(BF16).reshape(parts, rows, PAIR)


VMEM_LIMIT = 60 * 1024 * 1024


def attend_backward(qkv, grad_att, totals, cos, sin):
    parts, _, units, rows, _ = qkv.shape
    length = parts * rows
    blocks = length // BLOCK
    return pl.pallas_call(
        attend_backward_kernel,
        grid=(units,),
        in_specs=[
            pl.BlockSpec((parts, 3, 1, rows, PAIR), lambda u: (0, 0, u, 0, 0)),
            pl.BlockSpec((parts, 1, rows, PAIR), lambda u: (0, u, 0, 0)),
            pl.BlockSpec((1, 2, blocks, BLOCK), lambda u: (u, 0, 0, 0)),
            pl.BlockSpec((length, PAIR), lambda u: (0, 0)),
            pl.BlockSpec((length, PAIR), lambda u: (0, 0)),
        ],
        out_specs=pl.BlockSpec((parts, 3, 1, rows, PAIR), lambda u: (0, 0, u, 0, 0)),
        out_shape=jax.ShapeDtypeStruct((parts, 3, units, rows, PAIR), BF16),
        scratch_shapes=[pltpu.VMEM((length, PAIR), F32), pltpu.VMEM((length, PAIR), F32)],
        compiler_params=pltpu.CompilerParams(vmem_limit_bytes=VMEM_LIMIT),
        name="attend_backward",
        cost_estimate=cost(units * length * length, 22),
    )(qkv, grad_att, totals, cos, sin)


def swap(array, name, distance):
    size = lax.axis_size(name)
    return lax.ppermute(array, name, [(i, i ^ distance) for i in range(size)])


def pick(array, index, axis):
    return lax.dynamic_index_in_dim(array, index, axis, keepdims=False)


def arrange(pieces, at):
    bit = 1
    while bit < len(pieces):
        odd = (at & bit) != 0
        pieces = [jnp.where(odd, pieces[j ^ bit], pieces[j]) for j in range(len(pieces))]
        bit *= 2
    return pieces


def stage_rows(rows, order, relative=ALL):
    sizes = [lax.axis_size(name) for name in order]
    per = rows // functools.reduce(lambda a, b: a * b, sizes)
    index = lax.broadcasted_iota(jnp.int32, (rows, 1), 0)
    left, inner = index // per, index % per
    place = {}
    for name, size in zip(reversed(order), reversed(sizes)):
        place[name] = left % size
        if name in relative:
            place[name] = place[name] ^ lax.axis_index(name)
        left = left // size
    device = jnp.zeros_like(index)
    for name in ALL:
        device = device * lax.axis_size(name) + place[name]
    return device * per + inner


def add_stage(value, name):
    size = lax.axis_size(name)
    value = value.astype(BF16).reshape(size, -1, value.shape[1])
    received = [swap(value[k], name, k) for k in range(1, size)]
    value = value[0].astype(F32)
    for piece in received:
        value = value + piece.astype(F32)
    return value


def together(*values):
    return lax.optimization_barrier(values)


def cost(size, factor):
    return pl.CostEstimate(flops=0, bytes_accessed=int(size * factor), transcendentals=0)


def params():
    return pltpu.CompilerParams(vmem_limit_bytes=VMEM_LIMIT)


def front_kernel(
    x_ref, first_ref, gain_ref, cos_ref, sin_ref, weight_ref, normed_out, qkv_out, att_ref, total_ref, weights, normed_ref,
    qkv_ref, left,
):
    parts, rows, width = x_ref.shape
    units = first_ref.shape[1]
    per_block = BLOCK // rows
    blocks = parts // per_block
    gain = gain_ref[...]
    for kind in range(3):
        for unit in range(units):
            at = (kind * units + unit) * PAIR
            weights[:, at : at + PAIR] = weight_ref[3 * unit + kind]
    wide = units * PAIR
    for block in range(blocks):
        lo, hi = block * per_block, (block + 1) * per_block
        x = x_ref[lo:hi].reshape(BLOCK, width).astype(F32)
        inv = lax.rsqrt(jnp.mean(x * x, axis=-1, keepdims=True) + EPSILON)
        normed = (x * inv * gain).astype(BF16)
        normed_ref[lo:hi] = normed.reshape(per_block, rows, width)
        values = dot(normed, weights[...])
        cos = jnp.concatenate([cos_ref[block * BLOCK : (block + 1) * BLOCK, :]] * (2 * units), axis=1)
        sin = jnp.concatenate([sin_ref[block * BLOCK : (block + 1) * BLOCK, :]] * (2 * units), axis=1)
        turning = values[:, : 2 * wide]
        turned = (turning * cos + partner(turning) * sin).astype(BF16)
        for unit in range(units):
            lanes = slice(unit * PAIR, (unit + 1) * PAIR)
            qkv_ref[lo:hi, 0, unit] = turned[:, :wide][:, lanes].reshape(per_block, rows, PAIR)
            qkv_ref[lo:hi, 1, unit] = turned[:, wide:][:, lanes].reshape(per_block, rows, PAIR)
            first = first_ref[lo:hi, unit].reshape(BLOCK, PAIR).astype(F32)
            mixed = (0.5 * values[:, 2 * wide :][:, lanes] + 0.5 * first).astype(BF16)
            qkv_ref[lo:hi, 2, unit] = mixed.reshape(per_block, rows, PAIR)
    sent = [
        pltpu.make_async_copy(normed_ref, normed_out, left.at[0]),
        pltpu.make_async_copy(qkv_ref, qkv_out, left.at[1]),
    ]
    for copy in sent:
        copy.start()
    for unit in range(units):
        one = pl.ds(unit, 1)
        attend_forward_kernel(qkv_ref.at[:, :, one], att_ref.at[:, one], total_ref.at[one])
    for copy in sent:
        copy.wait()


def front(x, first, gain, cos, sin, weights):
    parts, rows, width = x.shape
    units = first.shape[1]
    length = parts * rows
    blocks = length // BLOCK
    outside = pl.BlockSpec(memory_space=pl.ANY)
    normed = (parts, rows, width)
    qkv = (parts, 3, units, rows, PAIR)
    return pl.pallas_call(
        front_kernel,
        grid=(1,),
        in_specs=[
            still(*normed), still(*first.shape), still(1, width), still(length, PAIR), still(length, PAIR), still(*weights.shape),
        ],
        out_specs=[outside, outside, still(*first.shape), still(units, 2, blocks, BLOCK)],
        out_shape=[
            jax.ShapeDtypeStruct(normed, BF16),
            jax.ShapeDtypeStruct(qkv, BF16),
            jax.ShapeDtypeStruct(first.shape, BF16),
            jax.ShapeDtypeStruct((units, 2, blocks, BLOCK), F32),
        ],
        scratch_shapes=[
            pltpu.VMEM((width, 3 * units * PAIR), BF16),
            pltpu.VMEM(normed, BF16),
            pltpu.VMEM(qkv, BF16),
            pltpu.SemaphoreType.DMA((2,)),
        ],
        compiler_params=params(),
        name="front",
        cost_estimate=cost(units * length * length, 27),
    )(x, first, gain, cos, sin, weights)


def sections(weight_ref):
    outer, parts, rows, columns = weight_ref.shape
    return [weight_ref[:, part].reshape(outer * rows, columns) for part in range(parts)]


def dot_sections(left, weight_ref):
    parts = sections(weight_ref)
    wide = left.shape[1] // len(parts)
    total = dot(left[:, :wide], parts[0])
    for at in range(1, len(parts)):
        total = total + dot(left[:, at * wide : (at + 1) * wide], parts[at])
    return total


def dot_t_sections(left, weight_ref):
    return jnp.concatenate([dot_t(left, part) for part in sections(weight_ref)], axis=1)


def mlp_kernel(
    x_ref, heads_ref, gain_ref, teacher_ref, cotangent_ref, valid_ref, rate_ref, gate_out, up_down,
    att_out, normed_out, act_out, result_out, grad_low_out, grads_out, loss_ref, grad_hidden_ref, branch_ref, out_heads_ref,
    wo, wg, wu, wd, gates, ups, hidden_ref, total, att_ref, normed_ref, act_ref, result_ref, grad_low_ref, grads_ref,
    arrived, left,
):
    tokens, width = x_ref.shape
    steps, _, sides, _, wide = wg.shape
    parts = steps * wide // width
    per = width // wide
    deep = sides // per

    def output_copy():
        return pltpu.make_async_copy(
            gate_out.at[:, :, :, pl.ds(parts * width, width)], wo, arrived.at[3 * steps]
        )

    def copies(step):
        lanes = pl.ds(step * wide, wide)
        rows = pl.ds(step % per * deep, deep)
        across = pl.ds((parts + step // per) * width, width)
        return (
            pltpu.make_async_copy(gate_out.at[:, :, :, lanes], wg.at[step], arrived.at[3 * step]),
            pltpu.make_async_copy(up_down.at[:, :, :, lanes], wu.at[step], arrived.at[3 * step + 1]),
            pltpu.make_async_copy(up_down.at[:, rows, :, across], wd.at[step], arrived.at[3 * step + 2]),
        )

    sent = [
        pltpu.make_async_copy(source, target, left.at[at])
        for at, (source, target) in enumerate(
            (
                (att_ref, att_out),
                (normed_ref, normed_out),
                (act_ref, act_out),
                (result_ref, result_out),
                (grad_low_ref, grad_low_out),
            )
        )
    ]
    sent += [
        pltpu.make_async_copy(
            grads_ref.at[step], grads_out.at[:, pl.ds(2 * step * wide, 2 * wide)], left.at[5 + step]
        )
        for step in range(steps)
    ]

    output_copy().start()
    for step in range(steps):
        for copy in copies(step):
            copy.start()

    for pair in range(width // PAIR):
        at, unit = divmod(pair, heads_ref.shape[2])
        att_ref[:, pair * PAIR : (pair + 1) * PAIR] = heads_ref[at, :, unit].reshape(tokens, PAIR)
    output_copy().wait()
    hidden = x_ref[...].astype(F32) + dot_sections(att_ref[...], wo)
    inv = lax.rsqrt(jnp.mean(hidden * hidden, axis=-1, keepdims=True) + EPSILON)
    hidden_ref[...] = hidden
    result_ref[...] = hidden
    normed_ref[...] = (hidden * inv * gain_ref[...]).astype(BF16)
    sent[0].start()
    sent[1].start()

    for step in range(steps):
        for copy in copies(step):
            copy.wait()
        gate = dot_sections(normed_ref[...], wg.at[step])
        up = dot_sections(normed_ref[...], wu.at[step])
        act = (gate * jax.nn.sigmoid(gate) * up).astype(BF16)
        gates[step] = gate
        ups[step] = up
        act_ref[:, step * wide : (step + 1) * wide] = act
        result_ref[...] += dot_sections(act, wd.at[step])

    sent[2].start()
    sent[3].start()
    error = result_ref[...] - teacher_ref[...].astype(F32)
    valid = valid_ref[...]
    grad = cotangent_ref[...].astype(F32) + rate_ref[0:1, 0:1] * valid * error
    grad_hidden_ref[...] = grad
    grad_low_ref[...] = grad.astype(BF16)
    sent[4].start()
    losses = jnp.sum(error * error * (valid / width), axis=0, keepdims=True)
    loss = losses[:, :PAIR]
    for at in range(PAIR, width, PAIR):
        loss = loss + losses[:, at : at + PAIR]
    loss_ref[...] = loss
    total[...] = jnp.zeros_like(total)

    for step in range(steps):
        gate = gates[step]
        up = ups[step]
        sigmoid = jax.nn.sigmoid(gate)
        grad_act = dot_t_sections(grad_low_ref[...], wd.at[step])
        grad_gate = (grad_act * up * (sigmoid * (1.0 + gate * (1.0 - sigmoid)))).astype(BF16)
        grad_up = (grad_act * (gate * sigmoid)).astype(BF16)
        grads_ref[step, :, :wide] = grad_gate
        grads_ref[step, :, wide:] = grad_up
        sent[5 + step].start()
        total[...] += dot_t_sections(grad_gate, wg.at[step]) + dot_t_sections(grad_up, wu.at[step])

    hidden = hidden_ref[...]
    inv = lax.rsqrt(jnp.mean(hidden * hidden, axis=-1, keepdims=True) + EPSILON)
    scaled = hidden * inv
    scaled_grad = total[...] * gain_ref[...]
    grad = grad_hidden_ref[...] + inv * (
        scaled_grad - scaled * jnp.mean(scaled_grad * scaled, axis=-1, keepdims=True)
    )
    grad_hidden_ref[...] = grad
    branch = grad.astype(BF16)
    branch_ref[...] = branch
    value = dot_t_sections(branch, wo).astype(BF16)
    _, batch, units, rows, _ = out_heads_ref.shape
    for pair in range(width // PAIR):
        at, unit = divmod(pair, units)
        out_heads_ref[at, :, unit] = value[:, pair * PAIR : (pair + 1) * PAIR].reshape(batch, rows, PAIR)
    for copy in sent:
        copy.wait()


def still(*shape):
    return pl.BlockSpec(shape, lambda j: (0,) * len(shape))


def mlp(x, heads, gain, teacher, cotangent, valid, rate, gate_out, up_down):
    tokens, width = x.shape
    outer, sides, rows, _ = gate_out.shape
    parts = gate_out.shape[3] // width - 1
    wide = MLP_STEP
    steps = parts * width // wide
    deep = sides * wide // width
    whole = still(tokens, width)
    outside = pl.BlockSpec(memory_space=pl.ANY)
    low = jax.ShapeDtypeStruct((tokens, width), BF16)
    full = jax.ShapeDtypeStruct((tokens, width), F32)
    hidden = (tokens, parts * width)
    grads = (tokens, 2 * parts * width)
    return pl.pallas_call(
        mlp_kernel,
        grid=(1,),
        in_specs=[whole, still(*heads.shape), still(1, width), whole, whole, still(tokens, 1), still(1, PAIR)]
        + [outside, outside],
        out_specs=[outside] * 6 + [still(1, PAIR), whole, whole, still(*heads.shape)],
        out_shape=[
            low,
            low,
            jax.ShapeDtypeStruct(hidden, BF16),
            full,
            low,
            jax.ShapeDtypeStruct(grads, BF16),
            jax.ShapeDtypeStruct((1, PAIR), F32),
            full,
            low,
            jax.ShapeDtypeStruct(heads.shape, BF16),
        ],
        scratch_shapes=[
            pltpu.VMEM((outer, sides, rows, width), BF16),
            pltpu.VMEM((steps, outer, sides, rows, wide), BF16),
            pltpu.VMEM((steps, outer, sides, rows, wide), BF16),
            pltpu.VMEM((steps, outer, deep, rows, width), BF16),
            pltpu.VMEM((steps, tokens, wide), F32),
            pltpu.VMEM((steps, tokens, wide), F32),
            pltpu.VMEM((tokens, width), F32),
            pltpu.VMEM((tokens, width), F32),
            pltpu.VMEM((tokens, width), BF16),
            pltpu.VMEM((tokens, width), BF16),
            pltpu.VMEM(hidden, BF16),
            pltpu.VMEM((tokens, width), F32),
            pltpu.VMEM((tokens, width), BF16),
            pltpu.VMEM((steps, tokens, 2 * wide), BF16),
            pltpu.SemaphoreType.DMA((3 * steps + 1,)),
            pltpu.SemaphoreType.DMA((5 + steps,)),
        ],
        compiler_params=params(),
        name="mlp",
        cost_estimate=cost(tokens * width * parts, 80),
    )(x, heads, gain, teacher, cotangent, valid, rate, gate_out, up_down)


def picker(place, width):
    lane = lax.broadcasted_iota(jnp.int32, (place.shape[0], width), 1)
    return jnp.where(lane == place, 1.0, 0.0).astype(BF16)


def head_grads_kernel(normed_ref, grads_ref, loss_ref, pick_ref, out_ref, turned):
    parts, kinds, units, rows, _ = grads_ref.shape
    width = normed_ref.shape[2]
    normed = normed_ref[...].reshape(parts * rows, width)
    for unit in range(units):
        for kind in range(kinds):
            value = t_dot(grads_ref[:, kind, unit].reshape(parts * rows, PAIR), normed)
            if kind == 2:
                value = 0.5 * value
            at = (unit * kinds + kind) * PAIR
            turned[at : at + PAIR, :] = value.astype(BF16)
    columns = turned.shape[0]
    out_ref[:, :columns] = dot_t(pick_ref[...], turned[...]).astype(BF16)
    out_ref[:, columns:] = jnp.broadcast_to(loss_ref[...], (width, PAIR)).astype(BF16)


def head_grads(normed, grads, loss_row, pick):
    width = normed.shape[2]
    columns = 3 * grads.shape[2] * PAIR
    return pl.pallas_call(
        head_grads_kernel,
        out_shape=jax.ShapeDtypeStruct((width, columns + PAIR), BF16),
        scratch_shapes=[pltpu.VMEM((columns, width), BF16)],
        compiler_params=params(),
        name="head_grads",
        cost_estimate=cost(normed.size, 24),
    )(normed, grads, loss_row, pick)


def last_kernel(heads_ref, x_ref, gain_ref, weight_ref, grad_hidden_ref, grad_in_ref, first_ref, grads):
    tokens, width = x_ref.shape
    for kind in range(3):
        for pair in range(width // PAIR):
            at = kind * width + pair * PAIR
            place, unit = divmod(pair, heads_ref.shape[3])
            piece = heads_ref[place, :, kind, unit].reshape(tokens, PAIR)
            if kind == 2:
                half = 0.5 * piece.astype(F32)
                first_ref[:, pair * PAIR : (pair + 1) * PAIR] = half
                piece = half.astype(BF16)
            grads[:, at : at + PAIR] = piece
    grad_norm = dot_t_sections(grads[...], weight_ref)
    x = x_ref[...].astype(F32)
    inv = lax.rsqrt(jnp.mean(x * x, axis=-1, keepdims=True) + EPSILON)
    scaled = x * inv
    scaled_grad = grad_norm * gain_ref[...]
    grad_in_ref[...] = grad_hidden_ref[...] + inv * (
        scaled_grad - scaled * jnp.mean(scaled_grad * scaled, axis=-1, keepdims=True)
    )


def last(heads, x, gain, weights, grad_hidden):
    tokens, width = x.shape
    return pl.pallas_call(
        last_kernel,
        grid=(1,),
        in_specs=[
            still(*heads.shape),
            still(tokens, width),
            still(1, width),
            pl.BlockSpec(weights.shape[:3] + (3 * width,), lambda j: (0, 0, 0, 0)),
            still(tokens, width),
        ],
        out_specs=[still(tokens, width), still(tokens, width)],
        out_shape=[
            jax.ShapeDtypeStruct((tokens, width), F32),
            jax.ShapeDtypeStruct((tokens, width), F32),
        ],
        scratch_shapes=[pltpu.VMEM((tokens, 3 * width), BF16)],
        compiler_params=params(),
        name="last",
        cost_estimate=cost(tokens * width, 84),
    )(heads, x, gain, weights, grad_hidden)


def finish_kernel(*refs, own_down):
    pieces, (gate_w_ref, up_w_ref), (gate_ref, up_ref, gain_ref) = refs[:-5], refs[-5:-3], refs[-3:]
    rows, columns = pieces[0].shape
    total = pieces[0][...].astype(F32)
    for piece in pieces[1:]:
        total = total + piece[...].astype(F32)
    parts = -(-own_down // rows)
    width = columns // (2 * parts)
    gain = jnp.zeros((rows, 1), F32)
    for side, (weight_ref, out_ref) in enumerate(((gate_w_ref, gate_ref), (up_w_ref, up_ref))):
        values = []
        for device in range(width // rows):
            for part in range(parts):
                step, lane = divmod(part * width + device * rows, MLP_STEP)
                at = (2 * step + side) * MLP_STEP + lane
                values.append(total[:, at : at + min(rows, own_down - part * rows)])
        value = jnp.concatenate(values, axis=1)
        out_ref[...] = value
        gain = gain + jnp.sum(value * weight_ref[...].astype(F32), axis=1, keepdims=True)
    gain_ref[...] = jnp.broadcast_to(gain, gain_ref.shape)


def finish(pieces, w_gate, w_up, own_down):
    rows, hidden = w_gate.shape
    if rows % 8 == 0:
        gate, up, gain = pl.pallas_call(
            functools.partial(finish_kernel, own_down=own_down),
            out_shape=[
                jax.ShapeDtypeStruct((rows, hidden), F32),
                jax.ShapeDtypeStruct((rows, hidden), F32),
                jax.ShapeDtypeStruct((rows, PAIR), F32),
            ],
            compiler_params=params(),
            name="finish",
        )(*pieces, w_gate, w_up)
        return gate, up, gain[:, 0]
    total = sum(piece.astype(F32) for piece in pieces).reshape(rows, -1, 2, MLP_STEP)
    parts = -(-own_down // rows)

    def unpack(grad):
        grad = grad.reshape(rows, parts, -1, rows).transpose(0, 2, 1, 3)
        return grad.reshape(rows, -1, parts * rows)[:, :, :own_down].reshape(rows, hidden)

    gate, up = unpack(total[:, :, 0]), unpack(total[:, :, 1])
    return gate, up, jnp.sum(gate * w_gate.astype(F32) + up * w_up.astype(F32), axis=1)


STAGES_NATIVE = ("c", "y", "x", "z")
STAGES_OUTPUT = ("c", "z", "y", "x")
STAGES_HEADS = ("c", "x", "y", "z")


def on_device(
    inputs,
    first_values,
    teacher_states,
    out_cotangent,
    token_valid,
    attn_gain,
    w_query,
    w_key,
    w_value,
    w_output,
    mlp_gain,
    w_gate,
    w_up,
    w_down,
):
    batch, local_len, width = inputs.shape
    seqs = lax.axis_size(SEQ)
    tokens = batch * local_len
    length = local_len * seqs
    pairs = width // PAIR
    own_rows = w_query.shape[0]
    own_down = w_down.shape[0]
    zs = lax.axis_size("z")
    units = pairs // zs
    mine = lax.axis_index("y")

    valid_float = token_valid.astype(F32)
    count = jnp.sum(token_valid)
    extra = jnp.stack(
        [
            attn_gain,
            mlp_gain,
            jnp.full((own_rows,), count // 256, jnp.int32).astype(BF16),
            jnp.full((own_rows,), count % 256, jnp.int32).astype(BF16),
        ],
        axis=1,
    )
    extra = jnp.pad(extra, ((0, 0), (0, PAIR - 4)))
    columns = jnp.stack([w_query, w_key, w_value]).reshape(3, own_rows, zs, units, PAIR)
    columns = columns.transpose(2, 3, 0, 1, 4).reshape(zs, 3 * units, own_rows, PAIR)
    columns = jnp.concatenate(
        [columns, jnp.broadcast_to(extra[None, None], (zs, 1, own_rows, PAIR))], axis=1
    )
    blocks = 3 * units + 1
    columns = jnp.broadcast_to(
        columns.reshape(zs, 1, blocks * own_rows, PAIR), (zs, batch, blocks * own_rows, PAIR)
    )
    firsts = first_values.reshape(batch, local_len, zs, units, PAIR).transpose(2, 0, 3, 1, 4)
    firsts = firsts.reshape(zs, batch, units * local_len, PAIR)
    parcel = jnp.concatenate([columns, firsts], axis=2).reshape(seqs, -1, PAIR)

    hidden_parts = -(-own_down // own_rows)
    padded = hidden_parts * own_rows - own_down

    def pack_columns(weight):
        weight = jnp.pad(weight.reshape(own_rows, -1, own_down), ((0, 0), (0, 0), (0, padded)))
        weight = weight.reshape(own_rows, -1, hidden_parts, own_rows)
        return weight.transpose(0, 2, 1, 3).reshape(own_rows, hidden_parts * width)

    down_rows = jnp.pad(w_down, ((0, padded), (0, 0))).reshape(hidden_parts, own_rows, width)
    down_rows = down_rows.transpose(1, 0, 2).reshape(own_rows, hidden_parts * width)
    def along_z(rows):
        pieces = [rows] + [swap(rows, "z", k) for k in range(1, zs)]
        return jnp.stack(arrange(pieces, lax.axis_index("z")), axis=0)

    def across(rows):
        rows = lax.all_gather(rows, ("y", "x", "c"), axis=0)
        if own_rows % 16:
            rows = rows.transpose(1, 0, 2, 3).reshape(1, width // BLOCK, BLOCK, rows.shape[3])
        return rows

    x_own, x_sent = pick(inputs, mine, 0), pick(inputs, 1 - mine, 0)
    x_sent = swap(x_sent, "y", 1)
    gate_out = along_z(jnp.concatenate([pack_columns(w_gate), w_output], axis=1))
    rest = jnp.concatenate([pack_columns(w_up), down_rows], axis=1)
    gate_out, rest, parcel, x_sent = together(gate_out, rest, parcel, x_sent)
    gate_out = across(gate_out)
    rest = along_z(rest)
    rest, x_own, x_sent, parcel = together(rest, x_own, x_sent, parcel)
    rest = across(rest)
    parcel = lax.all_to_all(parcel, SEQ, split_axis=0, concat_axis=0, tiled=True)
    x_all = along_z(jnp.stack(arrange([x_own, x_sent], mine), axis=0)).reshape(seqs, local_len, width)
    x_all, attn_rows = together(x_all, jnp.concatenate([w_query, w_key, w_value], axis=1))
    attn_w = along_z(attn_rows)

    first_all = parcel[:, blocks * own_rows :].reshape(seqs, units, local_len, PAIR)
    head_w = parcel[:, : blocks * own_rows].reshape(seqs, blocks, own_rows, PAIR).transpose(1, 0, 2, 3)
    for at, name in ((2, "x"), (3, "c")):
        pieces = [head_w] + [swap(head_w, name, k) for k in range(1, lax.axis_size(name))]
        head_w = jnp.stack(arrange(pieces, lax.axis_index(name)), axis=at)
    head_w = head_w.reshape(blocks, width, PAIR)
    extra_all = head_w[blocks - 1].astype(F32).T
    gain_a = extra_all[0:1, :]
    gain_m = extra_all[1:2, :]
    valid_total = jnp.sum(extra_all[2] * 256.0 + extra_all[3]) / own_rows

    cos_all, sin_all = rotary_tables(jnp.arange(length, dtype=jnp.int32))
    pick_native = picker(stage_rows(width, STAGES_NATIVE, ("c", "z")), width)
    pick_down = picker(stage_rows(width, STAGES_NATIVE), width)
    pick_output = picker(stage_rows(width, STAGES_OUTPUT), width)
    pick_heads = picker(stage_rows(width, STAGES_HEADS, ("c", "x", "y")), width)

    normed_all, qkv, attended, totals = front(x_all, first_all, gain_a, cos_all, sin_all, head_w)

    def exchange(array):
        return lax.all_to_all(array, SEQ, split_axis=0, concat_axis=0, tiled=True)

    att_heads = exchange(attended).reshape(zs, batch, units, local_len, PAIR)
    att_heads, attn_w = together(att_heads, attn_w)
    attn_w = across(attn_w)
    x_low = inputs.reshape(tokens, width)
    rate = jnp.full((1, PAIR), 2.0 / width, F32) / valid_total
    (
        att_low, normed_mlp, activated, result, grad_down_in, grads, loss_row, grad_hidden, grad_branch, grad_heads,
    ) = mlp(
        x_low,
        att_heads,
        gain_m,
        teacher_states.reshape(tokens, width),
        out_cotangent.reshape(tokens, width),
        valid_float.reshape(tokens, 1),
        rate,
        gate_out,
        rest,
    )

    half = width // 2
    def turned_down(rows):
        turned = [
            dot_t(pick_down[rows], activated[:, p * width : (p + 1) * width]).astype(BF16).reshape(-1, own_rows, tokens)
            for p in range(hidden_parts)
        ]
        return jnp.stack(turned, axis=1).reshape(hidden_parts * half, tokens)

    down_first = dot(turned_down(slice(half, None)), grad_down_in).astype(BF16)
    turned_mlp = dot_t(pick_native, normed_mlp).astype(BF16)
    turned_att = dot_t(pick_output, att_low).astype(BF16)
    out_first = dot(turned_att[half:], grad_branch).astype(BF16)
    mlp_first = dot(turned_mlp[half:], grads).astype(BF16)
    turned_kept, down_first, out_first, down_kept = together(
        turned_mlp[:half], down_first, out_first, turned_down(slice(half))
    )
    down_sum = (dot(down_kept, grad_down_in) + swap(down_first, "c", 1).astype(F32)).astype(BF16)

    def over_yx(value):
        value = value.reshape(2 * lax.axis_size("x"), -1, value.shape[1])
        value = lax.psum_scatter(value, ("y", "x"), scatter_dimension=0, tiled=True)
        return lax.optimization_barrier(value)[0]

    xs = lax.axis_size("x")
    down_sum = down_sum.reshape(2, xs, -1, width)

    def add_axis(value, name, axis):
        size = value.shape[axis]
        received = [swap(lax.index_in_dim(value, k, axis, False), name, k) for k in range(1, size)]
        value = lax.index_in_dim(value, 0, axis, False).astype(F32)
        for piece in received:
            value = value + piece.astype(F32)
        return value.astype(BF16)

    down_left = add_axis(down_sum[:, :, :, :half], "y", 0)
    down_right = add_axis(down_sum[:, :, :, half:], "x", 1)
    grad_heads = exchange(grad_heads.reshape(seqs, units, local_len, PAIR))
    down_sum = jnp.concatenate([add_axis(down_left, "x", 0), add_axis(down_right, "y", 0)], axis=1)
    mlp_sent = swap(mlp_first, "c", 1)
    mlp_sum = (dot(turned_kept, grads) + mlp_sent.astype(F32)).astype(BF16)

    out_sent = swap(out_first, "c", 1)
    out_sum = (dot(turned_att[:half], grad_branch) + out_sent.astype(F32)).astype(BF16)

    out_sum = add_stage(out_sum, "z").astype(BF16)
    grad_heads, attn_w, *_ = together(grad_heads, attn_w, mlp_sum, out_sum, down_sum)
    mlp_sum = over_yx(mlp_sum)

    grad_qkv = attend_backward(qkv, grad_heads, totals, cos_all, sin_all)
    grad_own = exchange(grad_qkv).reshape(zs, batch, 3, units, local_len, PAIR)

    value = head_grads(normed_all, grad_qkv, loss_row, pick_heads)
    for name in ("c", "x", "y"):
        value = add_stage(value, name)
    owned_down = add_stage(down_sum, "z")[:own_down]
    value, grad_own, owned_down, out_sum, mlp_sum = together(value, grad_own, owned_down, out_sum, mlp_sum)
    value = value.astype(BF16)
    out_sum = add_stage(add_stage(out_sum, "y"), "x")
    owned_output = out_sum
    value = value.reshape(zs, own_rows, value.shape[1])
    value = lax.all_to_all(value, "z", split_axis=0, concat_axis=0, tiled=True)
    columns = 3 * units * PAIR
    loss_value = jnp.sum(value[:, 0, columns:].astype(F32)) / valid_total
    value = value[:, :, :columns].reshape(zs, own_rows, units, 3, PAIR).astype(F32)
    owned_qkv = value.transpose(3, 1, 0, 2, 4).reshape(3, own_rows, width)

    mlp_sum = mlp_sum.reshape(zs, own_rows, -1)
    mlp_sum = [mlp_sum[0]] + [swap(mlp_sum[k], "z", k) for k in range(1, zs)]
    grad_in, grad_first = last(grad_own, x_low, gain_a, attn_w, grad_hidden)

    gain_grad_a = (
        jnp.sum(w_query.astype(F32) * owned_qkv[0], axis=1)
        + jnp.sum(w_key.astype(F32) * owned_qkv[1], axis=1)
        + jnp.sum(w_value.astype(F32) * owned_qkv[2], axis=1)
    ) / attn_gain.astype(F32)
    owned_gate, owned_up, gain_grad_m = finish(mlp_sum, w_gate, w_up, own_down)
    gain_grad_m = gain_grad_m / mlp_gain.astype(F32)
    return (
        result.reshape(batch, local_len, width),
        loss_value,
        grad_in.reshape(batch, local_len, width),
        grad_first.reshape(batch, local_len, width),
        gain_grad_a,
        owned_qkv[0],
        owned_qkv[1],
        owned_qkv[2],
        owned_output,
        gain_grad_m,
        owned_gate,
        owned_up,
        owned_down,
    )


def solution(mesh):
    seqs, dps = mesh.devices.shape
    fine = Mesh(mesh.devices.reshape(seqs // 2, 2, dps // 2, 2), ALL)
    tokens = P(("x", "c"), SEQ, None)
    rows = P(ALL, None)
    gain = P(ALL)
    return jax.shard_map(
        on_device,
        mesh=fine,
        in_specs=(
            tokens, tokens, tokens, tokens, P(("x", "c"), SEQ), gain, rows, rows, rows, rows, gain, rows, rows, rows,
        ),
        out_specs=(
            tokens, P(), tokens, tokens, gain, rows, rows, rows, rows, gain, rows, rows, rows,
        ),
        check_vma=False,
    )
```
